32 devices in a mesh: pipe: 2 (over core), ctx: 4 (over z), wa: 4 (over y, x).
Axes of the slice: x: 2, y: 2, z: 4, core: 2. Of those that a mesh axis runs over, the one named last changes fastest.
Arguments:
- section_inputs: bfloat16 [2, 2, 512, 1088], P('pipe', None, 'ctx'), may hold values from -6 to 6
- qkv_weight: bfloat16 [2, 17, 1088, 192], P('pipe', None, ('ctx', 'wa')), may hold values from -0.1875 to 0.1875
- out_weight: bfloat16 [2, 17, 1088, 64], P('pipe', None, ('ctx', 'wa')), may hold values from -6 to 6
- head_bias: float32 [2, 17, 128], P('pipe'), may hold values from -3 to 3
- mlp_weight: bfloat16 [2, 2, 1088, 4352], P('pipe', None, 'ctx', 'wa'), may hold values from -0.1875 to 0.1875
- hidden_bias: float32 [2, 4352], P('pipe', 'wa'), may hold values from -3 to 3
- feature_bias: float32 [2, 4, 1088], P('pipe'), may hold values from -3 to 3
- ln_gain: float32 [2, 2, 1088], P('pipe'), may hold values from 0.25 to 1.75
- block_table: int32 [4, 2], replicated, may hold values from 0 to 7, as said below
Outputs:
- section_outputs: float32 [2, 2, 512, 1088], P('pipe', None, 'ctx')
- qkv_grad: float32 [2, 17, 1088, 192], P('pipe', None, ('ctx', 'wa'))
- out_grad: float32 [2, 17, 1088, 64], P('pipe', None, ('ctx', 'wa'))
- head_bias_grad: float32 [2, 17, 128], P('pipe')
- mlp_grad: float32 [2, 2, 1088, 4352], P('pipe', None, 'ctx', 'wa')
- hidden_bias_grad: float32 [2, 4352], P('pipe', 'wa')
- feature_bias_grad: float32 [2, 4, 1088], P('pipe')
- ln_gain_grad: float32 [2, 2, 1088], P('pipe')
The draws below stay inside these ranges and needn't reach their ends.
Inputs may be any that keep to these rules, and one draw needn't show every extreme that they name: `block_table`: row c names a block b of 64 positions, b below 4, and its mirror 2 * 4 - 1 - b; every block appears once.
All inputs are finite; a program needn't handle non-finite values.
Results may differ from the reference program's by a relative error of at most 0.02.
Values may be sent and summed in bfloat16 or wider, within the bound.
A program may use at most 192 MiB of HBM per device.

```python
import math
import jax
import jax.numpy as jnp
from jax import lax

D = 1088
HEADS = 17
HD = 64
FF = 4352
MICRO = 2
BLOCK = 64
SEQ = 512
N_PIPE = 2
N_CTX = 4


def draw_block_table(key, part):
    order = jax.random.permutation(key, N_CTX).astype(jnp.int32)
    return jnp.stack([order, 2 * N_CTX - 1 - order], axis=1).astype(jnp.int32)


def steps_of(rng, shape, cuts, smallest, largest):
    level = 1.0
    for axis_at, shards_of in cuts:
        heights = jax.random.uniform(jax.random.fold_in(jax.random.fold_in(rng, 6), axis_at), (shards_of,), jnp.float32, smallest / len(cuts), largest / len(cuts))
        level = level * jnp.repeat(jnp.exp(heights), shape[axis_at] // shards_of).reshape((-1,) + (1,) * (len(shape) - 1 - axis_at))
    return level


def gaussian(key, dims, scale, reach, cuts=(), kind=jnp.bfloat16):
    level = steps_of(key, dims, cuts, -0.22, 0.18) if cuts else 1.0
    entries = jax.random.normal(key, dims, jnp.float32) * scale * level
    return jnp.minimum(jnp.maximum(entries, -reach), reach).astype(kind)


def setup_inputs(seed: int = 0) -> dict:
    key_list = jax.random.split(jax.random.key(seed), 10)
    section_inputs = gaussian(key_list[0], (N_PIPE, MICRO, SEQ, D), 1.0, 6.0, ((0, 2), (2, 4)))
    qkv_weight = gaussian(key_list[1], (N_PIPE, HEADS, D, 3 * HD), D ** -0.5, 0.1875, ((0, 2), (2, 16)))
    out_weight = gaussian(key_list[2], (N_PIPE, HEADS, D, HD), 1.0, 6.0, ((0, 2), (2, 16)))
    head_bias = gaussian(key_list[3], (N_PIPE, HEADS, 2 * HD), 0.5, 3.0, ((0, 2),), jnp.float32)
    mlp_weight = gaussian(key_list[4], (N_PIPE, 2, D, FF), D ** -0.5, 0.1875, ((0, 2), (2, 4), (3, 4)))
    hidden_bias = gaussian(key_list[5], (N_PIPE, FF), 0.5, 3.0, ((0, 2), (1, 4)), jnp.float32)
    feature_bias = gaussian(key_list[6], (N_PIPE, 4, D), 0.5, 3.0, ((0, 2),), jnp.float32)
    ln_gain = jnp.clip(1.0 + 0.15 * jax.random.normal(key_list[7], (N_PIPE, 2, D), jnp.float32), 0.25, 1.75)
    block_table = draw_block_table(jax.random.fold_in(key_list[9], 71), 0)
    return dict(section_inputs=section_inputs, qkv_weight=qkv_weight, out_weight=out_weight, head_bias=head_bias, mlp_weight=mlp_weight, hidden_bias=hidden_bias, feature_bias=feature_bias, ln_gain=ln_gain, block_table=block_table)


EPS = 1e-05
GELU_C = 0.7978845608028654
GELU_A = 0.044715

def norm_forward(stream, gain, offset):
    centre = lax.optimization_barrier(jnp.mean(stream, axis=-1, keepdims=True))
    centred = stream - centre
    variance = lax.optimization_barrier(jnp.mean(centred * centred, axis=-1, keepdims=True))
    inv_std = lax.rsqrt(variance + EPS)
    normed = centred * inv_std
    return (normed * gain + offset, normed, inv_std)

def norm_backward(grad_out, normed, inv_std, gain):
    grad_normed = grad_out * gain
    first_mean = lax.optimization_barrier(jnp.mean(grad_normed, axis=-1, keepdims=True))
    second_mean = lax.optimization_barrier(jnp.mean(grad_normed * normed, axis=-1, keepdims=True))
    return inv_std * (grad_normed - first_mean - normed * second_mean)

def gelu_value(hidden):
    tangent = jnp.tanh(GELU_C * (hidden + GELU_A * hidden * hidden * hidden))
    return 0.5 * hidden * (1.0 + tangent)

def gelu_slope(hidden):
    tangent = jnp.tanh(GELU_C * (hidden + GELU_A * hidden * hidden * hidden))
    return 0.5 * (1.0 + tangent) + 0.5 * hidden * (1.0 - tangent * tangent) * GELU_C * (1.0 + 3.0 * GELU_A * hidden * hidden)

def positions(block_table):
    starts = jnp.repeat(block_table.reshape(-1).astype(jnp.int32) * BLOCK, BLOCK)
    return starts + jnp.tile(jnp.arange(BLOCK, dtype=jnp.int32), 2 * N_CTX)

def block_layout():
    query_rows = math.gcd(SEQ, 512)
    return (query_rows, SEQ // query_rows)

def masked_scores(query_block, pos_block, key_wide, seq_pos):
    scores = jnp.einsum('hqe,hke->hqk', query_block.astype(jnp.float32), key_wide) * HD ** (-0.5)
    return jnp.where(seq_pos[None, None, :] <= pos_block[None, :, None], scores, -jnp.inf)

def layer_forward(layer_in, seq_pos, params):
    qkv_layer, out_layer, bias_heads, mlp_layer, bias_hidden, bias_feature, gain_layer = params
    query_rows, block_count = block_layout()
    stream = layer_in.astype(jnp.float32)
    normed_in, normed_one, inv_one = norm_forward(stream, gain_layer[0], bias_feature[0])
    attn_in = normed_in.astype(jnp.bfloat16)
    projected = jnp.einsum('td,hde->hte', attn_in.astype(jnp.float32), qkv_layer.astype(jnp.float32))
    queries = (projected[:, :, :HD] + bias_heads[:, None, :HD]).astype(jnp.bfloat16)
    key_rows = projected[:, :, HD:2 * HD].astype(jnp.bfloat16)
    values = (projected[:, :, 2 * HD:] + bias_heads[:, None, HD:]).astype(jnp.bfloat16)
    key_wide = key_rows.astype(jnp.float32)
    value_wide = values.astype(jnp.float32)
    query_blocks = queries.reshape(HEADS, block_count, query_rows, HD).transpose(1, 0, 2, 3)
    pos_blocks = seq_pos.reshape(block_count, query_rows)

    def attend(block_item):
        query_block, pos_block = block_item
        scores = masked_scores(query_block, pos_block, key_wide, seq_pos)
        row_top = lax.optimization_barrier(jnp.max(scores, axis=-1, keepdims=True))
        log_total = row_top + jnp.log(lax.optimization_barrier(jnp.sum(jnp.exp(scores - row_top), axis=-1, keepdims=True)))
        probs = jnp.exp(scores - log_total).astype(jnp.bfloat16)
        mixed_rows = jnp.einsum('hqk,hke->hqe', probs.astype(jnp.float32), value_wide).astype(jnp.bfloat16)
        return (mixed_rows, log_total[..., 0])
    mixed_blocks, total_blocks = lax.map(attend, (query_blocks, pos_blocks))
    mixed = mixed_blocks.transpose(1, 0, 2, 3).reshape(HEADS, SEQ, HD)
    log_total = total_blocks.transpose(1, 0, 2).reshape(HEADS, SEQ)
    attn_out = jnp.einsum('hte,hde->td', mixed.astype(jnp.float32), out_layer.astype(jnp.float32)) + bias_feature[1]
    first_sum = stream + attn_out
    normed_ffn, normed_two, inv_two = norm_forward(first_sum, gain_layer[1], bias_feature[2])
    ffn_in = normed_ffn.astype(jnp.bfloat16)
    pre = jnp.dot(ffn_in, mlp_layer[0], preferred_element_type=jnp.float32) + bias_hidden
    act = gelu_value(pre).astype(jnp.bfloat16)
    layer_out = first_sum + jnp.dot(act, mlp_layer[1].T, preferred_element_type=jnp.float32) + bias_feature[3]
    saved = (normed_one, inv_one, attn_in, queries, key_rows, values, mixed, log_total, normed_two, inv_two, ffn_in, pre, act)
    return (layer_out, saved)

def layer_backward(cot_low, seq_pos, saved, params):
    qkv_layer, out_layer, bias_heads, mlp_layer, bias_hidden, bias_feature, gain_layer = params
    normed_one, inv_one, attn_in, queries, key_rows, values, mixed, log_total, normed_two, inv_two, ffn_in, pre, act = saved
    query_rows, block_count = block_layout()
    cotangent = cot_low.astype(jnp.float32)
    grad_down = jnp.dot(cot_low.T, act, preferred_element_type=jnp.float32)
    d_act = jnp.dot(cot_low, mlp_layer[1], preferred_element_type=jnp.float32)
    d_pre = d_act * gelu_slope(pre)
    grad_hidden = lax.optimization_barrier(jnp.sum(d_pre, axis=0))
    d_pre_low = d_pre.astype(jnp.bfloat16)
    grad_up = jnp.dot(ffn_in.T, d_pre_low, preferred_element_type=jnp.float32)
    d_ffn = jnp.dot(d_pre_low, mlp_layer[0].T, preferred_element_type=jnp.float32)
    grad_gain_two = lax.optimization_barrier(jnp.sum(d_ffn * normed_two, axis=0))
    grad_shift_two = lax.optimization_barrier(jnp.sum(d_ffn, axis=0))
    d_first = cotangent + norm_backward(d_ffn, normed_two, inv_two, gain_layer[1])
    grad_attn_bias = lax.optimization_barrier(jnp.sum(d_first, axis=0))
    d_first_low = d_first.astype(jnp.bfloat16)
    grad_out = jnp.einsum('ti,hte->hie', d_first_low.astype(jnp.float32), mixed.astype(jnp.float32))
    d_mixed = jnp.einsum('ti,hie->hte', d_first_low.astype(jnp.float32), out_layer.astype(jnp.float32)).astype(jnp.bfloat16)
    key_wide = key_rows.astype(jnp.float32)
    value_wide = values.astype(jnp.float32)
    query_blocks = queries.reshape(HEADS, block_count, query_rows, HD).transpose(1, 0, 2, 3)
    dmix_blocks = d_mixed.reshape(HEADS, block_count, query_rows, HD).transpose(1, 0, 2, 3)
    total_blocks = log_total.reshape(HEADS, block_count, query_rows).transpose(1, 0, 2)
    pos_blocks = seq_pos.reshape(block_count, query_rows)

    def step_back(carry, block_item):
        key_acc, value_acc = carry
        query_block, dmix_block, total_block, pos_block = block_item
        scores = masked_scores(query_block, pos_block, key_wide, seq_pos)
        probs = jnp.exp(scores - total_block[..., None])
        d_probs = jnp.einsum('hqe,hke->hqk', dmix_block.astype(jnp.float32), value_wide)
        delta = lax.optimization_barrier(jnp.sum(probs * d_probs, axis=-1, keepdims=True))
        d_scores = (probs * (d_probs - delta) * HD ** (-0.5)).astype(jnp.bfloat16)
        d_query_block = jnp.einsum('hqk,hke->hqe', d_scores.astype(jnp.float32), key_wide)
        key_acc = key_acc + jnp.einsum('hqk,hqe->hke', d_scores.astype(jnp.float32), query_block.astype(jnp.float32))
        value_acc = value_acc + jnp.einsum('hqk,hqe->hke', probs.astype(jnp.bfloat16).astype(jnp.float32), dmix_block.astype(jnp.float32))
        return ((key_acc, value_acc), d_query_block)
    start = (jnp.zeros((HEADS, SEQ, HD), jnp.float32), jnp.zeros((HEADS, SEQ, HD), jnp.float32))
    (d_key, d_value), dq_blocks = lax.scan(step_back, start, (query_blocks, dmix_blocks, total_blocks, pos_blocks))
    d_query = dq_blocks.transpose(1, 0, 2, 3).reshape(HEADS, SEQ, HD)
    grad_heads = jnp.concatenate([lax.optimization_barrier(jnp.sum(d_query, axis=1)), lax.optimization_barrier(jnp.sum(d_value, axis=1))], axis=-1)
    d_proj = jnp.concatenate([d_query.astype(jnp.bfloat16), d_key.astype(jnp.bfloat16), d_value.astype(jnp.bfloat16)], axis=-1)
    grad_qkv = jnp.einsum('td,hte->hde', attn_in.astype(jnp.float32), d_proj.astype(jnp.float32))
    d_attn = jnp.einsum('hte,hde->td', d_proj.astype(jnp.float32), qkv_layer.astype(jnp.float32))
    grad_gain_one = lax.optimization_barrier(jnp.sum(d_attn * normed_one, axis=0))
    grad_shift_one = lax.optimization_barrier(jnp.sum(d_attn, axis=0))
    d_input = d_first + norm_backward(d_attn, normed_one, inv_one, gain_layer[0])
    grad_feature = jnp.stack([grad_shift_one, grad_attn_bias, grad_shift_two, lax.optimization_barrier(jnp.sum(cotangent, axis=0))])
    grad_gains = jnp.stack([grad_gain_one, grad_gain_two])
    grads = (grad_qkv, grad_out, grad_heads, jnp.stack([grad_up, grad_down]), grad_hidden, grad_feature, grad_gains)
    return (d_input, grads)

def reference(section_inputs, qkv_weight, out_weight, head_bias, mlp_weight, hidden_bias, feature_bias, ln_gain, block_table):
    seq_pos = positions(block_table)
    layer_params = []
    for layer in range(2):
        layer_params.append((qkv_weight[layer], out_weight[layer], head_bias[layer], mlp_weight[layer], hidden_bias[layer], feature_bias[layer], ln_gain[layer]))
    totals = [None, None]
    outputs_last = []
    input_grads = []
    for batch in range(MICRO):
        first_out, first_saved = layer_forward(section_inputs[0, batch], seq_pos, layer_params[0])
        middle = lax.optimization_barrier(first_out.astype(jnp.bfloat16))
        last_out, last_saved = layer_forward(middle, seq_pos, layer_params[1])
        outputs_last.append(last_out)
        back_grad, last_grads = layer_backward(section_inputs[1, batch], seq_pos, last_saved, layer_params[1])
        back_low = lax.optimization_barrier(back_grad.astype(jnp.bfloat16))
        input_grad, first_grads = layer_backward(back_low, seq_pos, first_saved, layer_params[0])
        input_grads.append(input_grad)
        for layer, grads in ((0, first_grads), (1, last_grads)):
            if totals[layer] is None:
                totals[layer] = grads
            else:
                totals[layer] = jax.tree.map(jnp.add, totals[layer], grads)
    section_outputs = jnp.stack([jnp.stack(input_grads), jnp.stack(outputs_last)])
    joined = [jnp.stack([totals[0][index], totals[1][index]]) for index in range(7)]
    return (section_outputs, joined[0], joined[1], joined[2], joined[3], joined[4], joined[5], joined[6])
```

```python
import functools

import jax
import jax.numpy as jnp
from jax import lax
from jax.experimental import pallas as pl
from jax.experimental.pallas import tpu as pltpu
from jax.sharding import PartitionSpec as P

EPS = 1e-05
GELU_C = 0.7978845608028654
GELU_A = 0.044715
KERNELS = True
MESH = pl.DeviceIdType.MESH
VM = pl.BlockSpec(memory_space=pltpu.VMEM)
IDS = {"sum_wa": 1, "swap_wa": 2, "swap_ctx": 3, "line_attn": 4, "line_mlp": 5, "line_pair": 6, "swap_mlp": 7,
       "swap_attn": 8, "all_small": 9, "all_heads": 10, "swap_grad": 11, "step": 12}


def remote(src, dst, send, recv, peer):
    return pltpu.make_async_remote_copy(
        src_ref=src, dst_ref=dst, send_sem=send, recv_sem=recv, device_id=peer, device_id_type=MESH
    )


def greet(peers):
    barrier = pltpu.get_barrier_semaphore()
    for peer in peers:
        pl.semaphore_signal(barrier, inc=1, device_id=peer, device_id_type=MESH)
    pl.semaphore_wait(barrier, len(peers))


def sum_kernel(axis, n, x_ref, o_ref, got, send_a, recv_a, send_b, recv_b):
    me = lax.axis_index(axis)
    peers = [{axis: lax.rem(me + d, n)} for d in range(1, n)]
    greet(peers)
    first = [
        remote(x_ref.at[lax.rem(me + d, n)], got.at[d - 1], send_a.at[d - 1], recv_a.at[d - 1], peers[d - 1])
        for d in range(1, n)
    ]
    for copy in first:
        copy.start()
    total = x_ref[me].astype(jnp.float32)
    for d, copy in enumerate(first):
        copy.wait_recv()
        total = total + got[d].astype(jnp.float32)
    o_ref[me] = total.astype(o_ref.dtype)
    second = [
        remote(o_ref.at[me], o_ref.at[me], send_b.at[d - 1], recv_b.at[d - 1], peers[d - 1]) for d in range(1, n)
    ]
    for copy in second:
        copy.start()
    for copy in first:
        copy.wait_send()
    for copy in second:
        copy.wait()


def swap_kernel(axis, n, x_ref, o_ref, send, recv, local):
    me = lax.axis_index(axis)
    peers = [{axis: lax.rem(me + d, n)} for d in range(1, n)]
    greet(peers)
    copies = [
        remote(x_ref.at[lax.rem(me + d, n)], o_ref.at[me], send.at[d - 1], recv.at[d - 1], peers[d - 1])
        for d in range(1, n)
    ]
    for copy in copies:
        copy.start()
    own = pltpu.make_async_copy(x_ref.at[me], o_ref.at[me], local)
    own.start()
    own.wait()
    for copy in copies:
        copy.wait()


def all_kernel(axis, n, x_ref, o_ref, send, recv, local):
    me = lax.axis_index(axis)
    peers = [{axis: lax.rem(me + d, n)} for d in range(1, n)]
    greet(peers)
    copies = [
        remote(x_ref, o_ref.at[me], send.at[d - 1], recv.at[d - 1], peers[d - 1]) for d in range(1, n)
    ]
    for copy in copies:
        copy.start()
    own = pltpu.make_async_copy(x_ref, o_ref.at[me], local)
    own.start()
    own.wait()
    for copy in copies:
        copy.wait()


def line_kernel(n, both, x_ref, o_ref, send_r, recv_r, send_l, recv_l, send_p, recv_p, local):
    me = lax.axis_index("ctx")
    side = lax.axis_index("pipe")
    row = side if both else 0
    right, left, mate = {"ctx": me + 1}, {"ctx": me - 1}, {"pipe": 1 - side}
    barrier = pltpu.get_barrier_semaphore()
    not_last, not_first = me + 1 < n, me > 0

    @pl.when(not_last)
    def _():
        pl.semaphore_signal(barrier, inc=1, device_id=right, device_id_type=MESH)

    @pl.when(not_first)
    def _():
        pl.semaphore_signal(barrier, inc=1, device_id=left, device_id_type=MESH)

    if both:
        pl.semaphore_signal(barrier, inc=1, device_id=mate, device_id_type=MESH)
    extra = 1 if both else 0

    @pl.when(not_first & not_last)
    def _():
        pl.semaphore_wait(barrier, 2 + extra)

    @pl.when(jnp.logical_not(not_first & not_last))
    def _():
        pl.semaphore_wait(barrier, 1 + extra)

    own = pltpu.make_async_copy(x_ref, o_ref.at[row, me], local)
    own.start()

    def block(at, fresh):
        return x_ref if fresh else o_ref.at[row, at]

    def to_right(s):
        return remote(block(me - s, s == 0), o_ref.at[row, me - s], send_r.at[s], recv_r.at[s], right)

    def to_left(s):
        return remote(block(me + s, s == 0), o_ref.at[row, me + s], send_l.at[s], recv_l.at[s], left)

    def to_mate(at, fresh):
        return remote(block(at, fresh), o_ref.at[row, at], send_p.at[at], recv_p.at[at], mate)

    def arrived(at, sem):
        return remote(o_ref.at[row, at], o_ref.at[row, at], send_r.at[0], sem, mate)

    for s in range(n):

        @pl.when(me - s >= 0)
        def _():
            if s > 0:
                arrived(me - s, recv_r.at[s - 1]).wait_recv()
            if s < n - 1:

                @pl.when(not_last)
                def _():
                    to_right(s).start()

            if both and s > 0:
                to_mate(me - s, False).start()

        @pl.when(me + s < n)
        def _():
            if s > 0:
                arrived(me + s, recv_l.at[s - 1]).wait_recv()
            if s < n - 1:

                @pl.when(not_first)
                def _():
                    to_left(s).start()

            if both:
                to_mate(me + s, s == 0).start()

    own.wait()
    for s in range(n - 1):

        @pl.when((me - s >= 0) & not_last)
        def _():
            to_right(s).wait_send()

        @pl.when((me + s < n) & not_first)
        def _():
            to_left(s).wait_send()

    if both:
        for at in range(n):
            to_mate(at, False).wait_send()
            remote(o_ref.at[1 - side, at], o_ref.at[1 - side, at], send_p.at[at], recv_p.at[at], mate).wait_recv()


def call(kernel, name, shape, scratch, x):
    return pl.pallas_call(
        kernel,
        out_shape=jax.ShapeDtypeStruct(shape, x.dtype),
        in_specs=[VM],
        out_specs=VM,
        scratch_shapes=scratch,
        compiler_params=pltpu.CompilerParams(
            collective_id=IDS[name], has_side_effects=True, vmem_limit_bytes=60 * 1024 * 1024
        ),
        name=name,
    )(x)


def dma(count):
    return pltpu.SemaphoreType.DMA((count,))


def summed(x):
    n = lax.axis_size("wa")
    low = x.astype(jnp.bfloat16)
    if not KERNELS:
        return lax.psum(low.astype(jnp.float32), "wa").astype(jnp.bfloat16).astype(jnp.float32)
    parts = low.reshape(n, low.shape[0] // n, low.shape[1])
    scratch = [pltpu.VMEM((n - 1,) + parts.shape[1:], jnp.bfloat16)] + [dma(n - 1)] * 4
    out = call(functools.partial(sum_kernel, "wa", n), "sum_wa", parts.shape, scratch, parts)
    return out.reshape(low.shape).astype(jnp.float32)


def swapped(x, axis, name):
    n = lax.axis_size(axis)
    if not KERNELS:
        return lax.all_to_all(x, axis, split_axis=0, concat_axis=0, tiled=True)
    scratch = [dma(n - 1)] * 2 + [pltpu.SemaphoreType.DMA]
    return call(functools.partial(swap_kernel, axis, n), name, x.shape, scratch, x)


def gathered(x, axis, name):
    n = lax.axis_size(axis)
    if not KERNELS:
        return lax.all_gather(x, axis)
    scratch = [dma(n - 1)] * 2 + [pltpu.SemaphoreType.DMA]
    return call(functools.partial(all_kernel, axis, n), name, (n,) + x.shape, scratch, x)


def lined(x, both, name):
    n = lax.axis_size("ctx")
    if not KERNELS:
        out = lax.all_gather(x, "ctx")
        return lax.all_gather(out, "pipe") if both else out[None]
    scratch = [dma(n - 1)] * 4 + [dma(n)] * 2 + [pltpu.SemaphoreType.DMA]
    return call(functools.partial(line_kernel, n, both), name, (2 if both else 1, n) + x.shape, scratch, x)


def dot(a, b, ca, cb):
    return lax.dot_general(a, b, (((ca,), (cb,)), ((), ())), preferred_element_type=jnp.float32)


def attend_kernel(scale, qpos, kpos, q_ref, kv_ref, mix_ref, total_ref):
    heads = q_ref.shape[0]
    allowed = kpos[...] <= qpos[...]
    for h in range(heads):
        kv = kv_ref[:, h].reshape(-1, kv_ref.shape[-1])
        scores = jnp.where(allowed, dot(q_ref[h], kv, 1, 1) * scale, -jnp.inf)
        top = jnp.max(scores, axis=-1, keepdims=True)
        total = top + jnp.log(jnp.sum(jnp.exp(scores - top), axis=-1, keepdims=True))
        probs = jnp.exp(scores - total).astype(jnp.bfloat16)
        mix_ref[h] = dot(probs, kv, 1, 0).astype(jnp.bfloat16)
        total_ref[h] = total


def attend_back_kernel(scale, qpos, kpos, q_ref, kv_ref, dm_ref, total_ref, dq_ref, dkv_ref):
    heads = q_ref.shape[0]
    allowed = kpos[...] <= qpos[...]
    for h in range(heads):
        kv = kv_ref[:, h].reshape(-1, kv_ref.shape[-1])
        scores = jnp.where(allowed, dot(q_ref[h], kv, 1, 1) * scale, -jnp.inf)
        probs = jnp.exp(scores - total_ref[h])
        d_probs = dot(dm_ref[h], kv, 1, 1)
        delta = jnp.sum(probs * d_probs, axis=-1, keepdims=True)
        d_scores = (probs * (d_probs - delta) * scale).astype(jnp.bfloat16)
        dq_ref[h] = dot(d_scores, kv, 1, 0)
        d_kv = dot(d_scores, q_ref[h], 0, 0) + dot(probs.astype(jnp.bfloat16), dm_ref[h], 0, 0)
        dkv_ref[:, h] = d_kv.astype(jnp.bfloat16).reshape(dkv_ref.shape[0], dkv_ref.shape[2], dkv_ref.shape[3])


def local_call(kernel, shapes, *args):
    return pl.pallas_call(
        kernel,
        out_shape=[jax.ShapeDtypeStruct(*s) for s in shapes],
        in_specs=[VM] * len(args),
        out_specs=[VM] * len(shapes),
        compiler_params=pltpu.CompilerParams(vmem_limit_bytes=48 * 1024 * 1024),
        interpret=not KERNELS,
    )(*args)

def norm_forward(stream, gain, offset):
    centre = jnp.mean(stream, axis=-1, keepdims=True)
    centred = stream - centre
    variance = jnp.mean(centred * centred, axis=-1, keepdims=True)
    inv_std = lax.rsqrt(variance + EPS)
    normed = centred * inv_std
    return (normed * gain + offset, normed, inv_std)


def norm_backward(grad_out, normed, inv_std, gain):
    grad_normed = grad_out * gain
    first_mean = jnp.mean(grad_normed, axis=-1, keepdims=True)
    second_mean = jnp.mean(grad_normed * normed, axis=-1, keepdims=True)
    return inv_std * (grad_normed - first_mean - normed * second_mean)


def gelu_value(hidden):
    tangent = jnp.tanh(GELU_C * (hidden + GELU_A * hidden * hidden * hidden))
    return 0.5 * hidden * (1.0 + tangent)


def gelu_slope(hidden):
    tangent = jnp.tanh(GELU_C * (hidden + GELU_A * hidden * hidden * hidden))
    return 0.5 * (1.0 + tangent) + 0.5 * hidden * (1.0 - tangent * tangent) * GELU_C * (
        1.0 + 3.0 * GELU_A * hidden * hidden
    )


def per_device(
    section_inputs,
    qkv_weight,
    out_weight,
    head_bias,
    mlp_weight,
    hidden_bias,
    feature_bias,
    ln_gain,
    block_table,
):
    ctx_count = lax.axis_size("ctx")
    shard_count = lax.axis_size("wa")
    side = lax.axis_index("pipe")
    ctx_index = lax.axis_index("ctx")
    shard_index = lax.axis_index("wa")
    rows = section_inputs.shape[2]
    width = section_inputs.shape[3]
    head_count = qkv_weight.shape[1]
    head_dim = out_weight.shape[3]
    part = qkv_weight.shape[2]
    slots = (head_count + shard_count - 1) // shard_count
    pad = slots * shard_count - head_count
    block_rows = rows // 2
    scale = head_dim ** (-0.5)
    swap = [(0, 1), (1, 0)]
    low = jnp.bfloat16

    own_blocks = lax.dynamic_index_in_dim(block_table, ctx_index, 0, keepdims=False)
    step = jnp.arange(block_rows, dtype=jnp.int32)
    query_pos = (own_blocks[:, None] * block_rows + step[None, :]).reshape(rows, 1)
    key_pos = (block_table.reshape(-1)[:, None] * block_rows + step[None, :]).reshape(1, rows * ctx_count)

    def mine(first, second):
        return jnp.where(side == 0, first, second)

    inputs = section_inputs[0]
    traded = lax.ppermute(mine(inputs[1], inputs[0]), "pipe", swap)
    layer_input = mine(inputs[0], traded)
    last_cot = mine(traded, inputs[1])

    packed = jnp.concatenate([qkv_weight[0], out_weight[0]], axis=-1)
    packed = jnp.pad(packed, ((0, pad), (0, 0), (0, 0)))
    packed = packed.reshape(slots, shard_count, part, 4 * head_dim).transpose(1, 0, 2, 3)
    attn_all = lined(swapped(packed, "wa", "swap_wa"), True, "line_attn")
    mlp_all = lined(mlp_weight[0], True, "line_mlp")

    sizes = [head_bias[0].size, hidden_bias[0].size, feature_bias[0].size]
    small = jnp.concatenate(
        [head_bias[0].reshape(-1), hidden_bias[0], feature_bias[0].reshape(-1), ln_gain[0].reshape(-1)]
    )
    small_mate = lax.ppermute(small, "pipe", swap)

    def params_of(layer):
        weight = attn_all[layer].transpose(2, 0, 1, 3, 4).reshape(slots, width, 4 * head_dim)
        up = mlp_all[layer][:, 0].reshape(width, -1)
        down = mlp_all[layer][:, 1].reshape(width, -1)
        flat = jnp.where(side == layer, small, small_mate)
        heads, hidden, feature, gains = jnp.split(flat, [sizes[0], sizes[0] + sizes[1], sum(sizes)])
        heads = jnp.pad(heads.reshape(head_count, 2 * head_dim), ((0, pad), (0, 0)))
        heads = heads.reshape(slots, shard_count, 2 * head_dim)
        heads = lax.dynamic_index_in_dim(heads, shard_index, 1, keepdims=False)
        return (
            weight[:, :, : 3 * head_dim],
            weight[:, :, 3 * head_dim :],
            heads,
            up,
            down,
            hidden,
            feature.reshape(4, width),
            gains.reshape(2, width),
        )

    def widened(x, before):
        zero = jnp.zeros_like(x)
        return jnp.concatenate([zero, x] if before else [x, zero], axis=-1)

    def forward(layer_in, params):
        w_qkv, w_out, bias, w_up, w_down, bias_hidden, shifts, gains = params
        stream = layer_in.astype(jnp.float32)
        normed_in, normed_one, inv_one = norm_forward(stream, gains[0], shifts[0])
        attn_in = normed_in.astype(low)
        projected = jnp.einsum("td,hde->hte", attn_in, w_qkv, preferred_element_type=jnp.float32)
        queries = widened((projected[:, :, :head_dim] + bias[:, None, :head_dim]).astype(low), False)
        key_rows = projected[:, :, head_dim : 2 * head_dim].astype(low)
        values = (projected[:, :, 2 * head_dim :] + bias[:, None, head_dim:]).astype(low)
        pairs = lined(jnp.concatenate([key_rows, values], axis=-1), False, "line_pair")[0]
        mixed, log_total = local_call(
            functools.partial(attend_kernel, scale),
            [((slots, rows, 2 * head_dim), low), ((slots, rows, 1), jnp.float32)],
            query_pos,
            key_pos,
            queries,
            pairs,
        )
        mixed = mixed[:, :, head_dim:]
        attn_out = summed(jnp.einsum("hte,hde->td", mixed, w_out, preferred_element_type=jnp.float32))
        first_sum = stream + attn_out + shifts[1]
        normed_ffn, normed_two, inv_two = norm_forward(first_sum, gains[1], shifts[2])
        ffn_in = normed_ffn.astype(low)
        pre = jnp.dot(ffn_in, w_up, preferred_element_type=jnp.float32) + bias_hidden
        act = gelu_value(pre).astype(low)
        layer_out = (
            first_sum
            + summed(jnp.einsum("tf,df->td", act, w_down, preferred_element_type=jnp.float32))
            + shifts[3]
        )
        return layer_out, (
            normed_one, inv_one, attn_in, queries, pairs, mixed, log_total, normed_two, inv_two, ffn_in, pre, act,
        )

    def backward(cot, saved, params):
        w_qkv, w_out, bias, w_up, w_down, bias_hidden, shifts, gains = params
        normed_one, inv_one, attn_in, queries, pairs, mixed, log_total, normed_two, inv_two, ffn_in, pre, act = saved
        cotangent = cot.astype(jnp.float32)
        grad_down = jnp.einsum("ti,tf->if", cot, act, preferred_element_type=jnp.float32)
        d_act = jnp.einsum("ti,if->tf", cot, w_down, preferred_element_type=jnp.float32)
        d_pre = d_act * gelu_slope(pre)
        grad_hidden = jnp.sum(d_pre, axis=0)
        d_pre_low = d_pre.astype(low)
        grad_up = jnp.einsum("td,tf->df", ffn_in, d_pre_low, preferred_element_type=jnp.float32)
        d_ffn = summed(jnp.einsum("tf,df->td", d_pre_low, w_up, preferred_element_type=jnp.float32))
        d_first = cotangent + norm_backward(d_ffn, normed_two, inv_two, gains[1])
        d_first_low = d_first.astype(low)
        grad_out = jnp.einsum("ti,hte->hie", d_first_low, mixed, preferred_element_type=jnp.float32)
        d_mixed = jnp.einsum("ti,hie->hte", d_first_low, w_out, preferred_element_type=jnp.float32)
        d_query, pair_terms = local_call(
            functools.partial(attend_back_kernel, scale),
            [((slots, rows, 2 * head_dim), jnp.float32), (pairs.shape, low)],
            query_pos,
            key_pos,
            queries,
            pairs,
            widened(d_mixed.astype(low), True),
            log_total,
        )
        d_query = d_query[:, :, :head_dim]
        d_pair = swapped(pair_terms, "ctx", "swap_ctx").astype(jnp.float32).sum(axis=0)
        grad_heads = jnp.concatenate(
            [jnp.sum(d_query, axis=1), jnp.sum(d_pair[:, :, head_dim:], axis=1)], axis=-1
        )
        d_proj = jnp.concatenate([d_query.astype(low), d_pair.astype(low)], axis=-1)
        grad_qkv = jnp.einsum("td,hte->hde", attn_in, d_proj, preferred_element_type=jnp.float32)
        d_attn = summed(jnp.einsum("hte,hde->td", d_proj, w_qkv, preferred_element_type=jnp.float32))
        d_input = d_first + norm_backward(d_attn, normed_one, inv_one, gains[0])
        vectors = [
            jnp.sum(d_attn, axis=0),
            jnp.sum(d_first, axis=0),
            jnp.sum(d_ffn, axis=0),
            jnp.sum(cotangent, axis=0),
            jnp.sum(d_attn * normed_one, axis=0),
            jnp.sum(d_ffn * normed_two, axis=0),
            grad_hidden,
            grad_heads.reshape(-1),
        ]
        attn_grad = jnp.concatenate([grad_qkv, grad_out], axis=-1).astype(low)
        mlp_grad = jnp.stack([grad_up, grad_down]).astype(low)
        return d_input, attn_grad, mlp_grad, jnp.concatenate(vectors)

    params = [params_of(0), params_of(1)]
    first_out, first_saved = forward(layer_input, params[0])
    last_out, last_saved = forward(first_out.astype(low), params[1])
    back, attn_one, mlp_one, vec_one = backward(last_cot, last_saved, params[1])
    d_input, attn_zero, mlp_zero, vec_zero = backward(back.astype(low), first_saved, params[0])

    def over_pipe(zero, one):
        kept = mine(zero, one)
        got = lax.ppermute(mine(one, zero), "pipe", swap)
        return kept.astype(jnp.float32) + got.astype(jnp.float32)

    mlp_sum = over_pipe(mlp_zero, mlp_one).astype(low)
    mlp_sum = mlp_sum.reshape(2, ctx_count, width // ctx_count, -1).transpose(1, 0, 2, 3)
    mlp_out = swapped(mlp_sum, "ctx", "swap_mlp").astype(jnp.float32).sum(axis=0)

    attn_sum = over_pipe(attn_zero, attn_one).astype(low)
    attn_sum = attn_sum.reshape(slots, ctx_count, shard_count, part, 4 * head_dim).transpose(1, 2, 0, 3, 4)
    attn_part = swapped(attn_sum, "ctx", "swap_attn").astype(jnp.float32).sum(axis=0).astype(low)
    attn_out = swapped(attn_part, "wa", "swap_grad")
    attn_out = attn_out.transpose(1, 0, 2, 3).reshape(slots * shard_count, part, 4 * head_dim)
    attn_out = attn_out[:head_count].astype(jnp.float32)

    vec = over_pipe(vec_zero, vec_one)
    length = vec.shape[0]
    fill = -length % 128
    vec = jnp.pad(vec, (0, fill)).reshape(-1, 128)
    vec = gathered(vec, "ctx", "all_small").sum(axis=0).reshape(-1)[:length]
    feature_sum, gain_sum, hidden_own, head_own = jnp.split(
        vec, [4 * width, 6 * width, 6 * width + hidden_bias.shape[1]]
    )
    head_sum = gathered(head_own.reshape(slots, 2 * head_dim), "wa", "all_heads")
    head_sum = head_sum.transpose(1, 0, 2).reshape(slots * shard_count, 2 * head_dim)[:head_count]

    last_traded = lax.ppermute(mine(last_out, d_input), "pipe", swap)
    section_outputs = jnp.where(
        side == 0, jnp.stack([d_input, last_traded]), jnp.stack([last_traded, last_out])
    )
    return (
        section_outputs[None],
        attn_out[None, :, :, : 3 * head_dim],
        attn_out[None, :, :, 3 * head_dim :],
        head_sum[None],
        mlp_out[None],
        hidden_own[None],
        feature_sum.reshape(1, 4, width),
        gain_sum.reshape(1, 2, width),
    )


def tiles_of(total, size=256):
    return [(at, min(size, total - at)) for at in range(0, total, size)]


def step_kernel(n, m, sizes, scale, *refs):
    rows, width, ff, slots, micro, head_dim, part, padded = sizes
    (
        inp, pack, mlp, bias, hidden, shift, gain, table,
        out, g_mlp, g_attn, vec_sum, vec_own, vec_wa,
        w_in, stage, wt, mt, x_s, c_s, xf, a_s, q_s, pair, prob, mix,
        p1, p2, p3, p4, r1, r2, r3, r4, fi, dh, ob, act, slope, dpre, h1, dh1,
        dpair, rpair, dproj, gm, rgm, ga, rga, s1, sv, hv, svc, snd1, snd2,
        swap_s, swap_r, at_s, at_r, at_f, ml_s, ml_r, ml_f, pr_s, pr_r,
        rs_s, rs_r, ag_s, ag_r, x_ss, x_rs, o_ss, o_rs, dp_s, dp_r,
        gm_s, gm_r, ga_s, ga_r, sc_s, sc_r, sw_s, sw_r, gw_s, gw_r, loc, go,
    ) = refs
    side = lax.axis_index("pipe")
    c = lax.axis_index("ctx")
    w = lax.axis_index("wa")
    total = micro * rows
    chunk = total // m
    depth = width // n
    low = jnp.bfloat16
    f32 = jnp.float32
    mate = {"pipe": 1 - side}
    later = []

    def ring(axis, count, me):
        return [lax.rem(me + d, count) for d in range(1, count)]

    ctx_peers = ring("ctx", n, c)
    wa_peers = ring("wa", m, w)

    greet(
        [{"ctx": peer} for peer in ctx_peers]
        + [{"wa": peer} for peer in wa_peers]
        + [{"pipe": 1 - side, "wa": peer} for peer in [w] + wa_peers]
    )

    def arrive(ref, sem):
        remote(ref, ref, sem, sem, mate).wait_recv()

    def push(axis, src, dst, send, recv, base=0, rbase=0):
        me, count, peers = (c, n, ctx_peers) if axis == "ctx" else (w, m, wa_peers)

        def copy(d, peer):
            return remote(src(peer), dst(me), send.at[base + d], recv.at[rbase + me], {axis: peer})

        for d, peer in enumerate(peers):
            copy(d, peer).start()

        def drain():
            for d, peer in enumerate(peers):
                copy(d, peer).wait_send()

        return drain

    def crows(at):
        return pl.ds(pl.multiple_of(at * depth, 16), depth)

    def wrows(at):
        return pl.ds(pl.multiple_of(at * chunk, 16), chunk)

    own = wrows(w)

    own_pack = pltpu.make_async_copy(pack.at[w], w_in.at[w], loc.at[0])
    own_pack.start()
    own_mlp = pltpu.make_async_copy(mlp, mt.at[:, crows(c), :], loc.at[1])
    own_mlp.start()
    later.append(push("wa", lambda p: pack.at[p], lambda me: w_in.at[me], swap_s, swap_r))
    stage[...] = jnp.zeros_like(stage)
    mix[...] = jnp.zeros_like(mix)
    sv[...] = jnp.zeros_like(sv)
    own_pack.wait()
    for p in wa_peers:
        arrive(w_in.at[p], swap_r.at[p])

    def lay(s, _):
        for j in range(m):
            stage[j * part : (j + 1) * part, :] = w_in[j, s].astype(f32)[:part]
        wt[s, crows(c), :] = stage[:depth, :].astype(low)
        return 0

    lax.fori_loop(0, slots, lay, 0)

    def near(peer):
        return jnp.abs(peer - c) <= 2

    def line(src, dst, send, recv, fwd):
        def direct(d, peer):
            return remote(src, dst(c), send.at[d], recv.at[c], {"ctx": peer})

        def right(s):
            return remote(dst(c - s), dst(c - s), fwd.at[2 * (s - 2)], recv.at[c - s], {"ctx": c + 1})

        def left(s):
            return remote(dst(c + s), dst(c + s), fwd.at[2 * (s - 2) + 1], recv.at[c + s], {"ctx": c - 1})

        def start():
            for d, peer in enumerate(ctx_peers):

                @pl.when(near(peer))
                def _():
                    direct(d, peer).start()

        def pump():
            for s in range(2, n - 1):

                @pl.when((c - s >= 0) & (c + 1 < n))
                def _():
                    arrive(dst(c - s), recv.at[c - s])
                    right(s).start()

                @pl.when((c + s < n) & (c >= 1))
                def _():
                    arrive(dst(c + s), recv.at[c + s])
                    left(s).start()

        def finish():
            for peer in ctx_peers:
                done = ((peer - c <= -2) & (c + 1 < n)) | ((peer - c >= 2) & (c >= 1))

                @pl.when(jnp.logical_not(done))
                def _():
                    arrive(dst(peer), recv.at[peer])

        def drain():
            for d, peer in enumerate(ctx_peers):

                @pl.when(near(peer))
                def _():
                    direct(d, peer).wait_send()

            for s in range(2, n - 1):

                @pl.when((c - s >= 0) & (c + 1 < n))
                def _():
                    right(s).wait_send()

                @pl.when((c + s < n) & (c >= 1))
                def _():
                    left(s).wait_send()

        later.append(drain)
        return start, pump, finish

    at_start, at_pump, at_finish = line(
        wt.at[:, crows(c), :], lambda at: wt.at[:, crows(at), :], at_s, at_r, at_f
    )
    ml_start, ml_pump, ml_finish = line(mlp, lambda at: mt.at[:, crows(at), :], ml_s, ml_r, ml_f)

    @pl.when(side == 1)
    def _():
        pl.semaphore_wait(go, 1)

    at_start()
    ml_start()
    at_pump()
    at_finish()

    @pl.when(side == 0)
    def _():
        x_s[...] = inp[...]

    @pl.when(side == 1)
    def _():
        ml_pump()
        c_s[...] = inp[...]
        for p in range(m):
            arrive(xf.at[wrows(p), :], x_rs.at[p])
        x_s[...] = xf[...]

    def norm(stream):
        centre = jnp.mean(stream, axis=-1, keepdims=True)
        centred = stream - centre
        variance = jnp.mean(centred * centred, axis=-1, keepdims=True)
        inv_std = lax.rsqrt(variance + EPS)
        return centred * inv_std, inv_std

    for at, size in tiles_of(total, 64):
        normed, _ = norm(x_s[at : at + size, :].astype(f32))
        a_s[at : at + size, :] = (normed * gain[0:1, :] + shift[0:1, :]).astype(low)

    lane = lax.broadcasted_iota(jnp.int32, (1, 2 * head_dim), 1)
    upper = lane >= head_dim

    def send_pair(s, start):
        for d, peer in enumerate(ctx_peers):
            copy = remote(
                pair.at[c, s], pair.at[c, s], pr_s.at[s * (n - 1) + d], pr_r.at[s * n + c], {"ctx": peer}
            )
            if start:
                copy.start()
            else:
                copy.wait_send()

    def project(s, _):
        made = dot(a_s[...], wt[s], 1, 0) + bias[s * m + w]
        pair[c, s] = made[:, : 2 * head_dim].astype(low)
        q_s[s] = jnp.where(upper, made[:, 2 * head_dim :], 0.0).astype(low)
        send_pair(s, True)
        return 0

    lax.fori_loop(0, slots, project, 0)

    block = rows // 2
    step = lax.broadcasted_iota(jnp.int32, (rows, 1), 0)
    qpos = jnp.where(step < block, table[c, 0] * block + step, table[c, 1] * block + step - block)
    along = lax.broadcasted_iota(jnp.int32, (1, n * rows), 1)
    kpos = along
    for i in range(2 * n):
        inside = (along >= i * block) & (along < (i + 1) * block)
        kpos = jnp.where(inside, table[i // 2, i % 2] * block + along - i * block, kpos)

    def attend(s, _):
        for p in ctx_peers:
            arrive(pair.at[p, s], pr_r.at[s * n + p])
        for b in range(micro):
            mine = slice(b * rows, (b + 1) * rows)
            kv = pair[:, s, mine, :].reshape(n * rows, 2 * head_dim)
            scores = jnp.where(kpos <= qpos, dot(q_s[s, mine, :], kv, 1, 1) * scale, -jnp.inf)
            top = jnp.max(scores, axis=-1, keepdims=True)
            raised = jnp.exp(scores - top)
            weight = raised / jnp.sum(raised, axis=-1, keepdims=True)
            prob[s * micro + b] = weight
            mixed = dot(weight.astype(low), kv, 1, 0)
            mix[s, mine, 2 * head_dim :] = jnp.where(upper, 0.0, mixed).astype(low)
        return 0

    @pl.when(side == 0)
    def _():
        ml_pump()

    lax.fori_loop(0, slots, attend, 0)

    def send_sum(k, part_s, got):
        later.append(
            push(
                "wa", lambda p: part_s.at[wrows(p), :], lambda me: got.at[me], rs_s, rs_r, k * (m - 1), k * m
            )
        )

    def wait_sum(k, part_s, got):
        value = part_s[own, :].astype(f32)
        for p in wa_peers:
            arrive(got.at[p], rs_r.at[k * m + p])
            value = value + got[p].astype(f32)
        return value

    for at, size in tiles_of(width):
        value = dot(mix[0, :, 2 * head_dim :], wt[0, at : at + size, 2 * head_dim :], 1, 1)
        for s in range(1, slots):
            value = value + dot(mix[s, :, 2 * head_dim :], wt[s, at : at + size, 2 * head_dim :], 1, 1)
        p1[:, at : at + size] = value.astype(low)
    send_sum(0, p1, r1)
    value = wait_sum(0, p1, r1)
    value = x_s[own, :].astype(f32) + value + shift[1:2, :]
    h1[...] = value
    normed, _ = norm(value)
    fi[own, :] = (normed * gain[1:2, :] + shift[2:3, :]).astype(low)
    later.append(push("wa", lambda p: fi.at[own, :], lambda me: fi.at[own, :], ag_s, ag_r))
    ml_finish()
    own_mlp.wait()

    @pl.when(side == 0)
    def _():
        pl.semaphore_signal(go, inc=1, device_id=mate, device_id_type=MESH)

    for p in wa_peers:
        arrive(fi.at[wrows(p), :], ag_r.at[p])

    for at, size in tiles_of(ff):
        pre = dot(fi[...], mt[0, :, at : at + size], 1, 0) + hidden[:, at : at + size]
        square = pre * pre
        tangent = jnp.tanh(GELU_C * (pre + GELU_A * square * pre))
        act[:, at : at + size] = (0.5 * pre * (1.0 + tangent)).astype(low)
        slope[:, at : at + size] = 0.5 * (1.0 + tangent) + 0.5 * pre * (1.0 - tangent * tangent) * GELU_C * (
            1.0 + 3.0 * GELU_A * square
        )
    for at, size in tiles_of(width):
        p2[:, at : at + size] = dot(act[...], mt[1, at : at + size, :], 1, 1).astype(low)
    send_sum(1, p2, r2)
    value = wait_sum(1, p2, r2)
    snd1[...] = (h1[...] + value + shift[3:4, :]).astype(low)

    def cross(snd, other):
        def copies():
            return [
                remote(snd, xf.at[own, :], x_ss.at[d], x_rs.at[w], {"pipe": other, "wa": peer})
                for d, peer in enumerate([w] + wa_peers)
            ]

        for copy in copies():
            copy.start()
        return copies

    def spread(snd):
        def copies():
            return [
                remote(snd, ob.at[own, :], o_ss.at[d], o_rs.at[w], {"wa": peer}) for d, peer in enumerate(wa_peers)
            ]

        for copy in copies():
            copy.start()
        ob[own, :] = snd[...]
        return copies

    @pl.when(side == 0)
    def _():
        cross(snd1, 1)
        for p in range(m):
            arrive(xf.at[wrows(p), :], x_rs.at[p])
        c_s[...] = xf[...]

    @pl.when(side == 1)
    def _():
        spread(snd1)

    for at, size in tiles_of(ff):
        d_pre = dot(c_s[...], mt[1, :, at : at + size], 1, 0) * slope[:, at : at + size]
        sv[6:7, at : at + size] = jnp.sum(d_pre, axis=0, keepdims=True)
        dpre[:, at : at + size] = d_pre.astype(low)
    for at, size in tiles_of(width):
        p3[:, at : at + size] = dot(dpre[...], mt[0, at : at + size, :], 1, 1).astype(low)
    send_sum(2, p3, r3)
    for at, size in tiles_of(width):
        gm[1, at : at + size, :] = dot(c_s[:, at : at + size], act[...], 0, 0).astype(low)
        gm[0, at : at + size, :] = dot(fi[:, at : at + size], dpre[...], 0, 0).astype(low)
    value = wait_sum(2, p3, r3)

    def column(at, x):
        sv[at : at + 1, :] = jnp.sum(x, axis=0, keepdims=True)

    def norm_back(d_out, normed, inv_std, row):
        lifted = d_out * gain[row : row + 1, :]
        first = jnp.mean(lifted, axis=-1, keepdims=True)
        second = jnp.mean(lifted * normed, axis=-1, keepdims=True)
        return inv_std * (lifted - first - normed * second)

    normed, inv_std = norm(h1[...])
    cot = c_s[own, :].astype(f32)
    column(2, value)
    column(5, value * normed)
    column(3, cot)
    value = cot + norm_back(value, normed, inv_std, 1)
    dh1[...] = value
    column(1, value)
    dh[own, :] = value.astype(low)
    later.append(
        push("wa", lambda p: dh.at[own, :], lambda me: dh.at[own, :], ag_s, ag_r, m - 1, m)
    )
    for p in wa_peers:
        arrive(dh.at[wrows(p), :], ag_r.at[m + p])

    def send_dpair(s, start):
        for d, peer in enumerate(ctx_peers):
            copy = remote(
                dpair.at[peer, s], rpair.at[c, s], dp_s.at[s * (n - 1) + d], dp_r.at[s * n + c], {"ctx": peer}
            )
            if start:
                copy.start()
            else:
                copy.wait_send()

    def attend_back(s, _):
        d_mixed = dot(dh[...], wt[s, :, 2 * head_dim :], 1, 0)
        d_mixed = jnp.where(upper, 0.0, d_mixed).astype(low)
        heads = jnp.zeros((1, 2 * head_dim), f32)
        for b in range(micro):
            mine = slice(b * rows, (b + 1) * rows)
            kv = pair[:, s, mine, :].reshape(n * rows, 2 * head_dim)
            weight = prob[s * micro + b]
            d_mine = d_mixed[mine, :]
            d_probs = dot(d_mine, kv, 1, 1)
            delta = jnp.sum(weight * d_probs, axis=-1, keepdims=True)
            d_scores = (weight * (d_probs - delta) * scale).astype(low)
            d_query = jnp.where(upper, dot(d_scores, kv, 1, 0), 0.0)
            heads = heads + jnp.sum(d_query, axis=0, keepdims=True)
            dproj[s, mine, 2 * head_dim :] = d_query.astype(low)
            d_kv = dot(d_scores, q_s[s, mine, :], 0, 0) + dot(weight.astype(low), d_mine, 0, 0)
            dpair[:, s, mine, :] = d_kv.astype(low).reshape(n, rows, 2 * head_dim)
        hv[s] = heads
        send_dpair(s, True)
        return 0

    lax.fori_loop(0, slots, attend_back, 0)
    later.append(push("ctx", lambda p: gm.at[:, crows(p), :], lambda me: rgm.at[me], gm_s, gm_r))

    def collect(s, _):
        value = dpair[c, s].astype(f32)
        for p in ctx_peers:
            arrive(rpair.at[p, s], dp_r.at[s * n + p])
            value = value + rpair[p, s].astype(f32)
        dproj[s, :, : 2 * head_dim] = value.astype(low)
        hv[s] = hv[s] + jnp.where(upper, 0.0, jnp.sum(value, axis=0, keepdims=True))
        return 0

    lax.fori_loop(0, slots, collect, 0)
    for at, size in tiles_of(width):
        value = dot(dproj[0], wt[0, at : at + size, :], 1, 1)
        for s in range(1, slots):
            value = value + dot(dproj[s], wt[s, at : at + size, :], 1, 1)
        p4[:, at : at + size] = value.astype(low)
    send_sum(3, p4, r4)

    def attn_grad(s, _):
        for at, size in tiles_of(width):
            value = dot(a_s[:, at : at + size], dproj[s], 0, 0) + dot(dh[:, at : at + size], mix[s], 0, 0)
            ga[s, at : at + size, :] = value.astype(low)
        return 0

    lax.fori_loop(0, slots, attn_grad, 0)
    later.append(push("ctx", lambda p: ga.at[:, crows(p), :], lambda me: rga.at[me], ga_s, ga_r))

    value = wait_sum(3, p4, r4)
    normed, inv_std = norm(x_s[own, :].astype(f32))
    column(0, value)
    column(4, value * normed)
    snd2[...] = (dh1[...] + norm_back(value, normed, inv_std, 0)).astype(low)

    @pl.when(side == 1)
    def _():
        cross(snd2, 0)

    @pl.when(side == 0)
    def _():
        spread(snd2)

    for s in range(slots):
        sv[8 + s : 9 + s, : 2 * head_dim] = hv[s]
    svc[c] = sv[...]
    later.append(push("ctx", lambda p: sv, lambda me: svc.at[me], sc_s, sc_r))

    for p in ctx_peers:
        arrive(svc.at[p], sc_r.at[p])
    value = svc[0]
    for p in range(1, n):
        value = value + svc[p]
    vec_own[...] = value
    vec_wa[w] = value
    later.append(push("wa", lambda p: vec_own, lambda me: vec_wa.at[me], sw_s, sw_r))

    for p in ctx_peers:
        arrive(rgm.at[p], gm_r.at[p])

    def mlp_grad(i, _):
        at = pl.ds(pl.multiple_of(i * 16, 16), 16)
        for k in range(2):
            value = gm[k, pl.ds(pl.multiple_of(c * depth + i * 16, 16), 16), :].astype(f32)
            for p in ctx_peers:
                value = value + rgm[p, k, at, :].astype(f32)
            g_mlp[k, at, :] = value
        return 0

    lax.fori_loop(0, depth // 16, mlp_grad, 0)
    for p in range(m):

        @pl.when(p != w)
        def _():
            arrive(ob.at[wrows(p), :], o_rs.at[p])

    for at, size in tiles_of(total, 64):
        out[at : at + size, :] = ob[at : at + size, :].astype(f32)

    for p in ctx_peers:
        arrive(rga.at[p], ga_r.at[p])

    def unlay(s, _):
        value = ga[s, crows(c), :].astype(f32)
        for p in ctx_peers:
            value = value + rga[p, s].astype(f32)
        stage[:depth, :] = value
        for j in range(m):
            s1[j, s] = stage[j * part : j * part + padded, :].astype(low)
        return 0

    lax.fori_loop(0, slots, unlay, 0)
    later.append(push("wa", lambda p: s1.at[p], lambda me: g_attn.at[me], gw_s, gw_r))
    own_out = pltpu.make_async_copy(s1.at[w], g_attn.at[w], loc.at[2])
    own_out.start()
    for p in wa_peers:
        arrive(vec_wa.at[p], sw_r.at[p])
    value = vec_wa[0]
    for p in range(1, m):
        value = value + vec_wa[p]
    vec_sum[...] = value
    own_out.wait()
    for p in wa_peers:
        arrive(g_attn.at[p], gw_r.at[p])

    for drain in later:
        drain()

    def drain_heads(s, _):
        send_pair(s, False)
        send_dpair(s, False)
        return 0

    lax.fori_loop(0, slots, drain_heads, 0)
    for snd, at in ((snd1, 0), (snd2, 1)):

        @pl.when(side == at)
        def _():
            for d, peer in enumerate([w] + wa_peers):
                remote(snd, xf.at[own, :], x_ss.at[d], x_rs.at[w], {"pipe": 1 - at, "wa": peer}).wait_send()

        @pl.when(side == 1 - at)
        def _():
            for d, peer in enumerate(wa_peers):
                remote(snd, ob.at[own, :], o_ss.at[d], o_rs.at[w], {"wa": peer}).wait_send()


def whole_step(
    section_inputs, qkv_weight, out_weight, head_bias, mlp_weight, hidden_bias, feature_bias, ln_gain, block_table
):
    n = lax.axis_size("ctx")
    m = lax.axis_size("wa")
    micro, rows, width = section_inputs.shape[1:]
    heads, part = qkv_weight.shape[1:3]
    head_dim = out_weight.shape[3]
    ff = mlp_weight.shape[3]
    depth = mlp_weight.shape[2]
    slots = (heads + m - 1) // m
    pad = slots * m - heads
    padded = part + (-part % 16)
    total = micro * rows
    chunk = total // m
    low = jnp.bfloat16
    f32 = jnp.float32
    two = 2 * head_dim
    scale = head_dim ** (-0.5)

    query, key, value = (qkv_weight[0, :, :, i * head_dim : (i + 1) * head_dim] for i in range(3))
    pack = jnp.concatenate([value, key, out_weight[0], query], axis=-1)
    pack = jnp.pad(pack, ((0, pad), (0, padded - part), (0, 0)))
    pack = pack.reshape(slots, m, padded, 2 * two).transpose(1, 0, 2, 3)
    bias = jnp.concatenate(
        [head_bias[0][:, head_dim:], jnp.zeros((heads, two), f32), head_bias[0][:, :head_dim]], axis=-1
    )
    bias = jnp.pad(bias, ((0, pad), (0, 0))).reshape(slots * m, 1, 2 * two)

    def v(shape, kind=low):
        return pltpu.VMEM(shape, kind)

    wide = (total, width)
    scratch = (
        [v((m, slots, padded, 2 * two)), v((depth + 16, 2 * two), f32), v((slots, width, 2 * two)), v((2, width, ff))]
        + [v(wide)] * 4
        + [v((slots, total, two)), v((n, slots, total, two)), v((slots * micro, rows, n * rows), f32)]
        + [v((slots, total, 2 * two))]
        + [v(wide)] * 4
        + [v((m, chunk, width))] * 4
        + [v(wide)] * 3
        + [v((total, ff)), v((total, ff), f32), v((total, ff)), v((chunk, width), f32), v((chunk, width), f32)]
        + [v((n, slots, total, two))] * 2
        + [v((slots, total, 2 * two)), v((2, width, ff)), v((n, 2, depth, ff))]
        + [v((slots, width, 2 * two)), v((n, slots, depth, 2 * two)), v((m, slots, padded, 2 * two))]
        + [v((16, width), f32), v((slots, 1, two), f32), v((n, 16, width), f32)]
        + [v((chunk, width))] * 2
        + [dma(m - 1), dma(m), dma(n - 1), dma(n), dma(2 * n), dma(n - 1), dma(n), dma(2 * n)]
        + [dma(slots * (n - 1)), dma(slots * n)]
        + [dma(4 * (m - 1)), dma(4 * m), dma(2 * (m - 1)), dma(2 * m), dma(m), dma(m), dma(m - 1), dma(m)]
        + [dma(slots * (n - 1)), dma(slots * n)]
        + [dma(n - 1), dma(n)] * 3
        + [dma(m - 1), dma(m)] * 2
        + [dma(3), pltpu.SemaphoreType.REGULAR]
    )
    shapes = [
        jax.ShapeDtypeStruct(wide, f32),
        jax.ShapeDtypeStruct((2, depth, ff), f32),
        jax.ShapeDtypeStruct((m, slots, padded, 2 * two), low),
        jax.ShapeDtypeStruct((16, width), f32),
        jax.ShapeDtypeStruct((16, width), f32),
        jax.ShapeDtypeStruct((m, 16, width), f32),
    ]
    sizes = (rows, width, ff, slots, micro, head_dim, part, padded)
    out, g_mlp, g_attn, vec_sum, vec_own, vec_wa = pl.pallas_call(
        functools.partial(step_kernel, n, m, sizes, scale),
        out_shape=shapes,
        in_specs=[VM] * 7 + [pl.BlockSpec(memory_space=pltpu.SMEM)],
        out_specs=[VM] * len(shapes),
        scratch_shapes=scratch,
        compiler_params=pltpu.CompilerParams(
            collective_id=IDS["step"], has_side_effects=True, vmem_limit_bytes=60 * 1024 * 1024
        ),
        name="step",
    )(
        section_inputs.reshape(total, width),
        pack,
        mlp_weight[0],
        bias,
        hidden_bias,
        feature_bias[0],
        ln_gain[0],
        block_table,
    )
    g_attn = g_attn.transpose(1, 0, 2, 3).reshape(slots * m, padded, 2 * two)[:heads, :part].astype(f32)
    g_value, g_key, g_out, g_query = (g_attn[:, :, i * head_dim : (i + 1) * head_dim] for i in range(4))
    g_heads = vec_wa[:, 8 : 8 + slots, :two].transpose(1, 0, 2).reshape(slots * m, two)[:heads]
    g_heads = jnp.concatenate([g_heads[:, head_dim:], g_heads[:, :head_dim]], axis=-1)
    return (
        out.reshape(1, micro, rows, width),
        jnp.concatenate([g_query, g_key, g_value], axis=-1)[None],
        g_out[None],
        g_heads[None],
        g_mlp[None],
        vec_own[6:7, :ff],
        vec_sum[None, 0:4],
        vec_sum[None, 4:6],
    )


def fits(mesh, rows, micro, width, ff):
    n, m = mesh.shape["ctx"], mesh.shape["wa"]
    depth, chunk = width // n, micro * rows // m
    return n <= 4 and m <= 4 and depth % 16 == 0 and chunk % 16 == 0 and ff <= width and rows % 16 == 0


def either(mesh, *args):
    micro, rows, width = args[0].shape[1:]
    if fits(mesh, rows, micro, width, args[4].shape[3]):
        return whole_step(*args)
    return per_device(*args)


def solution(mesh):
    return jax.shard_map(
        functools.partial(either, mesh),
        mesh=mesh,
        in_specs=(
            P("pipe", None, "ctx", None),
            P("pipe", None, ("ctx", "wa"), None),
            P("pipe", None, ("ctx", "wa"), None),
            P("pipe", None, None),
            P("pipe", None, "ctx", "wa"),
            P("pipe", "wa"),
            P("pipe", None, None),
            P("pipe", None, None),
            P(),
        ),
        out_specs=(
            P("pipe", None, "ctx", None),
            P("pipe", None, ("ctx", "wa"), None),
            P("pipe", None, ("ctx", "wa"), None),
            P("pipe", None, None),
            P("pipe", None, "ctx", "wa"),
            P("pipe", "wa"),
            P("pipe", None, None),
            P("pipe", None, None),
        ),
        check_vma=False,
    )
```

```python
import functools

import jax
import jax.numpy as jnp
from jax import lax
from jax.experimental import pallas as pl
from jax.experimental.pallas import tpu as pltpu
from jax.sharding import PartitionSpec as P

EPS = 1e-05
GELU_C = 0.7978845608028654
GELU_A = 0.044715
KERNELS = True
MESH = pl.DeviceIdType.MESH
VM = pl.BlockSpec(memory_space=pltpu.VMEM)
IDS = {"sum_wa": 1, "swap_wa": 2, "swap_ctx": 3, "line_attn": 4, "line_mlp": 5, "line_pair": 6, "swap_mlp": 7,
       "swap_attn": 8, "all_small": 9, "all_heads": 10, "swap_grad": 11, "step": 12}


def remote(src, dst, send, recv, peer):
    return pltpu.make_async_remote_copy(
        src_ref=src, dst_ref=dst, send_sem=send, recv_sem=recv, device_id=peer, device_id_type=MESH
    )


def greet(peers):
    barrier = pltpu.get_barrier_semaphore()
    for peer in peers:
        pl.semaphore_signal(barrier, inc=1, device_id=peer, device_id_type=MESH)
    pl.semaphore_wait(barrier, len(peers))


def sum_kernel(axis, n, x_ref, o_ref, got, send_a, recv_a, send_b, recv_b):
    me = lax.axis_index(axis)
    peers = [{axis: lax.rem(me + d, n)} for d in range(1, n)]
    greet(peers)
    first = [
        remote(x_ref.at[lax.rem(me + d, n)], got.at[d - 1], send_a.at[d - 1], recv_a.at[d - 1], peers[d - 1])
        for d in range(1, n)
    ]
    for copy in first:
        copy.start()
    total = x_ref[me].astype(jnp.float32)
    for d, copy in enumerate(first):
        copy.wait_recv()
        total = total + got[d].astype(jnp.float32)
    o_ref[me] = total.astype(o_ref.dtype)
    second = [
        remote(o_ref.at[me], o_ref.at[me], send_b.at[d - 1], recv_b.at[d - 1], peers[d - 1]) for d in range(1, n)
    ]
    for copy in second:
        copy.start()
    for copy in first:
        copy.wait_send()
    for copy in second:
        copy.wait()


def swap_kernel(axis, n, x_ref, o_ref, send, recv, local):
    me = lax.axis_index(axis)
    peers = [{axis: lax.rem(me + d, n)} for d in range(1, n)]
    greet(peers)
    copies = [
        remote(x_ref.at[lax.rem(me + d, n)], o_ref.at[me], send.at[d - 1], recv.at[d - 1], peers[d - 1])
        for d in range(1, n)
    ]
    for copy in copies:
        copy.start()
    own = pltpu.make_async_copy(x_ref.at[me], o_ref.at[me], local)
    own.start()
    own.wait()
    for copy in copies:
        copy.wait()


def all_kernel(axis, n, x_ref, o_ref, send, recv, local):
    me = lax.axis_index(axis)
    peers = [{axis: lax.rem(me + d, n)} for d in range(1, n)]
    greet(peers)
    copies = [
        remote(x_ref, o_ref.at[me], send.at[d - 1], recv.at[d - 1], peers[d - 1]) for d in range(1, n)
    ]
    for copy in copies:
        copy.start()
    own = pltpu.make_async_copy(x_ref, o_ref.at[me], local)
    own.start()
    own.wait()
    for copy in copies:
        copy.wait()


def line_kernel(n, both, x_ref, o_ref, send_r, recv_r, send_l, recv_l, send_p, recv_p, local):
    me = lax.axis_index("ctx")
    side = lax.axis_index("pipe")
    row = side if both else 0
    right, left, mate = {"ctx": me + 1}, {"ctx": me - 1}, {"pipe": 1 - side}
    barrier = pltpu.get_barrier_semaphore()
    not_last, not_first = me + 1 < n, me > 0

    @pl.when(not_last)
    def _():
        pl.semaphore_signal(barrier, inc=1, device_id=right, device_id_type=MESH)

    @pl.when(not_first)
    def _():
        pl.semaphore_signal(barrier, inc=1, device_id=left, device_id_type=MESH)

    if both:
        pl.semaphore_signal(barrier, inc=1, device_id=mate, device_id_type=MESH)
    extra = 1 if both else 0

    @pl.when(not_first & not_last)
    def _():
        pl.semaphore_wait(barrier, 2 + extra)

    @pl.when(jnp.logical_not(not_first & not_last))
    def _():
        pl.semaphore_wait(barrier, 1 + extra)

    own = pltpu.make_async_copy(x_ref, o_ref.at[row, me], local)
    own.start()

    def block(at, fresh):
        return x_ref if fresh else o_ref.at[row, at]

    def to_right(s):
        return remote(block(me - s, s == 0), o_ref.at[row, me - s], send_r.at[s], recv_r.at[s], right)

    def to_left(s):
        return remote(block(me + s, s == 0), o_ref.at[row, me + s], send_l.at[s], recv_l.at[s], left)

    def to_mate(at, fresh):
        return remote(block(at, fresh), o_ref.at[row, at], send_p.at[at], recv_p.at[at], mate)

    def arrived(at, sem):
        return remote(o_ref.at[row, at], o_ref.at[row, at], send_r.at[0], sem, mate)

    for s in range(n):

        @pl.when(me - s >= 0)
        def _():
            if s > 0:
                arrived(me - s, recv_r.at[s - 1]).wait_recv()
            if s < n - 1:

                @pl.when(not_last)
                def _():
                    to_right(s).start()

            if both and s > 0:
                to_mate(me - s, False).start()

        @pl.when(me + s < n)
        def _():
            if s > 0:
                arrived(me + s, recv_l.at[s - 1]).wait_recv()
            if s < n - 1:

                @pl.when(not_first)
                def _():
                    to_left(s).start()

            if both:
                to_mate(me + s, s == 0).start()

    own.wait()
    for s in range(n - 1):

        @pl.when((me - s >= 0) & not_last)
        def _():
            to_right(s).wait_send()

        @pl.when((me + s < n) & not_first)
        def _():
            to_left(s).wait_send()

    if both:
        for at in range(n):
            to_mate(at, False).wait_send()
            remote(o_ref.at[1 - side, at], o_ref.at[1 - side, at], send_p.at[at], recv_p.at[at], mate).wait_recv()


def call(kernel, name, shape, scratch, x):
    return pl.pallas_call(
        kernel,
        out_shape=jax.ShapeDtypeStruct(shape, x.dtype),
        in_specs=[VM],
        out_specs=VM,
        scratch_shapes=scratch,
        compiler_params=pltpu.CompilerParams(
            collective_id=IDS[name], has_side_effects=True, vmem_limit_bytes=60 * 1024 * 1024
        ),
        name=name,
    )(x)


def dma(count):
    return pltpu.SemaphoreType.DMA((count,))


def summed(x):
    n = lax.axis_size("wa")
    low = x.astype(jnp.bfloat16)
    if not KERNELS:
        return lax.psum(low.astype(jnp.float32), "wa").astype(jnp.bfloat16).astype(jnp.float32)
    parts = low.reshape(n, low.shape[0] // n, low.shape[1])
    scratch = [pltpu.VMEM((n - 1,) + parts.shape[1:], jnp.bfloat16)] + [dma(n - 1)] * 4
    out = call(functools.partial(sum_kernel, "wa", n), "sum_wa", parts.shape, scratch, parts)
    return out.reshape(low.shape).astype(jnp.float32)


def swapped(x, axis, name):
    n = lax.axis_size(axis)
    if not KERNELS:
        return lax.all_to_all(x, axis, split_axis=0, concat_axis=0, tiled=True)
    scratch = [dma(n - 1)] * 2 + [pltpu.SemaphoreType.DMA]
    return call(functools.partial(swap_kernel, axis, n), name, x.shape, scratch, x)


def gathered(x, axis, name):
    n = lax.axis_size(axis)
    if not KERNELS:
        return lax.all_gather(x, axis)
    scratch = [dma(n - 1)] * 2 + [pltpu.SemaphoreType.DMA]
    return call(functools.partial(all_kernel, axis, n), name, (n,) + x.shape, scratch, x)


def lined(x, both, name):
    n = lax.axis_size("ctx")
    if not KERNELS:
        out = lax.all_gather(x, "ctx")
        return lax.all_gather(out, "pipe") if both else out[None]
    scratch = [dma(n - 1)] * 4 + [dma(n)] * 2 + [pltpu.SemaphoreType.DMA]
    return call(functools.partial(line_kernel, n, both), name, (2 if both else 1, n) + x.shape, scratch, x)


def dot(a, b, ca, cb):
    return lax.dot_general(a, b, (((ca,), (cb,)), ((), ())), preferred_element_type=jnp.float32)


def attend_kernel(scale, qpos, kpos, q_ref, kv_ref, mix_ref, total_ref):
    heads = q_ref.shape[0]
    allowed = kpos[...] <= qpos[...]
    for h in range(heads):
        kv = kv_ref[:, h].reshape(-1, kv_ref.shape[-1])
        scores = jnp.where(allowed, dot(q_ref[h], kv, 1, 1) * scale, -jnp.inf)
        top = jnp.max(scores, axis=-1, keepdims=True)
        total = top + jnp.log(jnp.sum(jnp.exp(scores - top), axis=-1, keepdims=True))
        probs = jnp.exp(scores - total).astype(jnp.bfloat16)
        mix_ref[h] = dot(probs, kv, 1, 0).astype(jnp.bfloat16)
        total_ref[h] = total


def attend_back_kernel(scale, qpos, kpos, q_ref, kv_ref, dm_ref, total_ref, dq_ref, dkv_ref):
    heads = q_ref.shape[0]
    allowed = kpos[...] <= qpos[...]
    for h in range(heads):
        kv = kv_ref[:, h].reshape(-1, kv_ref.shape[-1])
        scores = jnp.where(allowed, dot(q_ref[h], kv, 1, 1) * scale, -jnp.inf)
        probs = jnp.exp(scores - total_ref[h])
        d_probs = dot(dm_ref[h], kv, 1, 1)
        delta = jnp.sum(probs * d_probs, axis=-1, keepdims=True)
        d_scores = (probs * (d_probs - delta) * scale).astype(jnp.bfloat16)
        dq_ref[h] = dot(d_scores, kv, 1, 0)
        d_kv = dot(d_scores, q_ref[h], 0, 0) + dot(probs.astype(jnp.bfloat16), dm_ref[h], 0, 0)
        dkv_ref[:, h] = d_kv.astype(jnp.bfloat16).reshape(dkv_ref.shape[0], dkv_ref.shape[2], dkv_ref.shape[3])


def local_call(kernel, shapes, *args):
    return pl.pallas_call(
        kernel,
        out_shape=[jax.ShapeDtypeStruct(*s) for s in shapes],
        in_specs=[VM] * len(args),
        out_specs=[VM] * len(shapes),
        compiler_params=pltpu.CompilerParams(vmem_limit_bytes=48 * 1024 * 1024),
        interpret=not KERNELS,
    )(*args)

def norm_forward(stream, gain, offset):
    centre = jnp.mean(stream, axis=-1, keepdims=True)
    centred = stream - centre
    variance = jnp.mean(centred * centred, axis=-1, keepdims=True)
    inv_std = lax.rsqrt(variance + EPS)
    normed = centred * inv_std
    return (normed * gain + offset, normed, inv_std)


def norm_backward(grad_out, normed, inv_std, gain):
    grad_normed = grad_out * gain
    first_mean = jnp.mean(grad_normed, axis=-1, keepdims=True)
    second_mean = jnp.mean(grad_normed * normed, axis=-1, keepdims=True)
    return inv_std * (grad_normed - first_mean - normed * second_mean)


def gelu_value(hidden):
    tangent = jnp.tanh(GELU_C * (hidden + GELU_A * hidden * hidden * hidden))
    return 0.5 * hidden * (1.0 + tangent)


def gelu_slope(hidden):
    tangent = jnp.tanh(GELU_C * (hidden + GELU_A * hidden * hidden * hidden))
    return 0.5 * (1.0 + tangent) + 0.5 * hidden * (1.0 - tangent * tangent) * GELU_C * (
        1.0 + 3.0 * GELU_A * hidden * hidden
    )


def per_device(
    section_inputs,
    qkv_weight,
    out_weight,
    head_bias,
    mlp_weight,
    hidden_bias,
    feature_bias,
    ln_gain,
    block_table,
):
    ctx_count = lax.axis_size("ctx")
    shard_count = lax.axis_size("wa")
    side = lax.axis_index("pipe")
    ctx_index = lax.axis_index("ctx")
    shard_index = lax.axis_index("wa")
    rows = section_inputs.shape[2]
    width = section_inputs.shape[3]
    head_count = qkv_weight.shape[1]
    head_dim = out_weight.shape[3]
    part = qkv_weight.shape[2]
    slots = (head_count + shard_count - 1) // shard_count
    pad = slots * shard_count - head_count
    block_rows = rows // 2
    scale = head_dim ** (-0.5)
    swap = [(0, 1), (1, 0)]
    low = jnp.bfloat16

    own_blocks = lax.dynamic_index_in_dim(block_table, ctx_index, 0, keepdims=False)
    step = jnp.arange(block_rows, dtype=jnp.int32)
    query_pos = (own_blocks[:, None] * block_rows + step[None, :]).reshape(rows, 1)
    key_pos = (block_table.reshape(-1)[:, None] * block_rows + step[None, :]).reshape(1, rows * ctx_count)

    def mine(first, second):
        return jnp.where(side == 0, first, second)

    inputs = section_inputs[0]
    traded = lax.ppermute(mine(inputs[1], inputs[0]), "pipe", swap)
    layer_input = mine(inputs[0], traded)
    last_cot = mine(traded, inputs[1])

    packed = jnp.concatenate([qkv_weight[0], out_weight[0]], axis=-1)
    packed = jnp.pad(packed, ((0, pad), (0, 0), (0, 0)))
    packed = packed.reshape(slots, shard_count, part, 4 * head_dim).transpose(1, 0, 2, 3)
    attn_all = lined(swapped(packed, "wa", "swap_wa"), True, "line_attn")
    mlp_all = lined(mlp_weight[0], True, "line_mlp")

    sizes = [head_bias[0].size, hidden_bias[0].size, feature_bias[0].size]
    small = jnp.concatenate(
        [head_bias[0].reshape(-1), hidden_bias[0], feature_bias[0].reshape(-1), ln_gain[0].reshape(-1)]
    )
    small_mate = lax.ppermute(small, "pipe", swap)

    def params_of(layer):
        weight = attn_all[layer].transpose(2, 0, 1, 3, 4).reshape(slots, width, 4 * head_dim)
        up = mlp_all[layer][:, 0].reshape(width, -1)
        down = mlp_all[layer][:, 1].reshape(width, -1)
        flat = jnp.where(side == layer, small, small_mate)
        heads, hidden, feature, gains = jnp.split(flat, [sizes[0], sizes[0] + sizes[1], sum(sizes)])
        heads = jnp.pad(heads.reshape(head_count, 2 * head_dim), ((0, pad), (0, 0)))
        heads = heads.reshape(slots, shard_count, 2 * head_dim)
        heads = lax.dynamic_index_in_dim(heads, shard_index, 1, keepdims=False)
        return (
            weight[:, :, : 3 * head_dim],
            weight[:, :, 3 * head_dim :],
            heads,
            up,
            down,
            hidden,
            feature.reshape(4, width),
            gains.reshape(2, width),
        )

    def widened(x, before):
        zero = jnp.zeros_like(x)
        return jnp.concatenate([zero, x] if before else [x, zero], axis=-1)

    def forward(layer_in, params):
        w_qkv, w_out, bias, w_up, w_down, bias_hidden, shifts, gains = params
        stream = layer_in.astype(jnp.float32)
        normed_in, normed_one, inv_one = norm_forward(stream, gains[0], shifts[0])
        attn_in = normed_in.astype(low)
        projected = jnp.einsum("td,hde->hte", attn_in, w_qkv, preferred_element_type=jnp.float32)
        queries = widened((projected[:, :, :head_dim] + bias[:, None, :head_dim]).astype(low), False)
        key_rows = projected[:, :, head_dim : 2 * head_dim].astype(low)
        values = (projected[:, :, 2 * head_dim :] + bias[:, None, head_dim:]).astype(low)
        pairs = lined(jnp.concatenate([key_rows, values], axis=-1), False, "line_pair")[0]
        mixed, log_total = local_call(
            functools.partial(attend_kernel, scale),
            [((slots, rows, 2 * head_dim), low), ((slots, rows, 1), jnp.float32)],
            query_pos,
            key_pos,
            queries,
            pairs,
        )
        mixed = mixed[:, :, head_dim:]
        attn_out = summed(jnp.einsum("hte,hde->td", mixed, w_out, preferred_element_type=jnp.float32))
        first_sum = stream + attn_out + shifts[1]
        normed_ffn, normed_two, inv_two = norm_forward(first_sum, gains[1], shifts[2])
        ffn_in = normed_ffn.astype(low)
        pre = jnp.dot(ffn_in, w_up, preferred_element_type=jnp.float32) + bias_hidden
        act = gelu_value(pre).astype(low)
        layer_out = (
            first_sum
            + summed(jnp.einsum("tf,df->td", act, w_down, preferred_element_type=jnp.float32))
            + shifts[3]
        )
        return layer_out, (
            normed_one, inv_one, attn_in, queries, pairs, mixed, log_total, normed_two, inv_two, ffn_in, pre, act,
        )

    def backward(cot, saved, params):
        w_qkv, w_out, bias, w_up, w_down, bias_hidden, shifts, gains = params
        normed_one, inv_one, attn_in, queries, pairs, mixed, log_total, normed_two, inv_two, ffn_in, pre, act = saved
        cotangent = cot.astype(jnp.float32)
        grad_down = jnp.einsum("ti,tf->if", cot, act, preferred_element_type=jnp.float32)
        d_act = jnp.einsum("ti,if->tf", cot, w_down, preferred_element_type=jnp.float32)
        d_pre = d_act * gelu_slope(pre)
        grad_hidden = jnp.sum(d_pre, axis=0)
        d_pre_low = d_pre.astype(low)
        grad_up = jnp.einsum("td,tf->df", ffn_in, d_pre_low, preferred_element_type=jnp.float32)
        d_ffn = summed(jnp.einsum("tf,df->td", d_pre_low, w_up, preferred_element_type=jnp.float32))
        d_first = cotangent + norm_backward(d_ffn, normed_two, inv_two, gains[1])
        d_first_low = d_first.astype(low)
        grad_out = jnp.einsum("ti,hte->hie", d_first_low, mixed, preferred_element_type=jnp.float32)
        d_mixed = jnp.einsum("ti,hie->hte", d_first_low, w_out, preferred_element_type=jnp.float32)
        d_query, pair_terms = local_call(
            functools.partial(attend_back_kernel, scale),
            [((slots, rows, 2 * head_dim), jnp.float32), (pairs.shape, low)],
            query_pos,
            key_pos,
            queries,
            pairs,
            widened(d_mixed.astype(low), True),
            log_total,
        )
        d_query = d_query[:, :, :head_dim]
        d_pair = swapped(pair_terms, "ctx", "swap_ctx").astype(jnp.float32).sum(axis=0)
        grad_heads = jnp.concatenate(
            [jnp.sum(d_query, axis=1), jnp.sum(d_pair[:, :, head_dim:], axis=1)], axis=-1
        )
        d_proj = jnp.concatenate([d_query.astype(low), d_pair.astype(low)], axis=-1)
        grad_qkv = jnp.einsum("td,hte->hde", attn_in, d_proj, preferred_element_type=jnp.float32)
        d_attn = summed(jnp.einsum("hte,hde->td", d_proj, w_qkv, preferred_element_type=jnp.float32))
        d_input = d_first + norm_backward(d_attn, normed_one, inv_one, gains[0])
        vectors = [
            jnp.sum(d_attn, axis=0),
            jnp.sum(d_first, axis=0),
            jnp.sum(d_ffn, axis=0),
            jnp.sum(cotangent, axis=0),
            jnp.sum(d_attn * normed_one, axis=0),
            jnp.sum(d_ffn * normed_two, axis=0),
            grad_hidden,
            grad_heads.reshape(-1),
        ]
        attn_grad = jnp.concatenate([grad_qkv, grad_out], axis=-1).astype(low)
        mlp_grad = jnp.stack([grad_up, grad_down]).astype(low)
        return d_input, attn_grad, mlp_grad, jnp.concatenate(vectors)

    params = [params_of(0), params_of(1)]
    first_out, first_saved = forward(layer_input, params[0])
    last_out, last_saved = forward(first_out.astype(low), params[1])
    back, attn_one, mlp_one, vec_one = backward(last_cot, last_saved, params[1])
    d_input, attn_zero, mlp_zero, vec_zero = backward(back.astype(low), first_saved, params[0])

    def over_pipe(zero, one):
        kept = mine(zero, one)
        got = lax.ppermute(mine(one, zero), "pipe", swap)
        return kept.astype(jnp.float32) + got.astype(jnp.float32)

    mlp_sum = over_pipe(mlp_zero, mlp_one).astype(low)
    mlp_sum = mlp_sum.reshape(2, ctx_count, width // ctx_count, -1).transpose(1, 0, 2, 3)
    mlp_out = swapped(mlp_sum, "ctx", "swap_mlp").astype(jnp.float32).sum(axis=0)

    attn_sum = over_pipe(attn_zero, attn_one).astype(low)
    attn_sum = attn_sum.reshape(slots, ctx_count, shard_count, part, 4 * head_dim).transpose(1, 2, 0, 3, 4)
    attn_part = swapped(attn_sum, "ctx", "swap_attn").astype(jnp.float32).sum(axis=0).astype(low)
    attn_out = swapped(attn_part, "wa", "swap_grad")
    attn_out = attn_out.transpose(1, 0, 2, 3).reshape(slots * shard_count, part, 4 * head_dim)
    attn_out = attn_out[:head_count].astype(jnp.float32)

    vec = over_pipe(vec_zero, vec_one)
    length = vec.shape[0]
    fill = -length % 128
    vec = jnp.pad(vec, (0, fill)).reshape(-1, 128)
    vec = gathered(vec, "ctx", "all_small").sum(axis=0).reshape(-1)[:length]
    feature_sum, gain_sum, hidden_own, head_own = jnp.split(
        vec, [4 * width, 6 * width, 6 * width + hidden_bias.shape[1]]
    )
    head_sum = gathered(head_own.reshape(slots, 2 * head_dim), "wa", "all_heads")
    head_sum = head_sum.transpose(1, 0, 2).reshape(slots * shard_count, 2 * head_dim)[:head_count]

    last_traded = lax.ppermute(mine(last_out, d_input), "pipe", swap)
    section_outputs = jnp.where(
        side == 0, jnp.stack([d_input, last_traded]), jnp.stack([last_traded, last_out])
    )
    return (
        section_outputs[None],
        attn_out[None, :, :, : 3 * head_dim],
        attn_out[None, :, :, 3 * head_dim :],
        head_sum[None],
        mlp_out[None],
        hidden_own[None],
        feature_sum.reshape(1, 4, width),
        gain_sum.reshape(1, 2, width),
    )


def tiles_of(total, size=256):
    return [(at, min(size, total - at)) for at in range(0, total, size)]


def shares(ff, n, m):
    share = ff // 128 // n * 128
    return share, ff - n * share


def step_kernel(n, m, sizes, scale, *refs):
    rows, width, ff, slots, micro, head_dim, part, padded = sizes
    (
        inp, pack, mlp, bias, hidden, shift, gain, table,
        out, g_mlp, g_attn, vec_sum, vec_own, vec_all,
        w_in, stage, wt, mt, xin, xx, hid_all, hid, a_s, q_s, pair, prob, mix,
        p1, p2, r1, r2, r3, r4, fi, dh, ost, ob, act, slope, dpre, h1, dh1,
        dpair, rpair, dproj, gm, rgm, rgh, sm, smh, zg, zh, ra, s2, sv, hv, svc, snd1, snd2,
        ssem, rsem, loc, go,
    ) = refs
    side = lax.axis_index("pipe")
    c = lax.axis_index("ctx")
    w = lax.axis_index("wa")
    total = micro * rows
    chunk = total // n
    depth = width // n
    share, rest = shares(ff, n, m)
    tail = slice(n * share, ff)
    two = 2 * head_dim
    low = jnp.bfloat16
    f32 = jnp.float32
    mate = {"pipe": 1 - side}
    later = []
    used = [0, 0]

    def take(sends, recvs):
        at = tuple(used)
        used[0] += sends
        used[1] += recvs
        return at

    ctx_peers = [lax.rem(c + d, n) for d in range(1, n)]
    wa_peers = [lax.rem(w + d, m) for d in range(1, m)]

    greet(
        [{"ctx": peer} for peer in ctx_peers]
        + [{"wa": peer} for peer in wa_peers]
        + [{"pipe": 1 - side, "ctx": peer} for peer in [c] + ctx_peers]
    )

    def arrive(ref, sem):
        remote(ref, ref, sem, sem, mate).wait_recv()

    def exchange(axis, src, dst, times=1):
        me, count, peers = (c, n, ctx_peers) if axis == "ctx" else (w, m, wa_peers)
        s0, r0 = take(times * (count - 1), times * count)

        def copy(d, peer, t):
            return remote(
                src(peer, t), dst(me, t), ssem.at[s0 + t * (count - 1) + d], rsem.at[r0 + t * count + me], {axis: peer}
            )

        def start(t=0):
            for d, peer in enumerate(peers):
                copy(d, peer, t).start()

        def got(t=0):
            for peer in peers:
                arrive(dst(peer, t), rsem.at[r0 + t * count + peer])

        def drain():
            def one(t, _):
                for d, peer in enumerate(peers):
                    copy(d, peer, t).wait_send()
                return 0

            if times == 1:
                one(0, 0)
            else:
                lax.fori_loop(0, times, one, 0)

        later.append(drain)
        return start, got

    def single(cond_send, src, dst, peer, cond_recvs, slot):
        s0, r0 = take(1, max(n, m))

        def copy():
            return remote(src, dst(slot), ssem.at[s0], rsem.at[r0 + slot], peer)

        def start():
            pl.when(cond_send)(lambda: copy().start())

        def got():
            for cond, p in cond_recvs:
                pl.when(cond)(functools.partial(arrive, dst(p), rsem.at[r0 + p]))

        later.append(lambda: pl.when(cond_send)(lambda: copy().wait_send()))
        return start, got

    def crows(at):
        return pl.ds(pl.multiple_of(at * depth, 16), depth)

    def chunks(at):
        return pl.ds(pl.multiple_of(at * chunk, 16), chunk)

    def lanes(at):
        return pl.ds(pl.multiple_of(at * share, 128), share)

    own = chunks(c)
    diagonal = c == w

    at_z = exchange("ctx", lambda p, t: pack.at[p], lambda me, t: w_in.at[w, me])
    at_p = exchange("wa", lambda p, t: w_in.at[w], lambda me, t: w_in.at[me])
    x_z = exchange("ctx", lambda p, t: inp.at[chunks(w), :], lambda me, t: xin.at[me])
    x_p = exchange("wa", lambda p, t: xin.at[p], lambda me, t: xx.at[0, chunks(me), :])
    hid_p = exchange("wa", lambda p, t: hidden, lambda me, t: hid_all.at[me])
    ml_z = exchange("ctx", lambda p, t: mlp.at[:, :, lanes(p)], lambda me, t: mt.at[:, crows(me), lanes(w)])
    ml_p = exchange("wa", lambda p, t: mt.at[:, :, lanes(w)], lambda me, t: mt.at[:, :, lanes(me)])
    mh_z = single(
        jnp.logical_not(diagonal), mlp.at[:, :, tail], lambda at: mt.at[:, crows(at), tail], {"ctx": w},
        [(diagonal, p) for p in ctx_peers], c,
    )
    mh_s, mh_r = take(m - 1, 1)

    def mh_copy(d, peer):
        return remote(mt.at[:, :, tail], mt.at[:, :, tail], ssem.at[mh_s + d], rsem.at[mh_r], {"wa": peer})

    own_pack = pltpu.make_async_copy(pack.at[c], w_in.at[w, c], loc.at[0])
    own_mlp = pltpu.make_async_copy(mlp.at[:, :, lanes(c)], mt.at[:, crows(c), lanes(w)], loc.at[1])
    own_x = pltpu.make_async_copy(inp.at[chunks(w), :], xin.at[c], loc.at[2])
    own_half = pltpu.make_async_copy(mlp.at[:, :, tail], mt.at[:, crows(c), tail], loc.at[3])

    own_pack.start()
    own_mlp.start()
    own_x.start()
    pl.when(diagonal)(lambda: own_half.start())

    pl.when(side == 1)(lambda: pl.semaphore_wait(go, 1))
    at_z[0]()
    x_z[0]()
    hid_p[0]()
    stage[...] = jnp.zeros_like(stage)
    mix[...] = jnp.zeros_like(mix)
    sv[...] = jnp.zeros_like(sv)
    own_pack.wait()
    at_z[1]()
    at_p[0]()
    ml_z[0]()
    mh_z[0]()
    own_x.wait()
    x_z[1]()
    x_p[0]()
    xx[0, chunks(w), :] = xin[w]
    hid_p[1]()
    hid_all[w] = hidden[...]
    for p in range(m):
        hid[:, p * share : (p + 1) * share] = hid_all[p, :, lanes(c)]
    hid[:, tail] = hid_all[c, :, tail]
    x_p[1]()
    x_ss, x_rs = take(n, n)
    x_at = side
    c_at = 1 - side

    def norm(stream):
        centre = jnp.mean(stream, axis=-1, keepdims=True)
        centred = stream - centre
        variance = jnp.mean(centred * centred, axis=-1, keepdims=True)
        inv_std = lax.rsqrt(variance + EPS)
        return centred * inv_std, inv_std

    def first_norm():
        for at, size in tiles_of(total, 64):
            normed, _ = norm(xx[x_at, at : at + size, :].astype(f32))
            a_s[at : at + size, :] = (normed * gain[0:1, :] + shift[0:1, :]).astype(low)

    pl.when(side == 0)(first_norm)
    at_p[1]()
    own_mlp.wait()
    ml_z[1]()
    ml_p[0]()

    @pl.when(diagonal)
    def _():
        own_half.wait()

    mh_z[1]()

    @pl.when(diagonal)
    def _():
        for d, peer in enumerate(wa_peers):
            mh_copy(d, peer).start()

    def mh_drain():
        for d, peer in enumerate(wa_peers):
            mh_copy(d, peer).wait_send()

    later.append(lambda: pl.when(diagonal)(mh_drain))

    def lay(s, _):
        for j in range(n):
            for p in range(m):
                at = (j * m + p) * part
                stage[at : at + part, :] = w_in[p, j, s].astype(f32)[:part]
        wt[s] = stage[:width, :].astype(low)
        return 0

    lax.fori_loop(0, slots, lay, 0)

    @pl.when(side == 1)
    def _():
        for p in range(n):
            arrive(xx.at[1, chunks(p), :], rsem.at[x_rs + p])
        first_norm()

    upper = lax.broadcasted_iota(jnp.int32, (1, two), 1) >= head_dim
    pairs = exchange("wa", lambda p, t: pair.at[w, t], lambda me, t: pair.at[me, t], slots)

    def project(s, _):
        made = dot(a_s[...], wt[s], 1, 0) + bias[s * n + c]
        pair[w, s] = made[:, :two].astype(low)
        q_s[s] = jnp.where(upper, made[:, two:], 0.0).astype(low)
        pairs[0](s)
        return 0

    lax.fori_loop(0, slots, project, 0)

    block = rows // 2
    step = lax.broadcasted_iota(jnp.int32, (rows, 1), 0)
    qpos = jnp.where(step < block, table[w, 0] * block + step, table[w, 1] * block + step - block)
    along = lax.broadcasted_iota(jnp.int32, (1, m * rows), 1)
    kpos = along
    for i in range(2 * m):
        inside = (along >= i * block) & (along < (i + 1) * block)
        kpos = jnp.where(inside, table[i // 2, i % 2] * block + along - i * block, kpos)

    def attend(s, _):
        pairs[1](s)
        for b in range(micro):
            mine = slice(b * rows, (b + 1) * rows)
            kv = pair[:, s, mine, :].reshape(m * rows, two)
            scores = jnp.where(kpos <= qpos, dot(q_s[s, mine, :], kv, 1, 1) * scale, -jnp.inf)
            top = jnp.max(scores, axis=-1, keepdims=True)
            raised = jnp.exp(scores - top)
            weight = raised / jnp.sum(raised, axis=-1, keepdims=True)
            prob[s * micro + b] = weight
            mixed = dot(weight.astype(low), kv, 1, 0)
            mix[s, mine, two:] = jnp.where(upper, 0.0, mixed).astype(low)
        return 0

    lax.fori_loop(0, slots, attend, 0)

    def summing(part_s, got_s):
        start, got = exchange("ctx", lambda p, t: part_s.at[chunks(p), :], lambda me, t: got_s.at[me])

        def finish():
            value = part_s[own, :].astype(f32)
            got()
            for p in ctx_peers:
                value = value + got_s[p].astype(f32)
            return value

        return start, finish, later[-1]

    sum1 = summing(p1, r1)
    for at, size in tiles_of(width):
        value = dot(mix[0, :, two:], wt[0, at : at + size, two:], 1, 1)
        for s in range(1, slots):
            value = value + dot(mix[s, :, two:], wt[s, at : at + size, two:], 1, 1)
        p1[:, at : at + size] = value.astype(low)
    sum1[0]()
    value = sum1[1]()
    value = xx[x_at, own, :].astype(f32) + value + shift[1:2, :]
    h1[...] = value
    normed, _ = norm(value)
    fi[own, :] = (normed * gain[1:2, :] + shift[2:3, :]).astype(low)
    fi_ag = exchange("ctx", lambda p, t: fi.at[own, :], lambda me, t: fi.at[chunks(me), :])
    fi_ag[0]()
    ml_p[1]()
    pl.when(jnp.logical_not(diagonal))(lambda: arrive(mt.at[:, :, tail], rsem.at[mh_r]))

    @pl.when(side == 0)
    def _():
        pl.semaphore_signal(go, inc=1, device_id=mate, device_id_type=MESH)

    fi_ag[1]()

    for at, size in tiles_of(ff):
        pre = dot(fi[...], mt[0, :, at : at + size], 1, 0) + hid[:, at : at + size]
        square = pre * pre
        tangent = jnp.tanh(GELU_C * (pre + GELU_A * square * pre))
        act[:, at : at + size] = (0.5 * pre * (1.0 + tangent)).astype(low)
        slope[:, at : at + size] = 0.5 * (1.0 + tangent) + 0.5 * pre * (1.0 - tangent * tangent) * GELU_C * (
            1.0 + 3.0 * GELU_A * square
        )
    sum2 = summing(p2, r2)
    for at, size in tiles_of(width):
        p2[:, at : at + size] = dot(act[...], mt[1, at : at + size, :], 1, 1).astype(low)
    sum2[0]()
    value = sum2[1]()
    snd1[...] = (h1[...] + value + shift[3:4, :]).astype(low)

    o_ss, o_rs = take(m - 1, m)
    back = exchange("ctx", lambda p, t: ost.at[p], lambda me, t: ob.at[chunks(me), :])
    back_drain = later.pop()

    def cross(snd, other):
        return [
            remote(snd, xx.at[1, own, :], ssem.at[x_ss + d], rsem.at[x_rs + c], {"pipe": other, "ctx": peer})
            for d, peer in enumerate([c] + ctx_peers)
        ]

    def spread(snd):
        return [
            remote(snd, ost.at[w], ssem.at[o_ss + d], rsem.at[o_rs + w], {"wa": peer})
            for d, peer in enumerate(wa_peers)
        ]

    def spread_on():
        for p in wa_peers:
            arrive(ost.at[p], rsem.at[o_rs + p])
        back[0]()
        ob[own, :] = ost[c]

    def spread_start(snd):
        for copy in spread(snd):
            copy.start()
        ost[w] = snd[...]

    @pl.when(side == 0)
    def _():
        for copy in cross(snd1, 1):
            copy.start()
        for p in range(n):
            arrive(xx.at[1, chunks(p), :], rsem.at[x_rs + p])

    pl.when(side == 1)(lambda: spread_start(snd1))

    later.remove(sum1[2])
    sum1[2]()
    for at, size in tiles_of(ff):
        d_pre = dot(xx[c_at], mt[1, :, at : at + size], 1, 0) * slope[:, at : at + size]
        sv[6:7, at : at + size] = jnp.sum(d_pre, axis=0, keepdims=True)
        dpre[:, at : at + size] = d_pre.astype(low)
    sum3 = summing(p1, r3)
    for at, size in tiles_of(width):
        p1[:, at : at + size] = dot(dpre[...], mt[0, at : at + size, :], 1, 1).astype(low)
    sum3[0]()
    for at, size in tiles_of(width):
        gm[1, at : at + size, :] = dot(xx[c_at, :, at : at + size], act[...], 0, 0).astype(low)
        gm[0, at : at + size, :] = dot(fi[:, at : at + size], dpre[...], 0, 0).astype(low)
    pl.when(side == 1)(spread_on)
    value = sum3[1]()

    def column(at, x):
        sv[at : at + 1, :] = jnp.sum(x, axis=0, keepdims=True)

    def norm_back(d_out, normed, inv_std, row):
        lifted = d_out * gain[row : row + 1, :]
        first = jnp.mean(lifted, axis=-1, keepdims=True)
        second = jnp.mean(lifted * normed, axis=-1, keepdims=True)
        return inv_std * (lifted - first - normed * second)

    normed, inv_std = norm(h1[...])
    cot = xx[c_at, own, :].astype(f32)
    column(2, value)
    column(5, value * normed)
    column(3, cot)
    value = cot + norm_back(value, normed, inv_std, 1)
    dh1[...] = value
    column(1, value)
    dh[own, :] = value.astype(low)
    dh_ag = exchange("ctx", lambda p, t: dh.at[own, :], lambda me, t: dh.at[chunks(me), :])
    dh_ag[0]()
    dh_ag[1]()

    dpairs = exchange("wa", lambda p, t: dpair.at[p, t], lambda me, t: rpair.at[me, t], slots)

    def attend_back(s, _):
        d_mixed = dot(dh[...], wt[s, :, two:], 1, 0)
        d_mixed = jnp.where(upper, 0.0, d_mixed).astype(low)
        heads = jnp.zeros((1, two), f32)
        for b in range(micro):
            mine = slice(b * rows, (b + 1) * rows)
            kv = pair[:, s, mine, :].reshape(m * rows, two)
            weight = prob[s * micro + b]
            d_mine = d_mixed[mine, :]
            d_probs = dot(d_mine, kv, 1, 1)
            delta = jnp.sum(weight * d_probs, axis=-1, keepdims=True)
            d_scores = (weight * (d_probs - delta) * scale).astype(low)
            d_query = jnp.where(upper, dot(d_scores, kv, 1, 0), 0.0)
            heads = heads + jnp.sum(d_query, axis=0, keepdims=True)
            dproj[s, mine, two:] = d_query.astype(low)
            d_kv = dot(d_scores, q_s[s, mine, :], 0, 0) + dot(weight.astype(low), d_mine, 0, 0)
            dpair[:, s, mine, :] = d_kv.astype(low).reshape(m, rows, two)
        hv[s] = heads
        dpairs[0](s)
        return 0

    lax.fori_loop(0, slots, attend_back, 0)
    gm_p = exchange("wa", lambda p, t: gm.at[:, :, lanes(p)], lambda me, t: rgm.at[me])
    gh_p = single(
        jnp.logical_not(diagonal), gm.at[:, :, tail], lambda at: rgh.at[at], {"wa": c},
        [(diagonal, p) for p in wa_peers], w,
    )
    gm_p[0]()
    gh_p[0]()

    def collect(s, _):
        value = dpair[w, s].astype(f32)
        dpairs[1](s)
        for p in wa_peers:
            value = value + rpair[p, s].astype(f32)
        dproj[s, :, :two] = value.astype(low)
        hv[s] = hv[s] + jnp.where(upper, 0.0, jnp.sum(value, axis=0, keepdims=True))
        return 0

    lax.fori_loop(0, slots, collect, 0)
    later.remove(sum2[2])
    sum2[2]()
    sum4 = summing(p2, r4)
    for at, size in tiles_of(width):
        value = dot(dproj[0], wt[0, at : at + size, :], 1, 1)
        for s in range(1, slots):
            value = value + dot(dproj[s], wt[s, at : at + size, :], 1, 1)
        p2[:, at : at + size] = value.astype(low)
    sum4[0]()

    at_drain = later.pop(0), later.pop(0)
    at_drain[0]()
    at_drain[1]()

    def attn_grad(s, _):
        for at, size in tiles_of(width):
            stage[at : at + size, :] = dot(a_s[:, at : at + size], dproj[s], 0, 0) + dot(
                dh[:, at : at + size], mix[s], 0, 0
            )
        for j in range(n):
            for p in range(m):
                at = (j * m + p) * part
                w_in[p, j, s] = stage[at : at + padded, :].astype(low)
        return 0

    lax.fori_loop(0, slots, attn_grad, 0)
    value = sum4[1]()
    normed, inv_std = norm(xx[x_at, own, :].astype(f32))
    column(0, value)
    column(4, value * normed)
    snd2[...] = (dh1[...] + norm_back(value, normed, inv_std, 0)).astype(low)

    @pl.when(side == 1)
    def _():
        for copy in cross(snd2, 0):
            copy.start()

    pl.when(side == 0)(lambda: spread_start(snd2))
    for s in range(slots):
        sv[8 + s : 9 + s, :two] = hv[s]
    svc[w] = sv[...]
    sv_p = exchange("wa", lambda p, t: sv, lambda me, t: svc.at[me])
    sv_p[0]()
    ga_p = exchange("wa", lambda p, t: w_in.at[p], lambda me, t: ra.at[me])
    ga_p[0]()

    gm_p[1]()
    gh_p[1]()

    def sum_mlp(i, _):
        for k in range(2):
            at = pl.ds(pl.multiple_of(i * 64, 64), 64)
            value = gm[k, at, lanes(w)].astype(f32)
            for p in wa_peers:
                value = value + rgm[p, k, at, :].astype(f32)
            sm[k, at, :] = value.astype(low)
        return 0

    lax.fori_loop(0, width // 64, sum_mlp, 0)
    gm_z = exchange("ctx", lambda p, t: sm.at[:, crows(p), :], lambda me, t: zg.at[me])
    gm_z[0]()
    zg[c] = sm[:, crows(c), :]
    gh_s, gh_r = take(n - 1, 1)

    def gh_copy(d, peer):
        return remote(smh.at[:, crows(peer), :], zh, ssem.at[gh_s + d], rsem.at[gh_r], {"ctx": peer})

    @pl.when(diagonal)
    def _():
        def sum_half(i, _):
            for k in range(2):
                at = pl.ds(pl.multiple_of(i * 64, 64), 64)
                value = gm[k, at, tail].astype(f32)
                for p in wa_peers:
                    value = value + rgh[p, k, at, :].astype(f32)
                smh[k, at, :] = value.astype(low)
            return 0

        lax.fori_loop(0, width // 64, sum_half, 0)
        for d, peer in enumerate(ctx_peers):
            gh_copy(d, peer).start()
        g_mlp[:, :, tail] = smh[:, crows(c), :].astype(f32)

    pl.when(side == 0)(spread_on)
    sv_p[1]()
    value = svc[0]
    for p in range(1, m):
        value = value + svc[p]
    vec_own[...] = value
    vec_all[c] = value
    sv_z = exchange("ctx", lambda p, t: vec_own, lambda me, t: vec_all.at[me])
    sv_z[0]()

    ga_p[1]()

    def sum_attn(s, _):
        for j in range(n):
            value = w_in[w, j, s].astype(f32)
            for p in wa_peers:
                value = value + ra[p, j, s].astype(f32)
            s2[j, s] = value.astype(low)
        return 0

    lax.fori_loop(0, slots, sum_attn, 0)
    ga_z = exchange("ctx", lambda p, t: s2.at[p], lambda me, t: g_attn.at[me])
    ga_z[0]()
    g_attn[c] = s2[c]

    gm_z[1]()
    for p in range(n):
        g_mlp[:, :, p * share : (p + 1) * share] = zg[p].astype(f32)

    @pl.when(jnp.logical_not(diagonal))
    def _():
        arrive(zh, rsem.at[gh_r])
        g_mlp[:, :, tail] = zh[...].astype(f32)

    back[1]()
    for at, size in tiles_of(total, 64):
        out[at : at + size, :] = ob[at : at + size, :].astype(f32)
    sv_z[1]()
    value = vec_all[0]
    for p in range(1, n):
        value = value + vec_all[p]
    vec_sum[...] = value
    for p in range(n):
        vec_sum[6:7, p * share : (p + 1) * share] = vec_all[p, 6:7, lanes(w)]
    vec_sum[6:7, tail] = vec_all[w, 6:7, tail]
    ga_z[1]()

    for drain in later:
        drain()
    back_drain()

    @pl.when(diagonal)
    def _():
        for d, peer in enumerate(ctx_peers):
            gh_copy(d, peer).wait_send()

    for snd, at in ((snd1, 0), (snd2, 1)):

        @pl.when(side == at)
        def _():
            for copy in cross(snd, 1 - at):
                copy.wait_send()

        @pl.when(side == 1 - at)
        def _():
            for copy in spread(snd):
                copy.wait_send()


def whole_step(
    section_inputs, qkv_weight, out_weight, head_bias, mlp_weight, hidden_bias, feature_bias, ln_gain, block_table
):
    n = lax.axis_size("ctx")
    m = lax.axis_size("wa")
    micro, rows, width = section_inputs.shape[1:]
    heads, part = qkv_weight.shape[1:3]
    head_dim = out_weight.shape[3]
    ff = mlp_weight.shape[3]
    depth = mlp_weight.shape[2]
    slots = (heads + n - 1) // n
    pad = slots * n - heads
    padded = part + (-part % 16)
    total = micro * rows
    chunk = total // n
    share, rest = shares(ff, n, m)
    low = jnp.bfloat16
    f32 = jnp.float32
    two = 2 * head_dim
    scale = head_dim ** (-0.5)

    query, key, value = (qkv_weight[0, :, :, i * head_dim : (i + 1) * head_dim] for i in range(3))
    pack = jnp.concatenate([value, key, out_weight[0], query], axis=-1)
    pack = jnp.pad(pack, ((0, pad), (0, padded - part), (0, 0)))
    pack = pack.reshape(slots, n, padded, 2 * two).transpose(1, 0, 2, 3)
    bias = jnp.concatenate(
        [head_bias[0][:, head_dim:], jnp.zeros((heads, two), f32), head_bias[0][:, :head_dim]], axis=-1
    )
    bias = jnp.pad(bias, ((0, pad), (0, 0))).reshape(slots * n, 1, 2 * two)

    def v(shape, kind=low):
        return pltpu.VMEM(shape, kind)

    wide = (total, width)
    parts = (slots, padded, 2 * two)
    scratch = (
        [v((m, n) + parts), v((width + 16, 2 * two), f32), v((slots, width, 2 * two)), v((2, width, ff))]
        + [v((n, chunk, width)), v((2,) + wide), v((m, 1, ff), f32), v((1, ff), f32), v(wide)]
        + [v((slots, total, two)), v((m, slots, total, two)), v((slots * micro, rows, m * rows), f32)]
        + [v((slots, total, 2 * two))]
        + [v(wide)] * 2
        + [v((n, chunk, width))] * 4
        + [v(wide), v(wide), v((m, chunk, width)), v(wide)]
        + [v((total, ff)), v((total, ff), f32), v((total, ff)), v((chunk, width), f32), v((chunk, width), f32)]
        + [v((m, slots, total, two))] * 2
        + [v((slots, total, 2 * two)), v((2, width, ff)), v((m, 2, width, share)), v((m, 2, width, rest))]
        + [v((2, width, share)), v((2, width, rest)), v((n, 2, depth, share)), v((2, depth, rest))]
        + [v((m, n) + parts), v((n,) + parts)]
        + [v((16, width), f32), v((slots, 1, two), f32), v((m, 16, width), f32)]
        + [v((chunk, width))] * 2
        + [dma(160), dma(200), dma(4), pltpu.SemaphoreType.REGULAR]
    )
    shapes = [
        jax.ShapeDtypeStruct(wide, f32),
        jax.ShapeDtypeStruct((2, depth, ff), f32),
        jax.ShapeDtypeStruct((n,) + parts, low),
        jax.ShapeDtypeStruct((16, width), f32),
        jax.ShapeDtypeStruct((16, width), f32),
        jax.ShapeDtypeStruct((n, 16, width), f32),
    ]
    sizes = (rows, width, ff, slots, micro, head_dim, part, padded)
    out, g_mlp, g_attn, vec_sum, vec_own, vec_all = pl.pallas_call(
        functools.partial(step_kernel, n, m, sizes, scale),
        out_shape=shapes,
        in_specs=[VM] * 7 + [pl.BlockSpec(memory_space=pltpu.SMEM)],
        out_specs=[VM] * len(shapes),
        scratch_shapes=scratch,
        compiler_params=pltpu.CompilerParams(
            collective_id=IDS["step"], has_side_effects=True, vmem_limit_bytes=61 * 1024 * 1024
        ),
        name="step",
    )(
        section_inputs.reshape(total, width),
        pack,
        mlp_weight[0],
        bias,
        hidden_bias,
        feature_bias[0],
        ln_gain[0],
        block_table,
    )
    g_attn = g_attn.transpose(1, 0, 2, 3).reshape(slots * n, padded, 2 * two)[:heads, :part].astype(f32)
    g_value, g_key, g_out, g_query = (g_attn[:, :, i * head_dim : (i + 1) * head_dim] for i in range(4))
    g_heads = vec_all[:, 8 : 8 + slots, :two].transpose(1, 0, 2).reshape(slots * n, two)[:heads]
    g_heads = jnp.concatenate([g_heads[:, head_dim:], g_heads[:, :head_dim]], axis=-1)
    return (
        out.reshape(1, micro, rows, width),
        jnp.concatenate([g_query, g_key, g_value], axis=-1)[None],
        g_out[None],
        g_heads[None],
        g_mlp[None],
        vec_sum[6:7, :ff],
        vec_sum[None, 0:4],
        vec_sum[None, 4:6],
    )


def fits(mesh, rows, micro, width, ff):
    n, m = mesh.shape["ctx"], mesh.shape["wa"]
    depth, chunk = width // n, micro * rows // n
    share, rest = shares(ff, n, m)
    even = depth % 16 == 0 and chunk % 16 == 0 and rows % 16 == 0 and width % 64 == 0
    return n == m and n <= 4 and even and ff <= width and 0 < rest <= 128 and share > 0


def either(mesh, *args):
    micro, rows, width = args[0].shape[1:]
    if fits(mesh, rows, micro, width, args[4].shape[3]):
        return whole_step(*args)
    return per_device(*args)


def solution(mesh):
    return jax.shard_map(
        functools.partial(either, mesh),
        mesh=mesh,
        in_specs=(
            P("pipe", None, "ctx", None),
            P("pipe", None, ("ctx", "wa"), None),
            P("pipe", None, ("ctx", "wa"), None),
            P("pipe", None, None),
            P("pipe", None, "ctx", "wa"),
            P("pipe", "wa"),
            P("pipe", None, None),
            P("pipe", None, None),
            P(),
        ),
        out_specs=(
            P("pipe", None, "ctx", None),
            P("pipe", None, ("ctx", "wa"), None),
            P("pipe", None, ("ctx", "wa"), None),
            P("pipe", None, None),
            P("pipe", None, "ctx", "wa"),
            P("pipe", "wa"),
            P("pipe", None, None),
            P("pipe", None, None),
        ),
        check_vma=False,
    )
```

```python
import functools

import jax
import jax.numpy as jnp
from jax import lax
from jax.experimental import pallas as pl
from jax.experimental.pallas import tpu as pltpu
from jax.sharding import PartitionSpec as P

EPS = 1e-05
GELU_C = 0.7978845608028654
GELU_A = 0.044715
KERNELS = True
MESH = pl.DeviceIdType.MESH
VM = pl.BlockSpec(memory_space=pltpu.VMEM)
IDS = {"sum_wa": 1, "swap_wa": 2, "swap_ctx": 3, "line_attn": 4, "line_mlp": 5, "line_pair": 6, "swap_mlp": 7,
       "swap_attn": 8, "all_small": 9, "all_heads": 10, "swap_grad": 11, "step": 12}


def remote(src, dst, send, recv, peer):
    return pltpu.make_async_remote_copy(
        src_ref=src, dst_ref=dst, send_sem=send, recv_sem=recv, device_id=peer, device_id_type=MESH
    )


def greet(peers):
    barrier = pltpu.get_barrier_semaphore()
    for peer in peers:
        pl.semaphore_signal(barrier, inc=1, device_id=peer, device_id_type=MESH)
    pl.semaphore_wait(barrier, len(peers))


def sum_kernel(axis, n, x_ref, o_ref, got, send_a, recv_a, send_b, recv_b):
    me = lax.axis_index(axis)
    peers = [{axis: lax.rem(me + d, n)} for d in range(1, n)]
    greet(peers)
    first = [
        remote(x_ref.at[lax.rem(me + d, n)], got.at[d - 1], send_a.at[d - 1], recv_a.at[d - 1], peers[d - 1])
        for d in range(1, n)
    ]
    for copy in first:
        copy.start()
    total = x_ref[me].astype(jnp.float32)
    for d, copy in enumerate(first):
        copy.wait_recv()
        total = total + got[d].astype(jnp.float32)
    o_ref[me] = total.astype(o_ref.dtype)
    second = [
        remote(o_ref.at[me], o_ref.at[me], send_b.at[d - 1], recv_b.at[d - 1], peers[d - 1]) for d in range(1, n)
    ]
    for copy in second:
        copy.start()
    for copy in first:
        copy.wait_send()
    for copy in second:
        copy.wait()


def swap_kernel(axis, n, x_ref, o_ref, send, recv, local):
    me = lax.axis_index(axis)
    peers = [{axis: lax.rem(me + d, n)} for d in range(1, n)]
    greet(peers)
    copies = [
        remote(x_ref.at[lax.rem(me + d, n)], o_ref.at[me], send.at[d - 1], recv.at[d - 1], peers[d - 1])
        for d in range(1, n)
    ]
    for copy in copies:
        copy.start()
    own = pltpu.make_async_copy(x_ref.at[me], o_ref.at[me], local)
    own.start()
    own.wait()
    for copy in copies:
        copy.wait()


def all_kernel(axis, n, x_ref, o_ref, send, recv, local):
    me = lax.axis_index(axis)
    peers = [{axis: lax.rem(me + d, n)} for d in range(1, n)]
    greet(peers)
    copies = [
        remote(x_ref, o_ref.at[me], send.at[d - 1], recv.at[d - 1], peers[d - 1]) for d in range(1, n)
    ]
    for copy in copies:
        copy.start()
    own = pltpu.make_async_copy(x_ref, o_ref.at[me], local)
    own.start()
    own.wait()
    for copy in copies:
        copy.wait()


def line_kernel(n, both, x_ref, o_ref, send_r, recv_r, send_l, recv_l, send_p, recv_p, local):
    me = lax.axis_index("ctx")
    side = lax.axis_index("pipe")
    row = side if both else 0
    right, left, mate = {"ctx": me + 1}, {"ctx": me - 1}, {"pipe": 1 - side}
    barrier = pltpu.get_barrier_semaphore()
    not_last, not_first = me + 1 < n, me > 0

    @pl.when(not_last)
    def _():
        pl.semaphore_signal(barrier, inc=1, device_id=right, device_id_type=MESH)

    @pl.when(not_first)
    def _():
        pl.semaphore_signal(barrier, inc=1, device_id=left, device_id_type=MESH)

    if both:
        pl.semaphore_signal(barrier, inc=1, device_id=mate, device_id_type=MESH)
    extra = 1 if both else 0

    @pl.when(not_first & not_last)
    def _():
        pl.semaphore_wait(barrier, 2 + extra)

    @pl.when(jnp.logical_not(not_first & not_last))
    def _():
        pl.semaphore_wait(barrier, 1 + extra)

    own = pltpu.make_async_copy(x_ref, o_ref.at[row, me], local)
    own.start()

    def block(at, fresh):
        return x_ref if fresh else o_ref.at[row, at]

    def to_right(s):
        return remote(block(me - s, s == 0), o_ref.at[row, me - s], send_r.at[s], recv_r.at[s], right)

    def to_left(s):
        return remote(block(me + s, s == 0), o_ref.at[row, me + s], send_l.at[s], recv_l.at[s], left)

    def to_mate(at, fresh):
        return remote(block(at, fresh), o_ref.at[row, at], send_p.at[at], recv_p.at[at], mate)

    def arrived(at, sem):
        return remote(o_ref.at[row, at], o_ref.at[row, at], send_r.at[0], sem, mate)

    for s in range(n):

        @pl.when(me - s >= 0)
        def _():
            if s > 0:
                arrived(me - s, recv_r.at[s - 1]).wait_recv()
            if s < n - 1:

                @pl.when(not_last)
                def _():
                    to_right(s).start()

            if both and s > 0:
                to_mate(me - s, False).start()

        @pl.when(me + s < n)
        def _():
            if s > 0:
                arrived(me + s, recv_l.at[s - 1]).wait_recv()
            if s < n - 1:

                @pl.when(not_first)
                def _():
                    to_left(s).start()

            if both:
                to_mate(me + s, s == 0).start()

    own.wait()
    for s in range(n - 1):

        @pl.when((me - s >= 0) & not_last)
        def _():
            to_right(s).wait_send()

        @pl.when((me + s < n) & not_first)
        def _():
            to_left(s).wait_send()

    if both:
        for at in range(n):
            to_mate(at, False).wait_send()
            remote(o_ref.at[1 - side, at], o_ref.at[1 - side, at], send_p.at[at], recv_p.at[at], mate).wait_recv()


def call(kernel, name, shape, scratch, x):
    return pl.pallas_call(
        kernel,
        out_shape=jax.ShapeDtypeStruct(shape, x.dtype),
        in_specs=[VM],
        out_specs=VM,
        scratch_shapes=scratch,
        compiler_params=pltpu.CompilerParams(
            collective_id=IDS[name], has_side_effects=True, vmem_limit_bytes=60 * 1024 * 1024
        ),
        name=name,
    )(x)


def dma(count):
    return pltpu.SemaphoreType.DMA((count,))


def summed(x):
    n = lax.axis_size("wa")
    low = x.astype(jnp.bfloat16)
    if not KERNELS:
        return lax.psum(low.astype(jnp.float32), "wa").astype(jnp.bfloat16).astype(jnp.float32)
    parts = low.reshape(n, low.shape[0] // n, low.shape[1])
    scratch = [pltpu.VMEM((n - 1,) + parts.shape[1:], jnp.bfloat16)] + [dma(n - 1)] * 4
    out = call(functools.partial(sum_kernel, "wa", n), "sum_wa", parts.shape, scratch, parts)
    return out.reshape(low.shape).astype(jnp.float32)


def swapped(x, axis, name):
    n = lax.axis_size(axis)
    if not KERNELS:
        return lax.all_to_all(x, axis, split_axis=0, concat_axis=0, tiled=True)
    scratch = [dma(n - 1)] * 2 + [pltpu.SemaphoreType.DMA]
    return call(functools.partial(swap_kernel, axis, n), name, x.shape, scratch, x)


def gathered(x, axis, name):
    n = lax.axis_size(axis)
    if not KERNELS:
        return lax.all_gather(x, axis)
    scratch = [dma(n - 1)] * 2 + [pltpu.SemaphoreType.DMA]
    return call(functools.partial(all_kernel, axis, n), name, (n,) + x.shape, scratch, x)


def lined(x, both, name):
    n = lax.axis_size("ctx")
    if not KERNELS:
        out = lax.all_gather(x, "ctx")
        return lax.all_gather(out, "pipe") if both else out[None]
    scratch = [dma(n - 1)] * 4 + [dma(n)] * 2 + [pltpu.SemaphoreType.DMA]
    return call(functools.partial(line_kernel, n, both), name, (2 if both else 1, n) + x.shape, scratch, x)


def dot(a, b, ca, cb):
    return lax.dot_general(a, b, (((ca,), (cb,)), ((), ())), preferred_element_type=jnp.float32)


def attend_kernel(scale, qpos, kpos, q_ref, kv_ref, mix_ref, total_ref):
    heads = q_ref.shape[0]
    allowed = kpos[...] <= qpos[...]
    for h in range(heads):
        kv = kv_ref[:, h].reshape(-1, kv_ref.shape[-1])
        scores = jnp.where(allowed, dot(q_ref[h], kv, 1, 1) * scale, -jnp.inf)
        top = jnp.max(scores, axis=-1, keepdims=True)
        total = top + jnp.log(jnp.sum(jnp.exp(scores - top), axis=-1, keepdims=True))
        probs = jnp.exp(scores - total).astype(jnp.bfloat16)
        mix_ref[h] = dot(probs, kv, 1, 0).astype(jnp.bfloat16)
        total_ref[h] = total


def attend_back_kernel(scale, qpos, kpos, q_ref, kv_ref, dm_ref, total_ref, dq_ref, dkv_ref):
    heads = q_ref.shape[0]
    allowed = kpos[...] <= qpos[...]
    for h in range(heads):
        kv = kv_ref[:, h].reshape(-1, kv_ref.shape[-1])
        scores = jnp.where(allowed, dot(q_ref[h], kv, 1, 1) * scale, -jnp.inf)
        probs = jnp.exp(scores - total_ref[h])
        d_probs = dot(dm_ref[h], kv, 1, 1)
        delta = jnp.sum(probs * d_probs, axis=-1, keepdims=True)
        d_scores = (probs * (d_probs - delta) * scale).astype(jnp.bfloat16)
        dq_ref[h] = dot(d_scores, kv, 1, 0)
        d_kv = dot(d_scores, q_ref[h], 0, 0) + dot(probs.astype(jnp.bfloat16), dm_ref[h], 0, 0)
        dkv_ref[:, h] = d_kv.astype(jnp.bfloat16).reshape(dkv_ref.shape[0], dkv_ref.shape[2], dkv_ref.shape[3])


def local_call(kernel, shapes, *args):
    return pl.pallas_call(
        kernel,
        out_shape=[jax.ShapeDtypeStruct(*s) for s in shapes],
        in_specs=[VM] * len(args),
        out_specs=[VM] * len(shapes),
        compiler_params=pltpu.CompilerParams(vmem_limit_bytes=48 * 1024 * 1024),
        interpret=not KERNELS,
    )(*args)

def norm_forward(stream, gain, offset):
    centre = jnp.mean(stream, axis=-1, keepdims=True)
    centred = stream - centre
    variance = jnp.mean(centred * centred, axis=-1, keepdims=True)
    inv_std = lax.rsqrt(variance + EPS)
    normed = centred * inv_std
    return (normed * gain + offset, normed, inv_std)


def norm_backward(grad_out, normed, inv_std, gain):
    grad_normed = grad_out * gain
    first_mean = jnp.mean(grad_normed, axis=-1, keepdims=True)
    second_mean = jnp.mean(grad_normed * normed, axis=-1, keepdims=True)
    return inv_std * (grad_normed - first_mean - normed * second_mean)


def gelu_value(hidden):
    tangent = jnp.tanh(GELU_C * (hidden + GELU_A * hidden * hidden * hidden))
    return 0.5 * hidden * (1.0 + tangent)


def gelu_slope(hidden):
    tangent = jnp.tanh(GELU_C * (hidden + GELU_A * hidden * hidden * hidden))
    return 0.5 * (1.0 + tangent) + 0.5 * hidden * (1.0 - tangent * tangent) * GELU_C * (
        1.0 + 3.0 * GELU_A * hidden * hidden
    )


def per_device(
    section_inputs,
    qkv_weight,
    out_weight,
    head_bias,
    mlp_weight,
    hidden_bias,
    feature_bias,
    ln_gain,
    block_table,
):
    ctx_count = lax.axis_size("ctx")
    shard_count = lax.axis_size("wa")
    side = lax.axis_index("pipe")
    ctx_index = lax.axis_index("ctx")
    shard_index = lax.axis_index("wa")
    rows = section_inputs.shape[2]
    width = section_inputs.shape[3]
    head_count = qkv_weight.shape[1]
    head_dim = out_weight.shape[3]
    part = qkv_weight.shape[2]
    slots = (head_count + shard_count - 1) // shard_count
    pad = slots * shard_count - head_count
    block_rows = rows // 2
    scale = head_dim ** (-0.5)
    swap = [(0, 1), (1, 0)]
    low = jnp.bfloat16

    own_blocks = lax.dynamic_index_in_dim(block_table, ctx_index, 0, keepdims=False)
    step = jnp.arange(block_rows, dtype=jnp.int32)
    query_pos = (own_blocks[:, None] * block_rows + step[None, :]).reshape(rows, 1)
    key_pos = (block_table.reshape(-1)[:, None] * block_rows + step[None, :]).reshape(1, rows * ctx_count)

    def mine(first, second):
        return jnp.where(side == 0, first, second)

    inputs = section_inputs[0]
    traded = lax.ppermute(mine(inputs[1], inputs[0]), "pipe", swap)
    layer_input = mine(inputs[0], traded)
    last_cot = mine(traded, inputs[1])

    packed = jnp.concatenate([qkv_weight[0], out_weight[0]], axis=-1)
    packed = jnp.pad(packed, ((0, pad), (0, 0), (0, 0)))
    packed = packed.reshape(slots, shard_count, part, 4 * head_dim).transpose(1, 0, 2, 3)
    attn_all = lined(swapped(packed, "wa", "swap_wa"), True, "line_attn")
    mlp_all = lined(mlp_weight[0], True, "line_mlp")

    sizes = [head_bias[0].size, hidden_bias[0].size, feature_bias[0].size]
    small = jnp.concatenate(
        [head_bias[0].reshape(-1), hidden_bias[0], feature_bias[0].reshape(-1), ln_gain[0].reshape(-1)]
    )
    small_mate = lax.ppermute(small, "pipe", swap)

    def params_of(layer):
        weight = attn_all[layer].transpose(2, 0, 1, 3, 4).reshape(slots, width, 4 * head_dim)
        up = mlp_all[layer][:, 0].reshape(width, -1)
        down = mlp_all[layer][:, 1].reshape(width, -1)
        flat = jnp.where(side == layer, small, small_mate)
        heads, hidden, feature, gains = jnp.split(flat, [sizes[0], sizes[0] + sizes[1], sum(sizes)])
        heads = jnp.pad(heads.reshape(head_count, 2 * head_dim), ((0, pad), (0, 0)))
        heads = heads.reshape(slots, shard_count, 2 * head_dim)
        heads = lax.dynamic_index_in_dim(heads, shard_index, 1, keepdims=False)
        return (
            weight[:, :, : 3 * head_dim],
            weight[:, :, 3 * head_dim :],
            heads,
            up,
            down,
            hidden,
            feature.reshape(4, width),
            gains.reshape(2, width),
        )

    def widened(x, before):
        zero = jnp.zeros_like(x)
        return jnp.concatenate([zero, x] if before else [x, zero], axis=-1)

    def forward(layer_in, params):
        w_qkv, w_out, bias, w_up, w_down, bias_hidden, shifts, gains = params
        stream = layer_in.astype(jnp.float32)
        normed_in, normed_one, inv_one = norm_forward(stream, gains[0], shifts[0])
        attn_in = normed_in.astype(low)
        projected = jnp.einsum("td,hde->hte", attn_in, w_qkv, preferred_element_type=jnp.float32)
        queries = widened((projected[:, :, :head_dim] + bias[:, None, :head_dim]).astype(low), False)
        key_rows = projected[:, :, head_dim : 2 * head_dim].astype(low)
        values = (projected[:, :, 2 * head_dim :] + bias[:, None, head_dim:]).astype(low)
        pairs = lined(jnp.concatenate([key_rows, values], axis=-1), False, "line_pair")[0]
        mixed, log_total = local_call(
            functools.partial(attend_kernel, scale),
            [((slots, rows, 2 * head_dim), low), ((slots, rows, 1), jnp.float32)],
            query_pos,
            key_pos,
            queries,
            pairs,
        )
        mixed = mixed[:, :, head_dim:]
        attn_out = summed(jnp.einsum("hte,hde->td", mixed, w_out, preferred_element_type=jnp.float32))
        first_sum = stream + attn_out + shifts[1]
        normed_ffn, normed_two, inv_two = norm_forward(first_sum, gains[1], shifts[2])
        ffn_in = normed_ffn.astype(low)
        pre = jnp.dot(ffn_in, w_up, preferred_element_type=jnp.float32) + bias_hidden
        act = gelu_value(pre).astype(low)
        layer_out = (
            first_sum
            + summed(jnp.einsum("tf,df->td", act, w_down, preferred_element_type=jnp.float32))
            + shifts[3]
        )
        return layer_out, (
            normed_one, inv_one, attn_in, queries, pairs, mixed, log_total, normed_two, inv_two, ffn_in, pre, act,
        )

    def backward(cot, saved, params):
        w_qkv, w_out, bias, w_up, w_down, bias_hidden, shifts, gains = params
        normed_one, inv_one, attn_in, queries, pairs, mixed, log_total, normed_two, inv_two, ffn_in, pre, act = saved
        cotangent = cot.astype(jnp.float32)
        grad_down = jnp.einsum("ti,tf->if", cot, act, preferred_element_type=jnp.float32)
        d_act = jnp.einsum("ti,if->tf", cot, w_down, preferred_element_type=jnp.float32)
        d_pre = d_act * gelu_slope(pre)
        grad_hidden = jnp.sum(d_pre, axis=0)
        d_pre_low = d_pre.astype(low)
        grad_up = jnp.einsum("td,tf->df", ffn_in, d_pre_low, preferred_element_type=jnp.float32)
        d_ffn = summed(jnp.einsum("tf,df->td", d_pre_low, w_up, preferred_element_type=jnp.float32))
        d_first = cotangent + norm_backward(d_ffn, normed_two, inv_two, gains[1])
        d_first_low = d_first.astype(low)
        grad_out = jnp.einsum("ti,hte->hie", d_first_low, mixed, preferred_element_type=jnp.float32)
        d_mixed = jnp.einsum("ti,hie->hte", d_first_low, w_out, preferred_element_type=jnp.float32)
        d_query, pair_terms = local_call(
            functools.partial(attend_back_kernel, scale),
            [((slots, rows, 2 * head_dim), jnp.float32), (pairs.shape, low)],
            query_pos,
            key_pos,
            queries,
            pairs,
            widened(d_mixed.astype(low), True),
            log_total,
        )
        d_query = d_query[:, :, :head_dim]
        d_pair = swapped(pair_terms, "ctx", "swap_ctx").astype(jnp.float32).sum(axis=0)
        grad_heads = jnp.concatenate(
            [jnp.sum(d_query, axis=1), jnp.sum(d_pair[:, :, head_dim:], axis=1)], axis=-1
        )
        d_proj = jnp.concatenate([d_query.astype(low), d_pair.astype(low)], axis=-1)
        grad_qkv = jnp.einsum("td,hte->hde", attn_in, d_proj, preferred_element_type=jnp.float32)
        d_attn = summed(jnp.einsum("hte,hde->td", d_proj, w_qkv, preferred_element_type=jnp.float32))
        d_input = d_first + norm_backward(d_attn, normed_one, inv_one, gains[0])
        vectors = [
            jnp.sum(d_attn, axis=0),
            jnp.sum(d_first, axis=0),
            jnp.sum(d_ffn, axis=0),
            jnp.sum(cotangent, axis=0),
            jnp.sum(d_attn * normed_one, axis=0),
            jnp.sum(d_ffn * normed_two, axis=0),
            grad_hidden,
            grad_heads.reshape(-1),
        ]
        attn_grad = jnp.concatenate([grad_qkv, grad_out], axis=-1).astype(low)
        mlp_grad = jnp.stack([grad_up, grad_down]).astype(low)
        return d_input, attn_grad, mlp_grad, jnp.concatenate(vectors)

    params = [params_of(0), params_of(1)]
    first_out, first_saved = forward(layer_input, params[0])
    last_out, last_saved = forward(first_out.astype(low), params[1])
    back, attn_one, mlp_one, vec_one = backward(last_cot, last_saved, params[1])
    d_input, attn_zero, mlp_zero, vec_zero = backward(back.astype(low), first_saved, params[0])

    def over_pipe(zero, one):
        kept = mine(zero, one)
        got = lax.ppermute(mine(one, zero), "pipe", swap)
        return kept.astype(jnp.float32) + got.astype(jnp.float32)

    mlp_sum = over_pipe(mlp_zero, mlp_one).astype(low)
    mlp_sum = mlp_sum.reshape(2, ctx_count, width // ctx_count, -1).transpose(1, 0, 2, 3)
    mlp_out = swapped(mlp_sum, "ctx", "swap_mlp").astype(jnp.float32).sum(axis=0)

    attn_sum = over_pipe(attn_zero, attn_one).astype(low)
    attn_sum = attn_sum.reshape(slots, ctx_count, shard_count, part, 4 * head_dim).transpose(1, 2, 0, 3, 4)
    attn_part = swapped(attn_sum, "ctx", "swap_attn").astype(jnp.float32).sum(axis=0).astype(low)
    attn_out = swapped(attn_part, "wa", "swap_grad")
    attn_out = attn_out.transpose(1, 0, 2, 3).reshape(slots * shard_count, part, 4 * head_dim)
    attn_out = attn_out[:head_count].astype(jnp.float32)

    vec = over_pipe(vec_zero, vec_one)
    length = vec.shape[0]
    fill = -length % 128
    vec = jnp.pad(vec, (0, fill)).reshape(-1, 128)
    vec = gathered(vec, "ctx", "all_small").sum(axis=0).reshape(-1)[:length]
    feature_sum, gain_sum, hidden_own, head_own = jnp.split(
        vec, [4 * width, 6 * width, 6 * width + hidden_bias.shape[1]]
    )
    head_sum = gathered(head_own.reshape(slots, 2 * head_dim), "wa", "all_heads")
    head_sum = head_sum.transpose(1, 0, 2).reshape(slots * shard_count, 2 * head_dim)[:head_count]

    last_traded = lax.ppermute(mine(last_out, d_input), "pipe", swap)
    section_outputs = jnp.where(
        side == 0, jnp.stack([d_input, last_traded]), jnp.stack([last_traded, last_out])
    )
    return (
        section_outputs[None],
        attn_out[None, :, :, : 3 * head_dim],
        attn_out[None, :, :, 3 * head_dim :],
        head_sum[None],
        mlp_out[None],
        hidden_own[None],
        feature_sum.reshape(1, 4, width),
        gain_sum.reshape(1, 2, width),
    )


def tiles_of(total, size=256):
    return [(at, min(size, total - at)) for at in range(0, total, size)]


def shares(ff, n, m):
    share = ff // 128 // n * 128
    return share, ff - n * share


def step_kernel(n, m, sizes, scale, *refs):
    rows, width, ff, slots, micro, head_dim, part, padded = sizes
    (
        inp, pack, mlp, bias, hidden, shift, gain, table,
        out, g_qkv, g_out, g_heads, g_mlp, g_hidden, g_feature, g_gain,
        w_in, stage, wt, mt, xin, xx, hid_all, hid, a_s, q_s, pair, prob, mix,
        p1, p2, r1, r2, r3, r4, fi, dh, ost, ob, act, slope, dpre, h1, dh1,
        dpair, rpair, dproj, gm, rgm, rgh, sm, smh, zg, zh, ra, s2, za, sv, hv, svc, vec_own, vec_all, snd1, snd2,
        ssem, rsem, loc, go,
    ) = refs
    side = lax.axis_index("pipe")
    c = lax.axis_index("ctx")
    w = lax.axis_index("wa")
    total = micro * rows
    chunk = total // n
    sub = rows // n
    heads = g_heads.shape[0]
    depth = width // n
    share, rest = shares(ff, n, m)
    tail = slice(n * share, ff)
    two = 2 * head_dim
    low = jnp.bfloat16
    f32 = jnp.float32
    mate = {"pipe": 1 - side}
    later = []
    used = [0, 0]

    def take(sends, recvs):
        at = tuple(used)
        used[0] += sends
        used[1] += recvs
        return at

    ctx_peers = [lax.rem(c + d, n) for d in range(1, n)]
    wa_peers = [lax.rem(w + d, m) for d in range(1, m)]

    greet(
        [{"ctx": peer} for peer in ctx_peers]
        + [{"wa": peer} for peer in wa_peers]
        + [{"pipe": 1 - side, "ctx": peer} for peer in [c] + ctx_peers]
    )

    def arrive(ref, sem):
        remote(ref, ref, sem, sem, mate).wait_recv()

    def exchange(axis, src, dst, times=1):
        me, count, peers = (c, n, ctx_peers) if axis == "ctx" else (w, m, wa_peers)
        s0, r0 = take(times * (count - 1), times * count)

        def copy(d, peer, t):
            return remote(
                src(peer, t), dst(me, t), ssem.at[s0 + t * (count - 1) + d], rsem.at[r0 + t * count + me], {axis: peer}
            )

        def start(t=0):
            for d, peer in enumerate(peers):
                copy(d, peer, t).start()

        def got(t=0):
            for peer in peers:
                arrive(dst(peer, t), rsem.at[r0 + t * count + peer])

        def drain():
            def one(t, _):
                for d, peer in enumerate(peers):
                    copy(d, peer, t).wait_send()
                return 0

            if times == 1:
                one(0, 0)
            else:
                lax.fori_loop(0, times, one, 0)

        later.append(drain)
        return start, got

    def single(cond_send, src, dst, peer, cond_recvs, slot):
        s0, r0 = take(1, max(n, m))

        def copy():
            return remote(src, dst(slot), ssem.at[s0], rsem.at[r0 + slot], peer)

        def start():
            pl.when(cond_send)(lambda: copy().start())

        def got():
            for cond, p in cond_recvs:
                pl.when(cond)(functools.partial(arrive, dst(p), rsem.at[r0 + p]))

        later.append(lambda: pl.when(cond_send)(lambda: copy().wait_send()))
        return start, got

    def crows(at):
        return pl.ds(pl.multiple_of(at * depth, 16), depth)

    def chunks(at):
        return pl.ds(pl.multiple_of(at * chunk, 16), chunk)

    def lanes(at):
        return pl.ds(pl.multiple_of(at * share, 128), share)

    def piece(b, at):
        return pl.ds(pl.multiple_of(b * rows + at * sub, 16), sub)

    def batch(b):
        return slice(b * rows, (b + 1) * rows)

    diagonal = c == w

    at_z = exchange("ctx", lambda p, t: pack.at[p, t], lambda me, t: w_in.at[w, t, me], slots)
    at_p = exchange("wa", lambda p, t: w_in.at[w, t], lambda me, t: w_in.at[me, t], slots)
    x_z = exchange("ctx", lambda p, t: inp.at[chunks(w), :], lambda me, t: xin.at[me])
    x_p = exchange("wa", lambda p, t: xin.at[p], lambda me, t: xx.at[0, chunks(me), :])
    hid_p = exchange("wa", lambda p, t: hidden, lambda me, t: hid_all.at[me])
    ml_z = exchange("ctx", lambda p, t: mlp.at[:, :, lanes(p)], lambda me, t: mt.at[:, crows(me), lanes(w)])
    ml_p = exchange("wa", lambda p, t: mt.at[t, :, lanes(w)], lambda me, t: mt.at[t, :, lanes(me)], 2)
    mh_z = single(
        jnp.logical_not(diagonal), mlp.at[:, :, tail], lambda at: mt.at[:, crows(at), tail], {"ctx": w},
        [(diagonal, p) for p in ctx_peers], c,
    )
    mh_s, mh_r = take(m - 1, 1)

    def mh_copy(d, peer):
        return remote(mt.at[:, :, tail], mt.at[:, :, tail], ssem.at[mh_s + d], rsem.at[mh_r], {"wa": peer})

    own_pack = pltpu.make_async_copy(pack.at[c], w_in.at[w, :, c], loc.at[0])
    own_mlp = pltpu.make_async_copy(mlp.at[:, :, lanes(c)], mt.at[:, crows(c), lanes(w)], loc.at[1])
    own_x = pltpu.make_async_copy(inp.at[chunks(w), :], xin.at[c], loc.at[2])
    own_half = pltpu.make_async_copy(mlp.at[:, :, tail], mt.at[:, crows(c), tail], loc.at[3])

    own_pack.start()
    own_mlp.start()
    own_x.start()
    pl.when(diagonal)(lambda: own_half.start())

    pl.when(side == 1)(lambda: pl.semaphore_wait(go, 1))
    def start_attn(t, _):
        at_z[0](t)
        return 0

    lax.fori_loop(0, slots, start_attn, 0)
    x_z[0]()
    hid_p[0]()
    ml_z[0]()
    mh_z[0]()
    stage[...] = jnp.zeros_like(stage)
    mix[...] = jnp.zeros_like(mix)
    sv[...] = jnp.zeros_like(sv)
    hv[...] = jnp.zeros_like(hv)
    own_pack.wait()

    def pass_attn(t, _):
        at_z[1](t)
        at_p[0](t)
        return 0

    lax.fori_loop(0, slots, pass_attn, 0)
    own_x.wait()
    x_z[1]()
    x_p[0]()
    xx[0, chunks(w), :] = xin[w]
    hid_p[1]()
    hid_all[w] = hidden[...]
    for p in range(m):
        hid[:, p * share : (p + 1) * share] = hid_all[p, :, lanes(c)]
    hid[:, tail] = hid_all[c, :, tail]
    x_p[1]()
    x_ss, x_rs = take(micro * n, micro * n)
    x_at = side
    c_at = 1 - side

    def norm(stream):
        centre = jnp.mean(stream, axis=-1, keepdims=True)
        centred = stream - centre
        variance = jnp.mean(centred * centred, axis=-1, keepdims=True)
        inv_std = lax.rsqrt(variance + EPS)
        return centred * inv_std, inv_std

    def first_norm(b):
        for at, size in tiles_of(rows, 64):
            here = slice(b * rows + at, b * rows + at + size)
            normed, _ = norm(xx[x_at, here, :].astype(f32))
            a_s[here, :] = (normed * gain[0:1, :] + shift[0:1, :]).astype(low)

    upper = lax.broadcasted_iota(jnp.int32, (1, two), 1) >= head_dim
    pairs = exchange(
        "wa",
        lambda p, t: pair.at[w, lax.rem(t, slots), pl.ds(pl.multiple_of(t // slots * rows, 16), rows), :],
        lambda me, t: pair.at[me, lax.rem(t, slots), pl.ds(pl.multiple_of(t // slots * rows, 16), rows), :],
        slots * micro,
    )

    def lay(s):
        at_p[1](s)
        for j in range(n):
            for p in range(m):
                at = (j * m + p) * part
                stage[at : at + part, :] = w_in[p, s, j].astype(f32)[:part]
        wt[s] = stage[:width, :].astype(low)

    def project(s, b):
        made = dot(a_s[batch(b), :], wt[s], 1, 0)
        row = pltpu.roll(bias[jnp.minimum(s * n + c, heads - 1)], two // 2, 1)
        pair[w, s, batch(b), :] = (made[:, :two] + jnp.where(upper, 0.0, row)).astype(low)
        q_s[s, batch(b), :] = jnp.where(upper, made[:, two:] + row, 0.0).astype(low)
        pairs[0](b * slots + s)

    @pl.when(side == 0)
    def _():
        for b in range(micro):
            first_norm(b)

        def both(s, _):
            lay(s)
            for b in range(micro):
                project(s, b)
            return 0

        lax.fori_loop(0, slots, both, 0)

    @pl.when(side == 1)
    def _():
        def alone(s, _):
            lay(s)
            return 0

        lax.fori_loop(0, slots, alone, 0)

    own_mlp.wait()
    ml_z[1]()
    ml_p[0](0)
    ml_p[0](1)

    @pl.when(diagonal)
    def _():
        own_half.wait()

    mh_z[1]()

    @pl.when(diagonal)
    def _():
        for d, peer in enumerate(wa_peers):
            mh_copy(d, peer).start()

    def mh_drain():
        for d, peer in enumerate(wa_peers):
            mh_copy(d, peer).wait_send()

    later.append(lambda: pl.when(diagonal)(mh_drain))

    @pl.when(side == 0)
    def _():
        pl.semaphore_signal(go, inc=1, device_id=mate, device_id_type=MESH)

    @pl.when(side == 1)
    def _():
        for b in range(micro):
            for p in range(n):
                arrive(xx.at[1, piece(b, p), :], rsem.at[x_rs + b * n + p])
            first_norm(b)

            def one(s, _):
                project(s, b)
                return 0

            lax.fori_loop(0, slots, one, 0)

    block = rows // 2
    step = lax.broadcasted_iota(jnp.int32, (rows, 1), 0)
    qpos = jnp.where(step < block, table[0, w] * block + step, table[1, w] * block + step - block)
    along = lax.broadcasted_iota(jnp.int32, (1, m * rows), 1)
    kpos = along
    for i in range(2 * m):
        inside = (along >= i * block) & (along < (i + 1) * block)
        kpos = jnp.where(inside, table[i % 2, i // 2] * block + along - i * block, kpos)

    def attend(s, b):
        pairs[1](b * slots + s)
        kv = pair[:, s, batch(b), :].reshape(m * rows, two)
        scores = jnp.where(kpos <= qpos, dot(q_s[s, batch(b), :], kv, 1, 1) * scale, -jnp.inf)
        top = jnp.max(scores, axis=-1, keepdims=True)
        raised = jnp.exp(scores - top)
        weight = raised / jnp.sum(raised, axis=-1, keepdims=True)
        prob[s * micro + b] = weight
        mixed = dot(weight.astype(low), kv, 1, 0)
        mix[s, batch(b), two:] = jnp.where(upper, 0.0, mixed).astype(low)

    def summing(part_s, got_s):
        start, got = exchange(
            "ctx", lambda p, t: part_s.at[piece(t, p), :], lambda me, t: got_s.at[me, t], micro
        )

        def finish(b):
            value = part_s[piece(b, c), :].astype(f32)
            got(b)
            for p in ctx_peers:
                value = value + got_s[p, b].astype(f32)
            return value

        return start, finish, later[-1]

    def sharing(ref):
        return exchange("ctx", lambda p, t: ref.at[piece(t, c), :], lambda me, t: ref.at[piece(t, me), :], micro)

    sum1 = summing(p1, r1)
    for b in range(micro):

        def attend_all(s, _):
            attend(s, b)
            return 0

        lax.fori_loop(0, slots, attend_all, 0)
        for at, size in tiles_of(width):
            value = dot(mix[0, batch(b), two:], wt[0, at : at + size, two:], 1, 1)
            for s in range(1, slots):
                value = value + dot(mix[s, batch(b), two:], wt[s, at : at + size, two:], 1, 1)
            p1[batch(b), at : at + size] = value.astype(low)
        sum1[0](b)
    fi_ag = sharing(fi)
    for b in range(micro):
        value = sum1[1](b)
        value = xx[x_at, piece(b, c), :].astype(f32) + value + shift[1:2, :]
        h1[b] = value
        normed, _ = norm(value)
        fi[piece(b, c), :] = (normed * gain[1:2, :] + shift[2:3, :]).astype(low)
        fi_ag[0](b)

    sum2 = summing(p2, r2)
    for b in range(micro):
        if b == 0:
            ml_p[1](0)
            pl.when(jnp.logical_not(diagonal))(lambda: arrive(mt.at[:, :, tail], rsem.at[mh_r]))
        fi_ag[1](b)
        for at, size in tiles_of(ff):
            pre = dot(fi[batch(b), :], mt[0, :, at : at + size], 1, 0) + hid[:, at : at + size]
            square = pre * pre
            tangent = jnp.tanh(GELU_C * (pre + GELU_A * square * pre))
            act[batch(b), at : at + size] = (0.5 * pre * (1.0 + tangent)).astype(low)
            slope[batch(b), at : at + size] = 0.5 * (1.0 + tangent) + 0.5 * pre * (
                1.0 - tangent * tangent
            ) * GELU_C * (1.0 + 3.0 * GELU_A * square)
        if b == 0:
            ml_p[1](1)
        for at, size in tiles_of(width):
            p2[batch(b), at : at + size] = dot(act[batch(b), :], mt[1, at : at + size, :], 1, 1).astype(low)
        sum2[0](b)

    o_ss, o_rs = take(micro * (m - 1), micro * m)
    back = exchange("ctx", lambda p, t: ost.at[p], lambda me, t: ob.at[:, me])
    back_drain = later.pop()

    def cross(snd, other, b):
        return [
            remote(
                snd.at[b], xx.at[1, piece(b, c), :], ssem.at[x_ss + b * n + d], rsem.at[x_rs + b * n + c],
                {"pipe": other, "ctx": peer},
            )
            for d, peer in enumerate([c] + ctx_peers)
        ]

    def spread(snd, b):
        return [
            remote(
                snd.at[b], ost.at[w, b], ssem.at[o_ss + b * (m - 1) + d], rsem.at[o_rs + b * m + w], {"wa": peer}
            )
            for d, peer in enumerate(wa_peers)
        ]

    def hand_on(snd, at, b):
        @pl.when(side == at)
        def _():
            for copy in cross(snd, 1 - at, b):
                copy.start()

        @pl.when(side == 1 - at)
        def _():
            for copy in spread(snd, b):
                copy.start()
            ost[w, b] = snd[b]

    def spread_on():
        for b in range(micro):
            for p in wa_peers:
                arrive(ost.at[p, b], rsem.at[o_rs + b * m + p])
        back[0]()
        ob[:, c] = ost[c]

    for b in range(micro):
        value = sum2[1](b)
        snd1[b] = (h1[b] + value + shift[3:4, :]).astype(low)
        hand_on(snd1, 0, b)

    later.remove(sum2[2])
    sum2[2]()
    later.remove(sum1[2])
    sum1[2]()
    def column(at, x):
        sv[at : at + 1, :] = sv[at : at + 1, :] + jnp.sum(x, axis=0, keepdims=True)

    def norm_back(d_out, normed, inv_std, row):
        lifted = d_out * gain[row : row + 1, :]
        first = jnp.mean(lifted, axis=-1, keepdims=True)
        second = jnp.mean(lifted * normed, axis=-1, keepdims=True)
        return inv_std * (lifted - first - normed * second)

    sum3 = summing(p1, r3)
    for b in range(micro):

        @pl.when(side == 0)
        def _():
            for p in range(n):
                arrive(xx.at[1, piece(b, p), :], rsem.at[x_rs + b * n + p])

        for at, size in tiles_of(ff):
            d_pre = dot(xx[c_at, batch(b), :], mt[1, :, at : at + size], 1, 0) * slope[batch(b), at : at + size]
            sv[6:7, at : at + size] = sv[6:7, at : at + size] + jnp.sum(d_pre, axis=0, keepdims=True)
            dpre[batch(b), at : at + size] = d_pre.astype(low)
        for at, size in tiles_of(width):
            p1[batch(b), at : at + size] = dot(dpre[batch(b), :], mt[0, at : at + size, :], 1, 1).astype(low)
        sum3[0](b)
    for at, size in tiles_of(width):
        gm[1, at : at + size, :] = dot(xx[c_at, :, at : at + size], act[...], 0, 0).astype(low)
        gm[0, at : at + size, :] = dot(fi[:, at : at + size], dpre[...], 0, 0).astype(low)
    dh_ag = sharing(dh)
    for b in range(micro):
        value = sum3[1](b)
        normed, inv_std = norm(h1[b])
        cot = xx[c_at, piece(b, c), :].astype(f32)
        column(2, value)
        column(5, value * normed)
        column(3, cot)
        value = cot + norm_back(value, normed, inv_std, 1)
        dh1[b] = value
        column(1, value)
        dh[piece(b, c), :] = value.astype(low)
        dh_ag[0](b)
    pl.when(side == 1)(spread_on)

    dpairs = exchange(
        "wa",
        lambda p, t: dpair.at[p, lax.rem(t, slots), pl.ds(pl.multiple_of(t // slots * rows, 16), rows), :],
        lambda me, t: rpair.at[me, lax.rem(t, slots), pl.ds(pl.multiple_of(t // slots * rows, 16), rows), :],
        slots * micro,
    )

    def attend_back(s, b):
        d_mixed = dot(dh[batch(b), :], wt[s, :, two:], 1, 0)
        d_mixed = jnp.where(upper, 0.0, d_mixed).astype(low)
        kv = pair[:, s, batch(b), :].reshape(m * rows, two)
        weight = prob[s * micro + b]
        d_probs = dot(d_mixed, kv, 1, 1)
        delta = jnp.sum(weight * d_probs, axis=-1, keepdims=True)
        d_scores = (weight * (d_probs - delta) * scale).astype(low)
        d_query = jnp.where(upper, dot(d_scores, kv, 1, 0), 0.0)
        hv[s] = hv[s] + jnp.sum(d_query, axis=0, keepdims=True)
        dproj[s, batch(b), two:] = d_query.astype(low)
        d_kv = dot(d_scores, q_s[s, batch(b), :], 0, 0) + dot(weight.astype(low), d_mixed, 0, 0)
        dpair[:, s, batch(b), :] = d_kv.astype(low).reshape(m, rows, two)
        dpairs[0](b * slots + s)

    for b in range(micro):
        dh_ag[1](b)

        def attend_back_all(s, _):
            attend_back(s, b)
            return 0

        lax.fori_loop(0, slots, attend_back_all, 0)
    gm_p = exchange("wa", lambda p, t: gm.at[t, :, lanes(p)], lambda me, t: rgm.at[me, t], 2)
    gh_p = single(
        jnp.logical_not(diagonal), gm.at[:, :, tail], lambda at: rgh.at[at], {"wa": c},
        [(diagonal, p) for p in wa_peers], w,
    )
    gm_p[0](1)
    gm_p[0](0)
    gh_p[0]()

    sum4 = summing(p2, r4)
    for b in range(micro):

        def collect(s, _):
            value = dpair[w, s, batch(b), :].astype(f32)
            dpairs[1](b * slots + s)
            for p in wa_peers:
                value = value + rpair[p, s, batch(b), :].astype(f32)
            dproj[s, batch(b), :two] = value.astype(low)
            hv[s] = hv[s] + jnp.where(upper, 0.0, jnp.sum(value, axis=0, keepdims=True))
            return 0

        lax.fori_loop(0, slots, collect, 0)
        for at, size in tiles_of(width):
            value = dot(dproj[0, batch(b), :], wt[0, at : at + size, :], 1, 1)
            for s in range(1, slots):
                value = value + dot(dproj[s, batch(b), :], wt[s, at : at + size, :], 1, 1)
            p2[batch(b), at : at + size] = value.astype(low)
        sum4[0](b)

    at_drain = later.pop(0), later.pop(0)
    at_drain[0]()
    at_drain[1]()

    ga_p = exchange("wa", lambda p, t: w_in.at[p, t], lambda me, t: ra.at[me, t], slots)

    def attn_grad(s, _):
        for at, size in tiles_of(width):
            stage[at : at + size, :] = dot(a_s[:, at : at + size], dproj[s], 0, 0) + dot(
                dh[:, at : at + size], mix[s], 0, 0
            )
        for j in range(n):
            for p in range(m):
                at = (j * m + p) * part
                w_in[p, s, j] = stage[at : at + padded, :].astype(low)
        ga_p[0](s)
        return 0

    lax.fori_loop(0, slots, attn_grad, 0)
    for b in range(micro):
        value = sum4[1](b)
        normed, inv_std = norm(xx[x_at, piece(b, c), :].astype(f32))
        column(0, value)
        column(4, value * normed)
        snd2[b] = (dh1[b] + norm_back(value, normed, inv_std, 0)).astype(low)
        hand_on(snd2, 1, b)
    for s in range(slots):
        sv[8 + s : 9 + s, :two] = hv[s]
    svc[w] = sv[...]
    sv_p = exchange("wa", lambda p, t: sv, lambda me, t: svc.at[me])
    sv_p[0]()

    gm_z = exchange("ctx", lambda p, t: sm.at[t, crows(p), :], lambda me, t: zg.at[me, t], 2)
    for k in (1, 0):
        gm_p[1](k)

        def sum_mlp(i, _):
            at = pl.ds(pl.multiple_of(i * 64, 64), 64)
            value = gm[k, at, lanes(w)].astype(f32)
            for p in wa_peers:
                value = value + rgm[p, k, at, :].astype(f32)
            sm[k, at, :] = value.astype(low)
            return 0

        lax.fori_loop(0, width // 64, sum_mlp, 0)
        gm_z[0](k)
        zg[c, k] = sm[k, crows(c), :]
    gh_p[1]()
    gh_s, gh_r = take(n - 1, 1)

    def gh_copy(d, peer):
        return remote(smh.at[:, crows(peer), :], zh, ssem.at[gh_s + d], rsem.at[gh_r], {"ctx": peer})

    @pl.when(diagonal)
    def _():
        def sum_half(i, _):
            for k in range(2):
                at = pl.ds(pl.multiple_of(i * 64, 64), 64)
                value = gm[k, at, tail].astype(f32)
                for p in wa_peers:
                    value = value + rgh[p, k, at, :].astype(f32)
                smh[k, at, :] = value.astype(low)
            return 0

        lax.fori_loop(0, width // 64, sum_half, 0)
        for d, peer in enumerate(ctx_peers):
            gh_copy(d, peer).start()
        g_mlp[:, :, tail] = smh[:, crows(c), :].astype(f32)

    pl.when(side == 0)(spread_on)
    sv_p[1]()
    value = svc[0]
    for p in range(1, m):
        value = value + svc[p]
    vec_own[...] = value
    vec_all[c] = value
    sv_z = exchange("ctx", lambda p, t: vec_own, lambda me, t: vec_all.at[me])
    sv_z[0]()
    ga_z = exchange("ctx", lambda p, t: s2.at[p, t], lambda me, t: za.at[me, t], slots)

    def sum_attn(s, _):
        ga_p[1](s)
        for j in range(n):
            value = w_in[w, s, j].astype(f32)
            for p in wa_peers:
                value = value + ra[p, s, j].astype(f32)
            s2[j, s] = value.astype(low)
        ga_z[0](s)
        za[c, s] = s2[c, s]
        return 0

    lax.fori_loop(0, slots, sum_attn, 0)

    for k in (1, 0):
        gm_z[1](k)
        for p in range(n):
            g_mlp[k, :, p * share : (p + 1) * share] = zg[p, k].astype(f32)

    @pl.when(jnp.logical_not(diagonal))
    def _():
        arrive(zh, rsem.at[gh_r])
        g_mlp[:, :, tail] = zh[...].astype(f32)

    back[1]()
    for b in range(micro):
        for p in range(n):
            at = b * rows + p * sub
            out[at : at + sub, :] = ob[b, p].astype(f32)
    sv_z[1]()
    value = vec_all[0]
    for p in range(1, n):
        value = value + vec_all[p]
    g_feature[...] = value[0:4, :]
    g_gain[...] = value[4:6, :]
    for p in range(n):
        g_hidden[:, p * share : (p + 1) * share] = vec_all[p, 6:7, lanes(w)]
        for s in range(slots):
            h = s * n + p
            if h < heads:
                g_heads[h] = pltpu.roll(vec_all[p, 8 + s : 9 + s, :two], two // 2, 1)
    g_hidden[:, tail] = vec_all[w, 6:7, tail]
    for s in range(slots):
        ga_z[1](s)
        for p in range(n):
            h = s * n + p
            if h < heads:
                first = za[p, s, :, :two].astype(f32)[:part]
                second = za[p, s, :, two:].astype(f32)[:part]
                g_qkv[h, :, :two] = jnp.where(upper, first, pltpu.roll(second, two // 2, 1))
                g_qkv[h, :, two:] = first[:, : two // 2]
                g_out[h] = second[:, : two // 2]

    for drain in later:
        drain()
    back_drain()

    @pl.when(diagonal)
    def _():
        for d, peer in enumerate(ctx_peers):
            gh_copy(d, peer).wait_send()

    for snd, at in ((snd1, 0), (snd2, 1)):

        for b in range(micro):

            @pl.when(side == at)
            def _():
                for copy in cross(snd, 1 - at, b):
                    copy.wait_send()

            @pl.when(side == 1 - at)
            def _():
                for copy in spread(snd, b):
                    copy.wait_send()


def whole_step(
    section_inputs, qkv_weight, out_weight, head_bias, mlp_weight, hidden_bias, feature_bias, ln_gain, block_table
):
    n = lax.axis_size("ctx")
    m = lax.axis_size("wa")
    micro, rows, width = section_inputs.shape[1:]
    heads, part = qkv_weight.shape[1:3]
    head_dim = out_weight.shape[3]
    ff = mlp_weight.shape[3]
    depth = mlp_weight.shape[2]
    slots = (heads + n - 1) // n
    pad = slots * n - heads
    padded = part + (-part % 16)
    total = micro * rows
    chunk = total // n
    share, rest = shares(ff, n, m)
    low = jnp.bfloat16
    f32 = jnp.float32
    two = 2 * head_dim
    scale = head_dim ** (-0.5)

    query, key, value = (qkv_weight[0, :, :, i * head_dim : (i + 1) * head_dim] for i in range(3))
    pack = jnp.concatenate([value, key, out_weight[0], query], axis=-1)
    pack = jnp.pad(pack, ((0, pad), (0, padded - part), (0, 0)))
    pack = pack.reshape(slots, n, padded, 2 * two).transpose(1, 0, 2, 3)
    def v(shape, kind=low):
        return pltpu.VMEM(shape, kind)

    sub = rows // n
    wide = (total, width)
    parts = (slots, padded, 2 * two)
    scratch = (
        [v((m, slots, n) + parts[1:]), v((width + 16, 2 * two), f32), v((slots, width, 2 * two)), v((2, width, ff))]
        + [v((n, chunk, width)), v((2,) + wide), v((m, 1, ff), f32), v((1, ff), f32), v(wide)]
        + [v((slots, total, two)), v((m, slots, total, two)), v((slots * micro, rows, m * rows), f32)]
        + [v((slots, total, 2 * two))]
        + [v(wide)] * 2
        + [v((n, micro, sub, width))] * 4
        + [v(wide), v(wide), v((m, micro, sub, width)), v((micro, n, sub, width))]
        + [v((total, ff)), v((total, ff), f32), v((total, ff))]
        + [v((micro, sub, width), f32), v((micro, sub, width), f32)]
        + [v((m, slots, total, two))] * 2
        + [v((slots, total, 2 * two)), v((2, width, ff)), v((m, 2, width, share)), v((m, 2, width, rest))]
        + [v((2, width, share)), v((2, width, rest)), v((n, 2, depth, share)), v((2, depth, rest))]
        + [v((m, slots, n) + parts[1:]), v((n,) + parts), v((n,) + parts)]
        + [v((16, width), f32), v((slots, 1, two), f32), v((m, 16, width), f32), v((16, width), f32)]
        + [v((n, 16, width), f32)]
        + [v((micro, sub, width))] * 2
        + [dma(256), dma(300), dma(4), pltpu.SemaphoreType.REGULAR]
    )
    shapes = [
        jax.ShapeDtypeStruct(shape, f32)
        for shape in (
            wide,
            (heads, part, 3 * head_dim),
            (heads, part, head_dim),
            (heads, 1, two),
            (2, depth, ff),
            (1, ff),
            (4, width),
            (2, width),
        )
    ]
    sizes = (rows, width, ff, slots, micro, head_dim, part, padded)
    out, g_qkv, g_out, g_heads, g_mlp, g_hidden, g_feature, g_gain = pl.pallas_call(
        functools.partial(step_kernel, n, m, sizes, scale),
        out_shape=shapes,
        in_specs=[VM] * 7 + [pl.BlockSpec(memory_space=pltpu.SMEM)],
        out_specs=[VM] * len(shapes),
        scratch_shapes=scratch,
        compiler_params=pltpu.CompilerParams(
            collective_id=IDS["step"], has_side_effects=True, vmem_limit_bytes=61 * 1024 * 1024
        ),
        name="step",
    )(
        section_inputs.reshape(total, width),
        pack,
        mlp_weight[0],
        head_bias.reshape(heads, 1, two),
        hidden_bias,
        feature_bias[0],
        ln_gain[0],
        block_table.T,
    )
    return (
        out.reshape(1, micro, rows, width),
        g_qkv[None],
        g_out[None],
        g_heads.reshape(1, heads, two),
        g_mlp[None],
        g_hidden,
        g_feature[None],
        g_gain[None],
    )


def fits(mesh, rows, micro, width, ff):
    n, m = mesh.shape["ctx"], mesh.shape["wa"]
    depth, chunk = width // n, micro * rows // n
    share, rest = shares(ff, n, m)
    even = depth % 16 == 0 and chunk % 16 == 0 and rows // n % 16 == 0 and width % 64 == 0
    return n == m and n <= 4 and even and ff <= width and 0 < rest <= 128 and share > 0


def either(mesh, *args):
    micro, rows, width = args[0].shape[1:]
    if fits(mesh, rows, micro, width, args[4].shape[3]):
        return whole_step(*args)
    return per_device(*args)


def solution(mesh):
    return jax.shard_map(
        functools.partial(either, mesh),
        mesh=mesh,
        in_specs=(
            P("pipe", None, "ctx", None),
            P("pipe", None, ("ctx", "wa"), None),
            P("pipe", None, ("ctx", "wa"), None),
            P("pipe", None, None),
            P("pipe", None, "ctx", "wa"),
            P("pipe", "wa"),
            P("pipe", None, None),
            P("pipe", None, None),
            P(),
        ),
        out_specs=(
            P("pipe", None, "ctx", None),
            P("pipe", None, ("ctx", "wa"), None),
            P("pipe", None, ("ctx", "wa"), None),
            P("pipe", None, None),
            P("pipe", None, "ctx", "wa"),
            P("pipe", "wa"),
            P("pipe", None, None),
            P("pipe", None, None),
        ),
        check_vma=False,
    )
```

```python
import functools

import jax
import jax.numpy as jnp
from jax import lax
from jax.experimental import pallas as pl
from jax.experimental.pallas import tpu as pltpu
from jax.sharding import PartitionSpec as P

EPS = 1e-05
GELU_C = 0.7978845608028654
GELU_A = 0.044715
KERNELS = True
MESH = pl.DeviceIdType.MESH
VM = pl.BlockSpec(memory_space=pltpu.VMEM)
IDS = {"sum_wa": 1, "swap_wa": 2, "swap_ctx": 3, "line_attn": 4, "line_mlp": 5, "line_pair": 6, "swap_mlp": 7,
       "swap_attn": 8, "all_small": 9, "all_heads": 10, "swap_grad": 11, "step": 12}


def remote(src, dst, send, recv, peer):
    return pltpu.make_async_remote_copy(
        src_ref=src, dst_ref=dst, send_sem=send, recv_sem=recv, device_id=peer, device_id_type=MESH
    )


def greet(peers):
    barrier = pltpu.get_barrier_semaphore()
    for peer in peers:
        pl.semaphore_signal(barrier, inc=1, device_id=peer, device_id_type=MESH)
    pl.semaphore_wait(barrier, len(peers))


def sum_kernel(axis, n, x_ref, o_ref, got, send_a, recv_a, send_b, recv_b):
    me = lax.axis_index(axis)
    peers = [{axis: lax.rem(me + d, n)} for d in range(1, n)]
    greet(peers)
    first = [
        remote(x_ref.at[lax.rem(me + d, n)], got.at[d - 1], send_a.at[d - 1], recv_a.at[d - 1], peers[d - 1])
        for d in range(1, n)
    ]
    for copy in first:
        copy.start()
    total = x_ref[me].astype(jnp.float32)
    for d, copy in enumerate(first):
        copy.wait_recv()
        total = total + got[d].astype(jnp.float32)
    o_ref[me] = total.astype(o_ref.dtype)
    second = [
        remote(o_ref.at[me], o_ref.at[me], send_b.at[d - 1], recv_b.at[d - 1], peers[d - 1]) for d in range(1, n)
    ]
    for copy in second:
        copy.start()
    for copy in first:
        copy.wait_send()
    for copy in second:
        copy.wait()


def swap_kernel(axis, n, x_ref, o_ref, send, recv, local):
    me = lax.axis_index(axis)
    peers = [{axis: lax.rem(me + d, n)} for d in range(1, n)]
    greet(peers)
    copies = [
        remote(x_ref.at[lax.rem(me + d, n)], o_ref.at[me], send.at[d - 1], recv.at[d - 1], peers[d - 1])
        for d in range(1, n)
    ]
    for copy in copies:
        copy.start()
    own = pltpu.make_async_copy(x_ref.at[me], o_ref.at[me], local)
    own.start()
    own.wait()
    for copy in copies:
        copy.wait()


def all_kernel(axis, n, x_ref, o_ref, send, recv, local):
    me = lax.axis_index(axis)
    peers = [{axis: lax.rem(me + d, n)} for d in range(1, n)]
    greet(peers)
    copies = [
        remote(x_ref, o_ref.at[me], send.at[d - 1], recv.at[d - 1], peers[d - 1]) for d in range(1, n)
    ]
    for copy in copies:
        copy.start()
    own = pltpu.make_async_copy(x_ref, o_ref.at[me], local)
    own.start()
    own.wait()
    for copy in copies:
        copy.wait()


def line_kernel(n, both, x_ref, o_ref, send_r, recv_r, send_l, recv_l, send_p, recv_p, local):
    me = lax.axis_index("ctx")
    side = lax.axis_index("pipe")
    row = side if both else 0
    right, left, mate = {"ctx": me + 1}, {"ctx": me - 1}, {"pipe": 1 - side}
    barrier = pltpu.get_barrier_semaphore()
    not_last, not_first = me + 1 < n, me > 0

    @pl.when(not_last)
    def _():
        pl.semaphore_signal(barrier, inc=1, device_id=right, device_id_type=MESH)

    @pl.when(not_first)
    def _():
        pl.semaphore_signal(barrier, inc=1, device_id=left, device_id_type=MESH)

    if both:
        pl.semaphore_signal(barrier, inc=1, device_id=mate, device_id_type=MESH)
    extra = 1 if both else 0

    @pl.when(not_first & not_last)
    def _():
        pl.semaphore_wait(barrier, 2 + extra)

    @pl.when(jnp.logical_not(not_first & not_last))
    def _():
        pl.semaphore_wait(barrier, 1 + extra)

    own = pltpu.make_async_copy(x_ref, o_ref.at[row, me], local)
    own.start()

    def block(at, fresh):
        return x_ref if fresh else o_ref.at[row, at]

    def to_right(s):
        return remote(block(me - s, s == 0), o_ref.at[row, me - s], send_r.at[s], recv_r.at[s], right)

    def to_left(s):
        return remote(block(me + s, s == 0), o_ref.at[row, me + s], send_l.at[s], recv_l.at[s], left)

    def to_mate(at, fresh):
        return remote(block(at, fresh), o_ref.at[row, at], send_p.at[at], recv_p.at[at], mate)

    def arrived(at, sem):
        return remote(o_ref.at[row, at], o_ref.at[row, at], send_r.at[0], sem, mate)

    for s in range(n):

        @pl.when(me - s >= 0)
        def _():
            if s > 0:
                arrived(me - s, recv_r.at[s - 1]).wait_recv()
            if s < n - 1:

                @pl.when(not_last)
                def _():
                    to_right(s).start()

            if both and s > 0:
                to_mate(me - s, False).start()

        @pl.when(me + s < n)
        def _():
            if s > 0:
                arrived(me + s, recv_l.at[s - 1]).wait_recv()
            if s < n - 1:

                @pl.when(not_first)
                def _():
                    to_left(s).start()

            if both:
                to_mate(me + s, s == 0).start()

    own.wait()
    for s in range(n - 1):

        @pl.when((me - s >= 0) & not_last)
        def _():
            to_right(s).wait_send()

        @pl.when((me + s < n) & not_first)
        def _():
            to_left(s).wait_send()

    if both:
        for at in range(n):
            to_mate(at, False).wait_send()
            remote(o_ref.at[1 - side, at], o_ref.at[1 - side, at], send_p.at[at], recv_p.at[at], mate).wait_recv()


def call(kernel, name, shape, scratch, x):
    return pl.pallas_call(
        kernel,
        out_shape=jax.ShapeDtypeStruct(shape, x.dtype),
        in_specs=[VM],
        out_specs=VM,
        scratch_shapes=scratch,
        compiler_params=pltpu.CompilerParams(
            collective_id=IDS[name], has_side_effects=True, vmem_limit_bytes=60 * 1024 * 1024
        ),
        name=name,
    )(x)


def dma(count):
    return pltpu.SemaphoreType.DMA((count,))


def summed(x):
    n = lax.axis_size("wa")
    low = x.astype(jnp.bfloat16)
    if not KERNELS:
        return lax.psum(low.astype(jnp.float32), "wa").astype(jnp.bfloat16).astype(jnp.float32)
    parts = low.reshape(n, low.shape[0] // n, low.shape[1])
    scratch = [pltpu.VMEM((n - 1,) + parts.shape[1:], jnp.bfloat16)] + [dma(n - 1)] * 4
    out = call(functools.partial(sum_kernel, "wa", n), "sum_wa", parts.shape, scratch, parts)
    return out.reshape(low.shape).astype(jnp.float32)


def swapped(x, axis, name):
    n = lax.axis_size(axis)
    if not KERNELS:
        return lax.all_to_all(x, axis, split_axis=0, concat_axis=0, tiled=True)
    scratch = [dma(n - 1)] * 2 + [pltpu.SemaphoreType.DMA]
    return call(functools.partial(swap_kernel, axis, n), name, x.shape, scratch, x)


def gathered(x, axis, name):
    n = lax.axis_size(axis)
    if not KERNELS:
        return lax.all_gather(x, axis)
    scratch = [dma(n - 1)] * 2 + [pltpu.SemaphoreType.DMA]
    return call(functools.partial(all_kernel, axis, n), name, (n,) + x.shape, scratch, x)


def lined(x, both, name):
    n = lax.axis_size("ctx")
    if not KERNELS:
        out = lax.all_gather(x, "ctx")
        return lax.all_gather(out, "pipe") if both else out[None]
    scratch = [dma(n - 1)] * 4 + [dma(n)] * 2 + [pltpu.SemaphoreType.DMA]
    return call(functools.partial(line_kernel, n, both), name, (2 if both else 1, n) + x.shape, scratch, x)


def dot(a, b, ca, cb):
    return lax.dot_general(a, b, (((ca,), (cb,)), ((), ())), preferred_element_type=jnp.float32)


def attend_kernel(scale, qpos, kpos, q_ref, kv_ref, mix_ref, total_ref):
    heads = q_ref.shape[0]
    allowed = kpos[...] <= qpos[...]
    for h in range(heads):
        kv = kv_ref[:, h].reshape(-1, kv_ref.shape[-1])
        scores = jnp.where(allowed, dot(q_ref[h], kv, 1, 1) * scale, -jnp.inf)
        top = jnp.max(scores, axis=-1, keepdims=True)
        total = top + jnp.log(jnp.sum(jnp.exp(scores - top), axis=-1, keepdims=True))
        probs = jnp.exp(scores - total).astype(jnp.bfloat16)
        mix_ref[h] = dot(probs, kv, 1, 0).astype(jnp.bfloat16)
        total_ref[h] = total


def attend_back_kernel(scale, qpos, kpos, q_ref, kv_ref, dm_ref, total_ref, dq_ref, dkv_ref):
    heads = q_ref.shape[0]
    allowed = kpos[...] <= qpos[...]
    for h in range(heads):
        kv = kv_ref[:, h].reshape(-1, kv_ref.shape[-1])
        scores = jnp.where(allowed, dot(q_ref[h], kv, 1, 1) * scale, -jnp.inf)
        probs = jnp.exp(scores - total_ref[h])
        d_probs = dot(dm_ref[h], kv, 1, 1)
        delta = jnp.sum(probs * d_probs, axis=-1, keepdims=True)
        d_scores = (probs * (d_probs - delta) * scale).astype(jnp.bfloat16)
        dq_ref[h] = dot(d_scores, kv, 1, 0)
        d_kv = dot(d_scores, q_ref[h], 0, 0) + dot(probs.astype(jnp.bfloat16), dm_ref[h], 0, 0)
        dkv_ref[:, h] = d_kv.astype(jnp.bfloat16).reshape(dkv_ref.shape[0], dkv_ref.shape[2], dkv_ref.shape[3])


def local_call(kernel, shapes, *args):
    return pl.pallas_call(
        kernel,
        out_shape=[jax.ShapeDtypeStruct(*s) for s in shapes],
        in_specs=[VM] * len(args),
        out_specs=[VM] * len(shapes),
        compiler_params=pltpu.CompilerParams(vmem_limit_bytes=48 * 1024 * 1024),
        interpret=not KERNELS,
    )(*args)

def norm_forward(stream, gain, offset):
    centre = jnp.mean(stream, axis=-1, keepdims=True)
    centred = stream - centre
    variance = jnp.mean(centred * centred, axis=-1, keepdims=True)
    inv_std = lax.rsqrt(variance + EPS)
    normed = centred * inv_std
    return (normed * gain + offset, normed, inv_std)


def norm_backward(grad_out, normed, inv_std, gain):
    grad_normed = grad_out * gain
    first_mean = jnp.mean(grad_normed, axis=-1, keepdims=True)
    second_mean = jnp.mean(grad_normed * normed, axis=-1, keepdims=True)
    return inv_std * (grad_normed - first_mean - normed * second_mean)


def gelu_value(hidden):
    tangent = jnp.tanh(GELU_C * (hidden + GELU_A * hidden * hidden * hidden))
    return 0.5 * hidden * (1.0 + tangent)


def gelu_slope(hidden):
    tangent = jnp.tanh(GELU_C * (hidden + GELU_A * hidden * hidden * hidden))
    return 0.5 * (1.0 + tangent) + 0.5 * hidden * (1.0 - tangent * tangent) * GELU_C * (
        1.0 + 3.0 * GELU_A * hidden * hidden
    )


def per_device(
    section_inputs,
    qkv_weight,
    out_weight,
    head_bias,
    mlp_weight,
    hidden_bias,
    feature_bias,
    ln_gain,
    block_table,
):
    ctx_count = lax.axis_size("ctx")
    shard_count = lax.axis_size("wa")
    side = lax.axis_index("pipe")
    ctx_index = lax.axis_index("ctx")
    shard_index = lax.axis_index("wa")
    rows = section_inputs.shape[2]
    width = section_inputs.shape[3]
    head_count = qkv_weight.shape[1]
    head_dim = out_weight.shape[3]
    part = qkv_weight.shape[2]
    slots = (head_count + shard_count - 1) // shard_count
    pad = slots * shard_count - head_count
    block_rows = rows // 2
    scale = head_dim ** (-0.5)
    swap = [(0, 1), (1, 0)]
    low = jnp.bfloat16

    own_blocks = lax.dynamic_index_in_dim(block_table, ctx_index, 0, keepdims=False)
    step = jnp.arange(block_rows, dtype=jnp.int32)
    query_pos = (own_blocks[:, None] * block_rows + step[None, :]).reshape(rows, 1)
    key_pos = (block_table.reshape(-1)[:, None] * block_rows + step[None, :]).reshape(1, rows * ctx_count)

    def mine(first, second):
        return jnp.where(side == 0, first, second)

    inputs = section_inputs[0]
    traded = lax.ppermute(mine(inputs[1], inputs[0]), "pipe", swap)
    layer_input = mine(inputs[0], traded)
    last_cot = mine(traded, inputs[1])

    packed = jnp.concatenate([qkv_weight[0], out_weight[0]], axis=-1)
    packed = jnp.pad(packed, ((0, pad), (0, 0), (0, 0)))
    packed = packed.reshape(slots, shard_count, part, 4 * head_dim).transpose(1, 0, 2, 3)
    attn_all = lined(swapped(packed, "wa", "swap_wa"), True, "line_attn")
    mlp_all = lined(mlp_weight[0], True, "line_mlp")

    sizes = [head_bias[0].size, hidden_bias[0].size, feature_bias[0].size]
    small = jnp.concatenate(
        [head_bias[0].reshape(-1), hidden_bias[0], feature_bias[0].reshape(-1), ln_gain[0].reshape(-1)]
    )
    small_mate = lax.ppermute(small, "pipe", swap)

    def params_of(layer):
        weight = attn_all[layer].transpose(2, 0, 1, 3, 4).reshape(slots, width, 4 * head_dim)
        up = mlp_all[layer][:, 0].reshape(width, -1)
        down = mlp_all[layer][:, 1].reshape(width, -1)
        flat = jnp.where(side == layer, small, small_mate)
        heads, hidden, feature, gains = jnp.split(flat, [sizes[0], sizes[0] + sizes[1], sum(sizes)])
        heads = jnp.pad(heads.reshape(head_count, 2 * head_dim), ((0, pad), (0, 0)))
        heads = heads.reshape(slots, shard_count, 2 * head_dim)
        heads = lax.dynamic_index_in_dim(heads, shard_index, 1, keepdims=False)
        return (
            weight[:, :, : 3 * head_dim],
            weight[:, :, 3 * head_dim :],
            heads,
            up,
            down,
            hidden,
            feature.reshape(4, width),
            gains.reshape(2, width),
        )

    def widened(x, before):
        zero = jnp.zeros_like(x)
        return jnp.concatenate([zero, x] if before else [x, zero], axis=-1)

    def forward(layer_in, params):
        w_qkv, w_out, bias, w_up, w_down, bias_hidden, shifts, gains = params
        stream = layer_in.astype(jnp.float32)
        normed_in, normed_one, inv_one = norm_forward(stream, gains[0], shifts[0])
        attn_in = normed_in.astype(low)
        projected = jnp.einsum("td,hde->hte", attn_in, w_qkv, preferred_element_type=jnp.float32)
        queries = widened((projected[:, :, :head_dim] + bias[:, None, :head_dim]).astype(low), False)
        key_rows = projected[:, :, head_dim : 2 * head_dim].astype(low)
        values = (projected[:, :, 2 * head_dim :] + bias[:, None, head_dim:]).astype(low)
        pairs = lined(jnp.concatenate([key_rows, values], axis=-1), False, "line_pair")[0]
        mixed, log_total = local_call(
            functools.partial(attend_kernel, scale),
            [((slots, rows, 2 * head_dim), low), ((slots, rows, 1), jnp.float32)],
            query_pos,
            key_pos,
            queries,
            pairs,
        )
        mixed = mixed[:, :, head_dim:]
        attn_out = summed(jnp.einsum("hte,hde->td", mixed, w_out, preferred_element_type=jnp.float32))
        first_sum = stream + attn_out + shifts[1]
        normed_ffn, normed_two, inv_two = norm_forward(first_sum, gains[1], shifts[2])
        ffn_in = normed_ffn.astype(low)
        pre = jnp.dot(ffn_in, w_up, preferred_element_type=jnp.float32) + bias_hidden
        act = gelu_value(pre).astype(low)
        layer_out = (
            first_sum
            + summed(jnp.einsum("tf,df->td", act, w_down, preferred_element_type=jnp.float32))
            + shifts[3]
        )
        return layer_out, (
            normed_one, inv_one, attn_in, queries, pairs, mixed, log_total, normed_two, inv_two, ffn_in, pre, act,
        )

    def backward(cot, saved, params):
        w_qkv, w_out, bias, w_up, w_down, bias_hidden, shifts, gains = params
        normed_one, inv_one, attn_in, queries, pairs, mixed, log_total, normed_two, inv_two, ffn_in, pre, act = saved
        cotangent = cot.astype(jnp.float32)
        grad_down = jnp.einsum("ti,tf->if", cot, act, preferred_element_type=jnp.float32)
        d_act = jnp.einsum("ti,if->tf", cot, w_down, preferred_element_type=jnp.float32)
        d_pre = d_act * gelu_slope(pre)
        grad_hidden = jnp.sum(d_pre, axis=0)
        d_pre_low = d_pre.astype(low)
        grad_up = jnp.einsum("td,tf->df", ffn_in, d_pre_low, preferred_element_type=jnp.float32)
        d_ffn = summed(jnp.einsum("tf,df->td", d_pre_low, w_up, preferred_element_type=jnp.float32))
        d_first = cotangent + norm_backward(d_ffn, normed_two, inv_two, gains[1])
        d_first_low = d_first.astype(low)
        grad_out = jnp.einsum("ti,hte->hie", d_first_low, mixed, preferred_element_type=jnp.float32)
        d_mixed = jnp.einsum("ti,hie->hte", d_first_low, w_out, preferred_element_type=jnp.float32)
        d_query, pair_terms = local_call(
            functools.partial(attend_back_kernel, scale),
            [((slots, rows, 2 * head_dim), jnp.float32), (pairs.shape, low)],
            query_pos,
            key_pos,
            queries,
            pairs,
            widened(d_mixed.astype(low), True),
            log_total,
        )
        d_query = d_query[:, :, :head_dim]
        d_pair = swapped(pair_terms, "ctx", "swap_ctx").astype(jnp.float32).sum(axis=0)
        grad_heads = jnp.concatenate(
            [jnp.sum(d_query, axis=1), jnp.sum(d_pair[:, :, head_dim:], axis=1)], axis=-1
        )
        d_proj = jnp.concatenate([d_query.astype(low), d_pair.astype(low)], axis=-1)
        grad_qkv = jnp.einsum("td,hte->hde", attn_in, d_proj, preferred_element_type=jnp.float32)
        d_attn = summed(jnp.einsum("hte,hde->td", d_proj, w_qkv, preferred_element_type=jnp.float32))
        d_input = d_first + norm_backward(d_attn, normed_one, inv_one, gains[0])
        vectors = [
            jnp.sum(d_attn, axis=0),
            jnp.sum(d_first, axis=0),
            jnp.sum(d_ffn, axis=0),
            jnp.sum(cotangent, axis=0),
            jnp.sum(d_attn * normed_one, axis=0),
            jnp.sum(d_ffn * normed_two, axis=0),
            grad_hidden,
            grad_heads.reshape(-1),
        ]
        attn_grad = jnp.concatenate([grad_qkv, grad_out], axis=-1).astype(low)
        mlp_grad = jnp.stack([grad_up, grad_down]).astype(low)
        return d_input, attn_grad, mlp_grad, jnp.concatenate(vectors)

    params = [params_of(0), params_of(1)]
    first_out, first_saved = forward(layer_input, params[0])
    last_out, last_saved = forward(first_out.astype(low), params[1])
    back, attn_one, mlp_one, vec_one = backward(last_cot, last_saved, params[1])
    d_input, attn_zero, mlp_zero, vec_zero = backward(back.astype(low), first_saved, params[0])

    def over_pipe(zero, one):
        kept = mine(zero, one)
        got = lax.ppermute(mine(one, zero), "pipe", swap)
        return kept.astype(jnp.float32) + got.astype(jnp.float32)

    mlp_sum = over_pipe(mlp_zero, mlp_one).astype(low)
    mlp_sum = mlp_sum.reshape(2, ctx_count, width // ctx_count, -1).transpose(1, 0, 2, 3)
    mlp_out = swapped(mlp_sum, "ctx", "swap_mlp").astype(jnp.float32).sum(axis=0)

    attn_sum = over_pipe(attn_zero, attn_one).astype(low)
    attn_sum = attn_sum.reshape(slots, ctx_count, shard_count, part, 4 * head_dim).transpose(1, 2, 0, 3, 4)
    attn_part = swapped(attn_sum, "ctx", "swap_attn").astype(jnp.float32).sum(axis=0).astype(low)
    attn_out = swapped(attn_part, "wa", "swap_grad")
    attn_out = attn_out.transpose(1, 0, 2, 3).reshape(slots * shard_count, part, 4 * head_dim)
    attn_out = attn_out[:head_count].astype(jnp.float32)

    vec = over_pipe(vec_zero, vec_one)
    length = vec.shape[0]
    fill = -length % 128
    vec = jnp.pad(vec, (0, fill)).reshape(-1, 128)
    vec = gathered(vec, "ctx", "all_small").sum(axis=0).reshape(-1)[:length]
    feature_sum, gain_sum, hidden_own, head_own = jnp.split(
        vec, [4 * width, 6 * width, 6 * width + hidden_bias.shape[1]]
    )
    head_sum = gathered(head_own.reshape(slots, 2 * head_dim), "wa", "all_heads")
    head_sum = head_sum.transpose(1, 0, 2).reshape(slots * shard_count, 2 * head_dim)[:head_count]

    last_traded = lax.ppermute(mine(last_out, d_input), "pipe", swap)
    section_outputs = jnp.where(
        side == 0, jnp.stack([d_input, last_traded]), jnp.stack([last_traded, last_out])
    )
    return (
        section_outputs[None],
        attn_out[None, :, :, : 3 * head_dim],
        attn_out[None, :, :, 3 * head_dim :],
        head_sum[None],
        mlp_out[None],
        hidden_own[None],
        feature_sum.reshape(1, 4, width),
        gain_sum.reshape(1, 2, width),
    )


def tiles_of(total, size=256):
    return [(at, min(size, total - at)) for at in range(0, total, size)]


def shares(ff, n, m):
    share = ff // 128 // n * 128
    return share, ff - n * share


def step_kernel(n, m, sizes, scale, *refs):
    rows, width, ff, slots, micro, head_dim, part, padded = sizes
    (
        inp, pack, mlp, bias, hidden, shift, gain, table,
        out, g_qkv, g_out, g_heads, g_mlp, g_hidden, g_feature, g_gain,
        w_in, stage, wt, mt, xin, xx, hid_all, hid, a_s, q_s, pair, prob, mix,
        p1, p2, r1, r2, r3, r4, fi, dh, ost, ob, act, slope, dpre, h1, dh1,
        dpair, rpair, dproj, gm, rgm, rgh, sm, smh, zg, zh, ra, s2, za, sv, hv, svc, vec_own, vec_all, snd1, snd2,
        ssem, rsem, loc, go,
    ) = refs
    side = lax.axis_index("pipe")
    c = lax.axis_index("ctx")
    w = lax.axis_index("wa")
    total = micro * rows
    chunk = total // n
    sub = rows // n
    heads = g_heads.shape[0]
    depth = width // n
    share, rest = shares(ff, n, m)
    tail = slice(n * share, ff)
    two = 2 * head_dim
    low = jnp.bfloat16
    f32 = jnp.float32
    mate = {"pipe": 1 - side}
    later = []
    used = [0, 0]

    def take(sends, recvs):
        at = tuple(used)
        used[0] += sends
        used[1] += recvs
        return at

    ctx_peers = [lax.rem(c + d, n) for d in range(1, n)]
    wa_peers = [lax.rem(w + d, m) for d in range(1, m)]

    greet(
        [{"ctx": peer} for peer in ctx_peers]
        + [{"wa": peer} for peer in wa_peers]
        + [{"pipe": 1 - side, "ctx": peer} for peer in [c] + ctx_peers]
    )

    def arrive(ref, sem):
        remote(ref, ref, sem, sem, mate).wait_recv()

    def exchange(axis, src, dst, times=1):
        me, count, peers = (c, n, ctx_peers) if axis == "ctx" else (w, m, wa_peers)
        s0, r0 = take(times * (count - 1), times * count)

        def copy(d, peer, t):
            return remote(
                src(peer, t), dst(me, t), ssem.at[s0 + t * (count - 1) + d], rsem.at[r0 + t * count + me], {axis: peer}
            )

        def start(t=0):
            for d, peer in enumerate(peers):
                copy(d, peer, t).start()

        def got(t=0):
            for peer in peers:
                arrive(dst(peer, t), rsem.at[r0 + t * count + peer])

        def drain():
            def one(t, _):
                for d, peer in enumerate(peers):
                    copy(d, peer, t).wait_send()
                return 0

            if times == 1:
                one(0, 0)
            else:
                lax.fori_loop(0, times, one, 0)

        later.append(drain)
        return start, got

    def single(cond_send, src, dst, peer, cond_recvs, slot):
        s0, r0 = take(1, max(n, m))

        def copy():
            return remote(src, dst(slot), ssem.at[s0], rsem.at[r0 + slot], peer)

        def start():
            pl.when(cond_send)(lambda: copy().start())

        def got():
            for cond, p in cond_recvs:
                pl.when(cond)(functools.partial(arrive, dst(p), rsem.at[r0 + p]))

        later.append(lambda: pl.when(cond_send)(lambda: copy().wait_send()))
        return start, got

    def crows(at):
        return pl.ds(pl.multiple_of(at * depth, 16), depth)

    def chunks(at):
        return pl.ds(pl.multiple_of(at * chunk, 16), chunk)

    def lanes(at):
        return pl.ds(pl.multiple_of(at * share, 128), share)

    def piece(b, at):
        return pl.ds(pl.multiple_of(b * rows + at * sub, 16), sub)

    def batch(b):
        return slice(b * rows, (b + 1) * rows)

    diagonal = c == w

    at_z = exchange("ctx", lambda p, t: pack.at[p, t], lambda me, t: w_in.at[w, t, me], slots)
    at_p = exchange("wa", lambda p, t: w_in.at[w, t], lambda me, t: w_in.at[me, t], slots)
    x_z = exchange("ctx", lambda p, t: inp.at[chunks(w), :], lambda me, t: xin.at[me])
    x_p = exchange("wa", lambda p, t: xin.at[p], lambda me, t: xx.at[0, chunks(me), :])
    hid_p = exchange("wa", lambda p, t: hidden, lambda me, t: hid_all.at[me])
    ml_z = exchange("ctx", lambda p, t: mlp.at[:, :, lanes(p)], lambda me, t: mt.at[:, crows(me), lanes(w)])
    ml_p = exchange("wa", lambda p, t: mt.at[t, :, lanes(w)], lambda me, t: mt.at[t, :, lanes(me)], 2)
    mh_z = single(
        jnp.logical_not(diagonal), mlp.at[:, :, tail], lambda at: mt.at[:, crows(at), tail], {"ctx": w},
        [(diagonal, p) for p in ctx_peers], c,
    )
    mh_s, mh_r = take(m - 1, 1)

    def mh_copy(d, peer):
        return remote(mt.at[:, :, tail], mt.at[:, :, tail], ssem.at[mh_s + d], rsem.at[mh_r], {"wa": peer})

    own_pack = pltpu.make_async_copy(pack.at[c], w_in.at[w, :, c], loc.at[0])
    own_mlp = pltpu.make_async_copy(mlp.at[:, :, lanes(c)], mt.at[:, crows(c), lanes(w)], loc.at[1])
    own_x = pltpu.make_async_copy(inp.at[chunks(w), :], xin.at[c], loc.at[2])
    own_half = pltpu.make_async_copy(mlp.at[:, :, tail], mt.at[:, crows(c), tail], loc.at[3])

    own_pack.start()
    own_mlp.start()
    own_x.start()
    pl.when(diagonal)(lambda: own_half.start())

    pl.when(side == 1)(lambda: pl.semaphore_wait(go, 1))
    def start_attn(t, _):
        at_z[0](t)
        return 0

    lax.fori_loop(0, slots, start_attn, 0)
    x_z[0]()
    hid_p[0]()
    ml_z[0]()
    mh_z[0]()
    stage[...] = jnp.zeros_like(stage)
    mix[...] = jnp.zeros_like(mix)
    sv[...] = jnp.zeros_like(sv)
    hv[...] = jnp.zeros_like(hv)
    own_pack.wait()

    def pass_attn(t, _):
        at_z[1](t)
        at_p[0](t)
        return 0

    lax.fori_loop(0, slots, pass_attn, 0)
    own_x.wait()
    x_z[1]()
    x_p[0]()
    xx[0, chunks(w), :] = xin[w]
    hid_p[1]()
    hid_all[w] = hidden[...]
    for p in range(m):
        hid[:, p * share : (p + 1) * share] = hid_all[p, :, lanes(c)]
    hid[:, tail] = hid_all[c, :, tail]
    x_p[1]()
    x_ss, x_rs = take(micro * n, micro * n)
    x_at = side
    c_at = 1 - side

    def norm(stream):
        centre = jnp.mean(stream, axis=-1, keepdims=True)
        centred = stream - centre
        variance = jnp.mean(centred * centred, axis=-1, keepdims=True)
        inv_std = lax.rsqrt(variance + EPS)
        return centred * inv_std, inv_std

    def first_norm(b):
        for at, size in tiles_of(rows, 64):
            here = slice(b * rows + at, b * rows + at + size)
            normed, _ = norm(xx[x_at, here, :].astype(f32))
            a_s[here, :] = (normed * gain[0:1, :] + shift[0:1, :]).astype(low)

    upper = lax.broadcasted_iota(jnp.int32, (1, two), 1) >= head_dim
    pairs = exchange(
        "wa",
        lambda p, t: pair.at[w, lax.rem(t, slots), pl.ds(pl.multiple_of(t // slots * rows, 16), rows), :],
        lambda me, t: pair.at[me, lax.rem(t, slots), pl.ds(pl.multiple_of(t // slots * rows, 16), rows), :],
        slots * micro,
    )

    def lay(s):
        at_p[1](s)
        for j in range(n):
            for p in range(m):
                at = (j * m + p) * part
                stage[at : at + part, :] = w_in[p, s, j].astype(f32)[:part]
        wt[s] = stage[:width, :].astype(low)

    def project(s, b):
        made = dot(a_s[batch(b), :], wt[s], 1, 0)
        row = pltpu.roll(bias[jnp.minimum(s * n + c, heads - 1)], two // 2, 1)
        pair[w, s, batch(b), :] = (made[:, :two] + jnp.where(upper, 0.0, row)).astype(low)
        q_s[s, batch(b), :] = jnp.where(upper, made[:, two:] + row, 0.0).astype(low)
        pairs[0](b * slots + s)

    @pl.when(side == 0)
    def _():
        for b in range(micro):
            first_norm(b)

        def both(s, _):
            lay(s)
            for b in range(micro):
                project(s, b)
            return 0

        lax.fori_loop(0, slots, both, 0)

    @pl.when(side == 1)
    def _():
        def alone(s, _):
            lay(s)
            return 0

        lax.fori_loop(0, slots, alone, 0)

    own_mlp.wait()
    ml_z[1]()
    ml_p[0](0)
    ml_p[0](1)

    @pl.when(diagonal)
    def _():
        own_half.wait()

    mh_z[1]()

    @pl.when(diagonal)
    def _():
        for d, peer in enumerate(wa_peers):
            mh_copy(d, peer).start()

    def mh_drain():
        for d, peer in enumerate(wa_peers):
            mh_copy(d, peer).wait_send()

    later.append(lambda: pl.when(diagonal)(mh_drain))

    @pl.when(side == 0)
    def _():
        pl.semaphore_signal(go, inc=1, device_id=mate, device_id_type=MESH)

    @pl.when(side == 1)
    def _():
        for b in range(micro):
            for p in range(n):
                arrive(xx.at[1, piece(b, p), :], rsem.at[x_rs + b * n + p])
            first_norm(b)

            def one(s, _):
                project(s, b)
                return 0

            lax.fori_loop(0, slots, one, 0)

    block = rows // 2
    step = lax.broadcasted_iota(jnp.int32, (rows, 1), 0)
    qpos = jnp.where(step < block, table[0, w] * block + step, table[1, w] * block + step - block)
    along = lax.broadcasted_iota(jnp.int32, (1, m * rows), 1)
    kpos = along
    for i in range(2 * m):
        inside = (along >= i * block) & (along < (i + 1) * block)
        kpos = jnp.where(inside, table[i % 2, i // 2] * block + along - i * block, kpos)

    def attend(s, b):
        pairs[1](b * slots + s)
        kv = pair[:, s, batch(b), :].reshape(m * rows, two)
        scores = jnp.where(kpos <= qpos, dot(q_s[s, batch(b), :], kv, 1, 1) * scale, -jnp.inf)
        top = jnp.max(scores, axis=-1, keepdims=True)
        raised = jnp.exp(scores - top)
        weight = raised / jnp.sum(raised, axis=-1, keepdims=True)
        prob[s * micro + b] = weight
        mixed = dot(weight.astype(low), kv, 1, 0)
        mix[s, batch(b), two:] = jnp.where(upper, 0.0, mixed).astype(low)

    def summing(part_s, got_s):
        start, got = exchange(
            "ctx", lambda p, t: part_s.at[piece(t, p), :], lambda me, t: got_s.at[me, t], micro
        )

        def finish(b):
            value = part_s[piece(b, c), :].astype(f32)
            got(b)
            for p in ctx_peers:
                value = value + got_s[p, b].astype(f32)
            return value

        return start, finish, later[-1]

    def sharing(ref):
        return exchange("ctx", lambda p, t: ref.at[piece(t, c), :], lambda me, t: ref.at[piece(t, me), :], micro)

    sum1 = summing(p1, r1)
    for b in range(micro):

        def attend_all(s, _):
            attend(s, b)
            return 0

        lax.fori_loop(0, slots, attend_all, 0)
        for at, size in tiles_of(width):
            value = dot(mix[0, batch(b), two:], wt[0, at : at + size, two:], 1, 1)
            for s in range(1, slots):
                value = value + dot(mix[s, batch(b), two:], wt[s, at : at + size, two:], 1, 1)
            p1[batch(b), at : at + size] = value.astype(low)
        sum1[0](b)
    fi_ag = sharing(fi)
    for b in range(micro):
        value = sum1[1](b)
        value = xx[x_at, piece(b, c), :].astype(f32) + value + shift[1:2, :]
        h1[b] = value
        normed, _ = norm(value)
        fi[piece(b, c), :] = (normed * gain[1:2, :] + shift[2:3, :]).astype(low)
        fi_ag[0](b)

    sum2 = summing(p2, r2)

    def down(b):
        for at, size in tiles_of(width):
            p2[batch(b), at : at + size] = dot(act[batch(b), :], mt[1, at : at + size, :], 1, 1).astype(low)
        sum2[0](b)

    for b in range(micro):
        if b == 0:
            ml_p[1](0)
            pl.when(jnp.logical_not(diagonal))(lambda: arrive(mt.at[:, :, tail], rsem.at[mh_r]))
        fi_ag[1](b)
        for at, size in tiles_of(ff):
            pre = dot(fi[batch(b), :], mt[0, :, at : at + size], 1, 0) + hid[:, at : at + size]
            square = pre * pre
            tangent = jnp.tanh(GELU_C * (pre + GELU_A * square * pre))
            act[batch(b), at : at + size] = (0.5 * pre * (1.0 + tangent)).astype(low)
            slope[batch(b), at : at + size] = 0.5 * (1.0 + tangent) + 0.5 * pre * (
                1.0 - tangent * tangent
            ) * GELU_C * (1.0 + 3.0 * GELU_A * square)
        if b == 0:
            ml_p[1](1)
        pl.when(side == 0)(functools.partial(down, b))

    o_ss, o_rs = take(micro * (m - 1), micro * m)
    back = exchange("ctx", lambda p, t: ost.at[p], lambda me, t: ob.at[:, me])
    back_drain = later.pop()

    def cross(snd, other, b):
        return [
            remote(
                snd.at[b], xx.at[1, piece(b, c), :], ssem.at[x_ss + b * n + d], rsem.at[x_rs + b * n + c],
                {"pipe": other, "ctx": peer},
            )
            for d, peer in enumerate([c] + ctx_peers)
        ]

    def spread(snd, b):
        return [
            remote(
                snd.at[b], ost.at[w, b], ssem.at[o_ss + b * (m - 1) + d], rsem.at[o_rs + b * m + w], {"wa": peer}
            )
            for d, peer in enumerate(wa_peers)
        ]

    def hand_on(snd, at, b):
        @pl.when(side == at)
        def _():
            for copy in cross(snd, 1 - at, b):
                copy.start()

        @pl.when(side == 1 - at)
        def _():
            for copy in spread(snd, b):
                copy.start()
            ost[w, b] = snd[b]

    def spread_on():
        for b in range(micro):
            for p in wa_peers:
                arrive(ost.at[p, b], rsem.at[o_rs + b * m + p])
        back[0]()
        ob[:, c] = ost[c]

    def layer_done(b):
        value = sum2[1](b)
        snd1[b] = (h1[b] + value + shift[3:4, :]).astype(low)
        hand_on(snd1, 0, b)

    @pl.when(side == 0)
    def _():
        for b in range(micro):
            layer_done(b)

    later.remove(sum1[2])
    sum1[2]()
    def column(at, x):
        sv[at : at + 1, :] = sv[at : at + 1, :] + jnp.sum(x, axis=0, keepdims=True)

    def norm_back(d_out, normed, inv_std, row):
        lifted = d_out * gain[row : row + 1, :]
        first = jnp.mean(lifted, axis=-1, keepdims=True)
        second = jnp.mean(lifted * normed, axis=-1, keepdims=True)
        return inv_std * (lifted - first - normed * second)

    sum3 = summing(p1, r3)
    for b in range(micro):

        @pl.when(side == 0)
        def _():
            for p in range(n):
                arrive(xx.at[1, piece(b, p), :], rsem.at[x_rs + b * n + p])

        for at, size in tiles_of(ff):
            d_pre = dot(xx[c_at, batch(b), :], mt[1, :, at : at + size], 1, 0) * slope[batch(b), at : at + size]
            sv[6:7, at : at + size] = sv[6:7, at : at + size] + jnp.sum(d_pre, axis=0, keepdims=True)
            dpre[batch(b), at : at + size] = d_pre.astype(low)
        for at, size in tiles_of(width):
            p1[batch(b), at : at + size] = dot(dpre[batch(b), :], mt[0, at : at + size, :], 1, 1).astype(low)
        sum3[0](b)
    gm_p = exchange("wa", lambda p, t: gm.at[t, :, lanes(p)], lambda me, t: rgm.at[me, t], 2)
    for at, size in tiles_of(width):
        gm[1, at : at + size, :] = dot(xx[c_at, :, at : at + size], act[...], 0, 0).astype(low)
    gm_p[0](1)
    for at, size in tiles_of(width):
        gm[0, at : at + size, :] = dot(fi[:, at : at + size], dpre[...], 0, 0).astype(low)
    dh_ag = sharing(dh)
    for b in range(micro):
        value = sum3[1](b)
        normed, inv_std = norm(h1[b])
        cot = xx[c_at, piece(b, c), :].astype(f32)
        column(2, value)
        column(5, value * normed)
        column(3, cot)
        value = cot + norm_back(value, normed, inv_std, 1)
        dh1[b] = value
        column(1, value)
        dh[piece(b, c), :] = value.astype(low)
        dh_ag[0](b)

    dpairs = exchange(
        "wa",
        lambda p, t: dpair.at[p, lax.rem(t, slots), pl.ds(pl.multiple_of(t // slots * rows, 16), rows), :],
        lambda me, t: rpair.at[me, lax.rem(t, slots), pl.ds(pl.multiple_of(t // slots * rows, 16), rows), :],
        slots * micro,
    )

    def attend_back(s, b):
        d_mixed = dot(dh[batch(b), :], wt[s, :, two:], 1, 0)
        d_mixed = jnp.where(upper, 0.0, d_mixed).astype(low)
        kv = pair[:, s, batch(b), :].reshape(m * rows, two)
        weight = prob[s * micro + b]
        d_probs = dot(d_mixed, kv, 1, 1)
        delta = jnp.sum(weight * d_probs, axis=-1, keepdims=True)
        d_scores = (weight * (d_probs - delta) * scale).astype(low)
        d_query = jnp.where(upper, dot(d_scores, kv, 1, 0), 0.0)
        hv[s] = hv[s] + jnp.sum(d_query, axis=0, keepdims=True)
        dproj[s, batch(b), two:] = d_query.astype(low)
        d_kv = dot(d_scores, q_s[s, batch(b), :], 0, 0) + dot(weight.astype(low), d_mixed, 0, 0)
        dpair[:, s, batch(b), :] = d_kv.astype(low).reshape(m, rows, two)
        dpairs[0](b * slots + s)

    for b in range(micro):
        dh_ag[1](b)

        def attend_back_all(s, _):
            attend_back(s, b)
            return 0

        lax.fori_loop(0, slots, attend_back_all, 0)
    gh_p = single(
        jnp.logical_not(diagonal), gm.at[:, :, tail], lambda at: rgh.at[at], {"wa": c},
        [(diagonal, p) for p in wa_peers], w,
    )
    gm_p[0](0)
    gh_p[0]()

    @pl.when(side == 1)
    def _():
        for b in range(micro):
            down(b)

    later.remove(sum3[2])
    sum3[2]()
    sum4 = summing(p1, r4)
    for b in range(micro):

        def collect(s, _):
            value = dpair[w, s, batch(b), :].astype(f32)
            dpairs[1](b * slots + s)
            for p in wa_peers:
                value = value + rpair[p, s, batch(b), :].astype(f32)
            dproj[s, batch(b), :two] = value.astype(low)
            hv[s] = hv[s] + jnp.where(upper, 0.0, jnp.sum(value, axis=0, keepdims=True))
            return 0

        lax.fori_loop(0, slots, collect, 0)
        for at, size in tiles_of(width):
            value = dot(dproj[0, batch(b), :], wt[0, at : at + size, :], 1, 1)
            for s in range(1, slots):
                value = value + dot(dproj[s, batch(b), :], wt[s, at : at + size, :], 1, 1)
            p1[batch(b), at : at + size] = value.astype(low)
        sum4[0](b)

    @pl.when(side == 1)
    def _():
        for b in range(micro):
            layer_done(b)

    at_drain = later.pop(0), later.pop(0)
    at_drain[0]()
    at_drain[1]()

    ga_p = exchange("wa", lambda p, t: w_in.at[p, t], lambda me, t: ra.at[me, t], slots)

    def attn_grad(s, _):
        for at, size in tiles_of(width):
            stage[at : at + size, :] = dot(a_s[:, at : at + size], dproj[s], 0, 0) + dot(
                dh[:, at : at + size], mix[s], 0, 0
            )
        for j in range(n):
            for p in range(m):
                at = (j * m + p) * part
                w_in[p, s, j] = stage[at : at + padded, :].astype(low)
        ga_p[0](s)
        return 0

    lax.fori_loop(0, slots, attn_grad, 0)
    for b in range(micro):
        value = sum4[1](b)
        normed, inv_std = norm(xx[x_at, piece(b, c), :].astype(f32))
        column(0, value)
        column(4, value * normed)
        snd2[b] = (dh1[b] + norm_back(value, normed, inv_std, 0)).astype(low)
        hand_on(snd2, 1, b)
    for s in range(slots):
        sv[8 + s : 9 + s, :two] = hv[s]
    svc[w] = sv[...]
    sv_p = exchange("wa", lambda p, t: sv, lambda me, t: svc.at[me])
    sv_p[0]()

    gm_z = exchange("ctx", lambda p, t: sm.at[t, crows(p), :], lambda me, t: zg.at[me, t], 2)
    for k in (1, 0):
        gm_p[1](k)

        def sum_mlp(i, _):
            at = pl.ds(pl.multiple_of(i * 64, 64), 64)
            value = gm[k, at, lanes(w)].astype(f32)
            for p in wa_peers:
                value = value + rgm[p, k, at, :].astype(f32)
            sm[k, at, :] = value.astype(low)
            return 0

        lax.fori_loop(0, width // 64, sum_mlp, 0)
        gm_z[0](k)
        zg[c, k] = sm[k, crows(c), :]
    gh_p[1]()
    gh_s, gh_r = take(n - 1, 1)

    def gh_copy(d, peer):
        return remote(smh.at[:, crows(peer), :], zh, ssem.at[gh_s + d], rsem.at[gh_r], {"ctx": peer})

    @pl.when(diagonal)
    def _():
        def sum_half(i, _):
            for k in range(2):
                at = pl.ds(pl.multiple_of(i * 64, 64), 64)
                value = gm[k, at, tail].astype(f32)
                for p in wa_peers:
                    value = value + rgh[p, k, at, :].astype(f32)
                smh[k, at, :] = value.astype(low)
            return 0

        lax.fori_loop(0, width // 64, sum_half, 0)
        for d, peer in enumerate(ctx_peers):
            gh_copy(d, peer).start()
        g_mlp[:, :, tail] = smh[:, crows(c), :].astype(f32)

    spread_on()
    sv_p[1]()
    value = svc[0]
    for p in range(1, m):
        value = value + svc[p]
    vec_own[...] = value
    vec_all[c] = value
    sv_z = exchange("ctx", lambda p, t: vec_own, lambda me, t: vec_all.at[me])
    sv_z[0]()
    ga_z = exchange("ctx", lambda p, t: s2.at[p, t], lambda me, t: za.at[me, t], slots)

    def sum_attn(s, _):
        ga_p[1](s)
        for j in range(n):
            value = w_in[w, s, j].astype(f32)
            for p in wa_peers:
                value = value + ra[p, s, j].astype(f32)
            s2[j, s] = value.astype(low)
        ga_z[0](s)
        za[c, s] = s2[c, s]
        return 0

    lax.fori_loop(0, slots, sum_attn, 0)

    for k in (1, 0):
        gm_z[1](k)
        for p in range(n):
            g_mlp[k, :, p * share : (p + 1) * share] = zg[p, k].astype(f32)

    @pl.when(jnp.logical_not(diagonal))
    def _():
        arrive(zh, rsem.at[gh_r])
        g_mlp[:, :, tail] = zh[...].astype(f32)

    back[1]()
    for b in range(micro):
        for p in range(n):
            at = b * rows + p * sub
            out[at : at + sub, :] = ob[b, p].astype(f32)
    sv_z[1]()
    value = vec_all[0]
    for p in range(1, n):
        value = value + vec_all[p]
    g_feature[...] = value[0:4, :]
    g_gain[...] = value[4:6, :]
    for p in range(n):
        g_hidden[:, p * share : (p + 1) * share] = vec_all[p, 6:7, lanes(w)]
        for s in range(slots):
            h = s * n + p
            if h < heads:
                g_heads[h] = pltpu.roll(vec_all[p, 8 + s : 9 + s, :two], two // 2, 1)
    g_hidden[:, tail] = vec_all[w, 6:7, tail]
    for s in range(slots):
        ga_z[1](s)
        for p in range(n):
            h = s * n + p
            if h < heads:
                first = za[p, s, :, :two].astype(f32)[:part]
                second = za[p, s, :, two:].astype(f32)[:part]
                g_qkv[h, :, :two] = jnp.where(upper, first, pltpu.roll(second, two // 2, 1))
                g_qkv[h, :, two:] = first[:, : two // 2]
                g_out[h] = second[:, : two // 2]

    for drain in later:
        drain()
    back_drain()

    @pl.when(diagonal)
    def _():
        for d, peer in enumerate(ctx_peers):
            gh_copy(d, peer).wait_send()

    for snd, at in ((snd1, 0), (snd2, 1)):

        for b in range(micro):

            @pl.when(side == at)
            def _():
                for copy in cross(snd, 1 - at, b):
                    copy.wait_send()

            @pl.when(side == 1 - at)
            def _():
                for copy in spread(snd, b):
                    copy.wait_send()


def whole_step(
    section_inputs, qkv_weight, out_weight, head_bias, mlp_weight, hidden_bias, feature_bias, ln_gain, block_table
):
    n = lax.axis_size("ctx")
    m = lax.axis_size("wa")
    micro, rows, width = section_inputs.shape[1:]
    heads, part = qkv_weight.shape[1:3]
    head_dim = out_weight.shape[3]
    ff = mlp_weight.shape[3]
    depth = mlp_weight.shape[2]
    slots = (heads + n - 1) // n
    pad = slots * n - heads
    padded = part + (-part % 16)
    total = micro * rows
    chunk = total // n
    share, rest = shares(ff, n, m)
    low = jnp.bfloat16
    f32 = jnp.float32
    two = 2 * head_dim
    scale = head_dim ** (-0.5)

    query, key, value = (qkv_weight[0, :, :, i * head_dim : (i + 1) * head_dim] for i in range(3))
    pack = jnp.concatenate([value, key, out_weight[0], query], axis=-1)
    pack = jnp.pad(pack, ((0, pad), (0, padded - part), (0, 0)))
    pack = pack.reshape(slots, n, padded, 2 * two).transpose(1, 0, 2, 3)
    def v(shape, kind=low):
        return pltpu.VMEM(shape, kind)

    sub = rows // n
    wide = (total, width)
    parts = (slots, padded, 2 * two)
    scratch = (
        [v((m, slots, n) + parts[1:]), v((width + 16, 2 * two), f32), v((slots, width, 2 * two)), v((2, width, ff))]
        + [v((n, chunk, width)), v((2,) + wide), v((m, 1, ff), f32), v((1, ff), f32), v(wide)]
        + [v((slots, total, two)), v((m, slots, total, two)), v((slots * micro, rows, m * rows), f32)]
        + [v((slots, total, 2 * two))]
        + [v(wide)] * 2
        + [v((n, micro, sub, width))] * 4
        + [v(wide), v(wide), v((m, micro, sub, width)), v((micro, n, sub, width))]
        + [v((total, ff)), v((total, ff), f32), v((total, ff))]
        + [v((micro, sub, width), f32), v((micro, sub, width), f32)]
        + [v((m, slots, total, two))] * 2
        + [v((slots, total, 2 * two)), v((2, width, ff)), v((m, 2, width, share)), v((m, 2, width, rest))]
        + [v((2, width, share)), v((2, width, rest)), v((n, 2, depth, share)), v((2, depth, rest))]
        + [v((m, slots, n) + parts[1:]), v((n,) + parts), v((n,) + parts)]
        + [v((16, width), f32), v((slots, 1, two), f32), v((m, 16, width), f32), v((16, width), f32)]
        + [v((n, 16, width), f32)]
        + [v((micro, sub, width))] * 2
        + [dma(256), dma(300), dma(4), pltpu.SemaphoreType.REGULAR]
    )
    shapes = [
        jax.ShapeDtypeStruct(shape, f32)
        for shape in (
            wide,
            (heads, part, 3 * head_dim),
            (heads, part, head_dim),
            (heads, 1, two),
            (2, depth, ff),
            (1, ff),
            (4, width),
            (2, width),
        )
    ]
    sizes = (rows, width, ff, slots, micro, head_dim, part, padded)
    out, g_qkv, g_out, g_heads, g_mlp, g_hidden, g_feature, g_gain = pl.pallas_call(
        functools.partial(step_kernel, n, m, sizes, scale),
        out_shape=shapes,
        in_specs=[VM] * 7 + [pl.BlockSpec(memory_space=pltpu.SMEM)],
        out_specs=[VM] * len(shapes),
        scratch_shapes=scratch,
        compiler_params=pltpu.CompilerParams(
            collective_id=IDS["step"], has_side_effects=True, vmem_limit_bytes=61 * 1024 * 1024
        ),
        name="step",
    )(
        section_inputs.reshape(total, width),
        pack,
        mlp_weight[0],
        head_bias.reshape(heads, 1, two),
        hidden_bias,
        feature_bias[0],
        ln_gain[0],
        block_table.T,
    )
    return (
        out.reshape(1, micro, rows, width),
        g_qkv[None],
        g_out[None],
        g_heads.reshape(1, heads, two),
        g_mlp[None],
        g_hidden,
        g_feature[None],
        g_gain[None],
    )


def fits(mesh, rows, micro, width, ff):
    n, m = mesh.shape["ctx"], mesh.shape["wa"]
    depth, chunk = width // n, micro * rows // n
    share, rest = shares(ff, n, m)
    even = depth % 16 == 0 and chunk % 16 == 0 and rows // n % 16 == 0 and width % 64 == 0
    return n == m and n <= 4 and even and ff <= width and 0 < rest <= 128 and share > 0


def either(mesh, *args):
    micro, rows, width = args[0].shape[1:]
    if fits(mesh, rows, micro, width, args[4].shape[3]):
        return whole_step(*args)
    return per_device(*args)


def solution(mesh):
    return jax.shard_map(
        functools.partial(either, mesh),
        mesh=mesh,
        in_specs=(
            P("pipe", None, "ctx", None),
            P("pipe", None, ("ctx", "wa"), None),
            P("pipe", None, ("ctx", "wa"), None),
            P("pipe", None, None),
            P("pipe", None, "ctx", "wa"),
            P("pipe", "wa"),
            P("pipe", None, None),
            P("pipe", None, None),
            P(),
        ),
        out_specs=(
            P("pipe", None, "ctx", None),
            P("pipe", None, ("ctx", "wa"), None),
            P("pipe", None, ("ctx", "wa"), None),
            P("pipe", None, None),
            P("pipe", None, "ctx", "wa"),
            P("pipe", "wa"),
            P("pipe", None, None),
            P("pipe", None, None),
        ),
        check_vma=False,
    )
```

```python
import functools

import jax
import jax.numpy as jnp
from jax import lax
from jax.experimental import pallas as pl
from jax.experimental.pallas import tpu as pltpu
from jax.sharding import PartitionSpec as P

EPS = 1e-05
GELU_C = 0.7978845608028654
GELU_A = 0.044715
KERNELS = True
MESH = pl.DeviceIdType.MESH
VM = pl.BlockSpec(memory_space=pltpu.VMEM)
IDS = {"sum_wa": 1, "swap_wa": 2, "swap_ctx": 3, "line_attn": 4, "line_mlp": 5, "line_pair": 6, "swap_mlp": 7,
       "swap_attn": 8, "all_small": 9, "all_heads": 10, "swap_grad": 11, "step": 12}


def remote(src, dst, send, recv, peer):
    return pltpu.make_async_remote_copy(
        src_ref=src, dst_ref=dst, send_sem=send, recv_sem=recv, device_id=peer, device_id_type=MESH
    )


def greet(peers):
    barrier = pltpu.get_barrier_semaphore()
    for peer in peers:
        pl.semaphore_signal(barrier, inc=1, device_id=peer, device_id_type=MESH)
    pl.semaphore_wait(barrier, len(peers))


def sum_kernel(axis, n, x_ref, o_ref, got, send_a, recv_a, send_b, recv_b):
    me = lax.axis_index(axis)
    peers = [{axis: lax.rem(me + d, n)} for d in range(1, n)]
    greet(peers)
    first = [
        remote(x_ref.at[lax.rem(me + d, n)], got.at[d - 1], send_a.at[d - 1], recv_a.at[d - 1], peers[d - 1])
        for d in range(1, n)
    ]
    for copy in first:
        copy.start()
    total = x_ref[me].astype(jnp.float32)
    for d, copy in enumerate(first):
        copy.wait_recv()
        total = total + got[d].astype(jnp.float32)
    o_ref[me] = total.astype(o_ref.dtype)
    second = [
        remote(o_ref.at[me], o_ref.at[me], send_b.at[d - 1], recv_b.at[d - 1], peers[d - 1]) for d in range(1, n)
    ]
    for copy in second:
        copy.start()
    for copy in first:
        copy.wait_send()
    for copy in second:
        copy.wait()


def swap_kernel(axis, n, x_ref, o_ref, send, recv, local):
    me = lax.axis_index(axis)
    peers = [{axis: lax.rem(me + d, n)} for d in range(1, n)]
    greet(peers)
    copies = [
        remote(x_ref.at[lax.rem(me + d, n)], o_ref.at[me], send.at[d - 1], recv.at[d - 1], peers[d - 1])
        for d in range(1, n)
    ]
    for copy in copies:
        copy.start()
    own = pltpu.make_async_copy(x_ref.at[me], o_ref.at[me], local)
    own.start()
    own.wait()
    for copy in copies:
        copy.wait()


def all_kernel(axis, n, x_ref, o_ref, send, recv, local):
    me = lax.axis_index(axis)
    peers = [{axis: lax.rem(me + d, n)} for d in range(1, n)]
    greet(peers)
    copies = [
        remote(x_ref, o_ref.at[me], send.at[d - 1], recv.at[d - 1], peers[d - 1]) for d in range(1, n)
    ]
    for copy in copies:
        copy.start()
    own = pltpu.make_async_copy(x_ref, o_ref.at[me], local)
    own.start()
    own.wait()
    for copy in copies:
        copy.wait()


def line_kernel(n, both, x_ref, o_ref, send_r, recv_r, send_l, recv_l, send_p, recv_p, local):
    me = lax.axis_index("ctx")
    side = lax.axis_index("pipe")
    row = side if both else 0
    right, left, mate = {"ctx": me + 1}, {"ctx": me - 1}, {"pipe": 1 - side}
    barrier = pltpu.get_barrier_semaphore()
    not_last, not_first = me + 1 < n, me > 0

    @pl.when(not_last)
    def _():
        pl.semaphore_signal(barrier, inc=1, device_id=right, device_id_type=MESH)

    @pl.when(not_first)
    def _():
        pl.semaphore_signal(barrier, inc=1, device_id=left, device_id_type=MESH)

    if both:
        pl.semaphore_signal(barrier, inc=1, device_id=mate, device_id_type=MESH)
    extra = 1 if both else 0

    @pl.when(not_first & not_last)
    def _():
        pl.semaphore_wait(barrier, 2 + extra)

    @pl.when(jnp.logical_not(not_first & not_last))
    def _():
        pl.semaphore_wait(barrier, 1 + extra)

    own = pltpu.make_async_copy(x_ref, o_ref.at[row, me], local)
    own.start()

    def block(at, fresh):
        return x_ref if fresh else o_ref.at[row, at]

    def to_right(s):
        return remote(block(me - s, s == 0), o_ref.at[row, me - s], send_r.at[s], recv_r.at[s], right)

    def to_left(s):
        return remote(block(me + s, s == 0), o_ref.at[row, me + s], send_l.at[s], recv_l.at[s], left)

    def to_mate(at, fresh):
        return remote(block(at, fresh), o_ref.at[row, at], send_p.at[at], recv_p.at[at], mate)

    def arrived(at, sem):
        return remote(o_ref.at[row, at], o_ref.at[row, at], send_r.at[0], sem, mate)

    for s in range(n):

        @pl.when(me - s >= 0)
        def _():
            if s > 0:
                arrived(me - s, recv_r.at[s - 1]).wait_recv()
            if s < n - 1:

                @pl.when(not_last)
                def _():
                    to_right(s).start()

            if both and s > 0:
                to_mate(me - s, False).start()

        @pl.when(me + s < n)
        def _():
            if s > 0:
                arrived(me + s, recv_l.at[s - 1]).wait_recv()
            if s < n - 1:

                @pl.when(not_first)
                def _():
                    to_left(s).start()

            if both:
                to_mate(me + s, s == 0).start()

    own.wait()
    for s in range(n - 1):

        @pl.when((me - s >= 0) & not_last)
        def _():
            to_right(s).wait_send()

        @pl.when((me + s < n) & not_first)
        def _():
            to_left(s).wait_send()

    if both:
        for at in range(n):
            to_mate(at, False).wait_send()
            remote(o_ref.at[1 - side, at], o_ref.at[1 - side, at], send_p.at[at], recv_p.at[at], mate).wait_recv()


def call(kernel, name, shape, scratch, x):
    return pl.pallas_call(
        kernel,
        out_shape=jax.ShapeDtypeStruct(shape, x.dtype),
        in_specs=[VM],
        out_specs=VM,
        scratch_shapes=scratch,
        compiler_params=pltpu.CompilerParams(
            collective_id=IDS[name], has_side_effects=True, vmem_limit_bytes=60 * 1024 * 1024
        ),
        name=name,
    )(x)


def dma(count):
    return pltpu.SemaphoreType.DMA((count,))


def summed(x):
    n = lax.axis_size("wa")
    low = x.astype(jnp.bfloat16)
    if not KERNELS:
        return lax.psum(low.astype(jnp.float32), "wa").astype(jnp.bfloat16).astype(jnp.float32)
    parts = low.reshape(n, low.shape[0] // n, low.shape[1])
    scratch = [pltpu.VMEM((n - 1,) + parts.shape[1:], jnp.bfloat16)] + [dma(n - 1)] * 4
    out = call(functools.partial(sum_kernel, "wa", n), "sum_wa", parts.shape, scratch, parts)
    return out.reshape(low.shape).astype(jnp.float32)


def swapped(x, axis, name):
    n = lax.axis_size(axis)
    if not KERNELS:
        return lax.all_to_all(x, axis, split_axis=0, concat_axis=0, tiled=True)
    scratch = [dma(n - 1)] * 2 + [pltpu.SemaphoreType.DMA]
    return call(functools.partial(swap_kernel, axis, n), name, x.shape, scratch, x)


def gathered(x, axis, name):
    n = lax.axis_size(axis)
    if not KERNELS:
        return lax.all_gather(x, axis)
    scratch = [dma(n - 1)] * 2 + [pltpu.SemaphoreType.DMA]
    return call(functools.partial(all_kernel, axis, n), name, (n,) + x.shape, scratch, x)


def lined(x, both, name):
    n = lax.axis_size("ctx")
    if not KERNELS:
        out = lax.all_gather(x, "ctx")
        return lax.all_gather(out, "pipe") if both else out[None]
    scratch = [dma(n - 1)] * 4 + [dma(n)] * 2 + [pltpu.SemaphoreType.DMA]
    return call(functools.partial(line_kernel, n, both), name, (2 if both else 1, n) + x.shape, scratch, x)


def dot(a, b, ca, cb):
    return lax.dot_general(a, b, (((ca,), (cb,)), ((), ())), preferred_element_type=jnp.float32)


def attend_kernel(scale, qpos, kpos, q_ref, kv_ref, mix_ref, total_ref):
    heads = q_ref.shape[0]
    allowed = kpos[...] <= qpos[...]
    for h in range(heads):
        kv = kv_ref[:, h].reshape(-1, kv_ref.shape[-1])
        scores = jnp.where(allowed, dot(q_ref[h], kv, 1, 1) * scale, -jnp.inf)
        top = jnp.max(scores, axis=-1, keepdims=True)
        total = top + jnp.log(jnp.sum(jnp.exp(scores - top), axis=-1, keepdims=True))
        probs = jnp.exp(scores - total).astype(jnp.bfloat16)
        mix_ref[h] = dot(probs, kv, 1, 0).astype(jnp.bfloat16)
        total_ref[h] = total


def attend_back_kernel(scale, qpos, kpos, q_ref, kv_ref, dm_ref, total_ref, dq_ref, dkv_ref):
    heads = q_ref.shape[0]
    allowed = kpos[...] <= qpos[...]
    for h in range(heads):
        kv = kv_ref[:, h].reshape(-1, kv_ref.shape[-1])
        scores = jnp.where(allowed, dot(q_ref[h], kv, 1, 1) * scale, -jnp.inf)
        probs = jnp.exp(scores - total_ref[h])
        d_probs = dot(dm_ref[h], kv, 1, 1)
        delta = jnp.sum(probs * d_probs, axis=-1, keepdims=True)
        d_scores = (probs * (d_probs - delta) * scale).astype(jnp.bfloat16)
        dq_ref[h] = dot(d_scores, kv, 1, 0)
        d_kv = dot(d_scores, q_ref[h], 0, 0) + dot(probs.astype(jnp.bfloat16), dm_ref[h], 0, 0)
        dkv_ref[:, h] = d_kv.astype(jnp.bfloat16).reshape(dkv_ref.shape[0], dkv_ref.shape[2], dkv_ref.shape[3])


def local_call(kernel, shapes, *args):
    return pl.pallas_call(
        kernel,
        out_shape=[jax.ShapeDtypeStruct(*s) for s in shapes],
        in_specs=[VM] * len(args),
        out_specs=[VM] * len(shapes),
        compiler_params=pltpu.CompilerParams(vmem_limit_bytes=48 * 1024 * 1024),
        interpret=not KERNELS,
    )(*args)

def norm_forward(stream, gain, offset):
    centre = jnp.mean(stream, axis=-1, keepdims=True)
    centred = stream - centre
    variance = jnp.mean(centred * centred, axis=-1, keepdims=True)
    inv_std = lax.rsqrt(variance + EPS)
    normed = centred * inv_std
    return (normed * gain + offset, normed, inv_std)


def norm_backward(grad_out, normed, inv_std, gain):
    grad_normed = grad_out * gain
    first_mean = jnp.mean(grad_normed, axis=-1, keepdims=True)
    second_mean = jnp.mean(grad_normed * normed, axis=-1, keepdims=True)
    return inv_std * (grad_normed - first_mean - normed * second_mean)


def gelu_value(hidden):
    tangent = jnp.tanh(GELU_C * (hidden + GELU_A * hidden * hidden * hidden))
    return 0.5 * hidden * (1.0 + tangent)


def gelu_slope(hidden):
    tangent = jnp.tanh(GELU_C * (hidden + GELU_A * hidden * hidden * hidden))
    return 0.5 * (1.0 + tangent) + 0.5 * hidden * (1.0 - tangent * tangent) * GELU_C * (
        1.0 + 3.0 * GELU_A * hidden * hidden
    )


def per_device(
    section_inputs,
    qkv_weight,
    out_weight,
    head_bias,
    mlp_weight,
    hidden_bias,
    feature_bias,
    ln_gain,
    block_table,
):
    ctx_count = lax.axis_size("ctx")
    shard_count = lax.axis_size("wa")
    side = lax.axis_index("pipe")
    ctx_index = lax.axis_index("ctx")
    shard_index = lax.axis_index("wa")
    rows = section_inputs.shape[2]
    width = section_inputs.shape[3]
    head_count = qkv_weight.shape[1]
    head_dim = out_weight.shape[3]
    part = qkv_weight.shape[2]
    slots = (head_count + shard_count - 1) // shard_count
    pad = slots * shard_count - head_count
    block_rows = rows // 2
    scale = head_dim ** (-0.5)
    swap = [(0, 1), (1, 0)]
    low = jnp.bfloat16

    own_blocks = lax.dynamic_index_in_dim(block_table, ctx_index, 0, keepdims=False)
    step = jnp.arange(block_rows, dtype=jnp.int32)
    query_pos = (own_blocks[:, None] * block_rows + step[None, :]).reshape(rows, 1)
    key_pos = (block_table.reshape(-1)[:, None] * block_rows + step[None, :]).reshape(1, rows * ctx_count)

    def mine(first, second):
        return jnp.where(side == 0, first, second)

    inputs = section_inputs[0]
    traded = lax.ppermute(mine(inputs[1], inputs[0]), "pipe", swap)
    layer_input = mine(inputs[0], traded)
    last_cot = mine(traded, inputs[1])

    packed = jnp.concatenate([qkv_weight[0], out_weight[0]], axis=-1)
    packed = jnp.pad(packed, ((0, pad), (0, 0), (0, 0)))
    packed = packed.reshape(slots, shard_count, part, 4 * head_dim).transpose(1, 0, 2, 3)
    attn_all = lined(swapped(packed, "wa", "swap_wa"), True, "line_attn")
    mlp_all = lined(mlp_weight[0], True, "line_mlp")

    sizes = [head_bias[0].size, hidden_bias[0].size, feature_bias[0].size]
    small = jnp.concatenate(
        [head_bias[0].reshape(-1), hidden_bias[0], feature_bias[0].reshape(-1), ln_gain[0].reshape(-1)]
    )
    small_mate = lax.ppermute(small, "pipe", swap)

    def params_of(layer):
        weight = attn_all[layer].transpose(2, 0, 1, 3, 4).reshape(slots, width, 4 * head_dim)
        up = mlp_all[layer][:, 0].reshape(width, -1)
        down = mlp_all[layer][:, 1].reshape(width, -1)
        flat = jnp.where(side == layer, small, small_mate)
        heads, hidden, feature, gains = jnp.split(flat, [sizes[0], sizes[0] + sizes[1], sum(sizes)])
        heads = jnp.pad(heads.reshape(head_count, 2 * head_dim), ((0, pad), (0, 0)))
        heads = heads.reshape(slots, shard_count, 2 * head_dim)
        heads = lax.dynamic_index_in_dim(heads, shard_index, 1, keepdims=False)
        return (
            weight[:, :, : 3 * head_dim],
            weight[:, :, 3 * head_dim :],
            heads,
            up,
            down,
            hidden,
            feature.reshape(4, width),
            gains.reshape(2, width),
        )

    def widened(x, before):
        zero = jnp.zeros_like(x)
        return jnp.concatenate([zero, x] if before else [x, zero], axis=-1)

    def forward(layer_in, params):
        w_qkv, w_out, bias, w_up, w_down, bias_hidden, shifts, gains = params
        stream = layer_in.astype(jnp.float32)
        normed_in, normed_one, inv_one = norm_forward(stream, gains[0], shifts[0])
        attn_in = normed_in.astype(low)
        projected = jnp.einsum("td,hde->hte", attn_in, w_qkv, preferred_element_type=jnp.float32)
        queries = widened((projected[:, :, :head_dim] + bias[:, None, :head_dim]).astype(low), False)
        key_rows = projected[:, :, head_dim : 2 * head_dim].astype(low)
        values = (projected[:, :, 2 * head_dim :] + bias[:, None, head_dim:]).astype(low)
        pairs = lined(jnp.concatenate([key_rows, values], axis=-1), False, "line_pair")[0]
        mixed, log_total = local_call(
            functools.partial(attend_kernel, scale),
            [((slots, rows, 2 * head_dim), low), ((slots, rows, 1), jnp.float32)],
            query_pos,
            key_pos,
            queries,
            pairs,
        )
        mixed = mixed[:, :, head_dim:]
        attn_out = summed(jnp.einsum("hte,hde->td", mixed, w_out, preferred_element_type=jnp.float32))
        first_sum = stream + attn_out + shifts[1]
        normed_ffn, normed_two, inv_two = norm_forward(first_sum, gains[1], shifts[2])
        ffn_in = normed_ffn.astype(low)
        pre = jnp.dot(ffn_in, w_up, preferred_element_type=jnp.float32) + bias_hidden
        act = gelu_value(pre).astype(low)
        layer_out = (
            first_sum
            + summed(jnp.einsum("tf,df->td", act, w_down, preferred_element_type=jnp.float32))
            + shifts[3]
        )
        return layer_out, (
            normed_one, inv_one, attn_in, queries, pairs, mixed, log_total, normed_two, inv_two, ffn_in, pre, act,
        )

    def backward(cot, saved, params):
        w_qkv, w_out, bias, w_up, w_down, bias_hidden, shifts, gains = params
        normed_one, inv_one, attn_in, queries, pairs, mixed, log_total, normed_two, inv_two, ffn_in, pre, act = saved
        cotangent = cot.astype(jnp.float32)
        grad_down = jnp.einsum("ti,tf->if", cot, act, preferred_element_type=jnp.float32)
        d_act = jnp.einsum("ti,if->tf", cot, w_down, preferred_element_type=jnp.float32)
        d_pre = d_act * gelu_slope(pre)
        grad_hidden = jnp.sum(d_pre, axis=0)
        d_pre_low = d_pre.astype(low)
        grad_up = jnp.einsum("td,tf->df", ffn_in, d_pre_low, preferred_element_type=jnp.float32)
        d_ffn = summed(jnp.einsum("tf,df->td", d_pre_low, w_up, preferred_element_type=jnp.float32))
        d_first = cotangent + norm_backward(d_ffn, normed_two, inv_two, gains[1])
        d_first_low = d_first.astype(low)
        grad_out = jnp.einsum("ti,hte->hie", d_first_low, mixed, preferred_element_type=jnp.float32)
        d_mixed = jnp.einsum("ti,hie->hte", d_first_low, w_out, preferred_element_type=jnp.float32)
        d_query, pair_terms = local_call(
            functools.partial(attend_back_kernel, scale),
            [((slots, rows, 2 * head_dim), jnp.float32), (pairs.shape, low)],
            query_pos,
            key_pos,
            queries,
            pairs,
            widened(d_mixed.astype(low), True),
            log_total,
        )
        d_query = d_query[:, :, :head_dim]
        d_pair = swapped(pair_terms, "ctx", "swap_ctx").astype(jnp.float32).sum(axis=0)
        grad_heads = jnp.concatenate(
            [jnp.sum(d_query, axis=1), jnp.sum(d_pair[:, :, head_dim:], axis=1)], axis=-1
        )
        d_proj = jnp.concatenate([d_query.astype(low), d_pair.astype(low)], axis=-1)
        grad_qkv = jnp.einsum("td,hte->hde", attn_in, d_proj, preferred_element_type=jnp.float32)
        d_attn = summed(jnp.einsum("hte,hde->td", d_proj, w_qkv, preferred_element_type=jnp.float32))
        d_input = d_first + norm_backward(d_attn, normed_one, inv_one, gains[0])
        vectors = [
            jnp.sum(d_attn, axis=0),
            jnp.sum(d_first, axis=0),
            jnp.sum(d_ffn, axis=0),
            jnp.sum(cotangent, axis=0),
            jnp.sum(d_attn * normed_one, axis=0),
            jnp.sum(d_ffn * normed_two, axis=0),
            grad_hidden,
            grad_heads.reshape(-1),
        ]
        attn_grad = jnp.concatenate([grad_qkv, grad_out], axis=-1).astype(low)
        mlp_grad = jnp.stack([grad_up, grad_down]).astype(low)
        return d_input, attn_grad, mlp_grad, jnp.concatenate(vectors)

    params = [params_of(0), params_of(1)]
    first_out, first_saved = forward(layer_input, params[0])
    last_out, last_saved = forward(first_out.astype(low), params[1])
    back, attn_one, mlp_one, vec_one = backward(last_cot, last_saved, params[1])
    d_input, attn_zero, mlp_zero, vec_zero = backward(back.astype(low), first_saved, params[0])

    def over_pipe(zero, one):
        kept = mine(zero, one)
        got = lax.ppermute(mine(one, zero), "pipe", swap)
        return kept.astype(jnp.float32) + got.astype(jnp.float32)

    mlp_sum = over_pipe(mlp_zero, mlp_one).astype(low)
    mlp_sum = mlp_sum.reshape(2, ctx_count, width // ctx_count, -1).transpose(1, 0, 2, 3)
    mlp_out = swapped(mlp_sum, "ctx", "swap_mlp").astype(jnp.float32).sum(axis=0)

    attn_sum = over_pipe(attn_zero, attn_one).astype(low)
    attn_sum = attn_sum.reshape(slots, ctx_count, shard_count, part, 4 * head_dim).transpose(1, 2, 0, 3, 4)
    attn_part = swapped(attn_sum, "ctx", "swap_attn").astype(jnp.float32).sum(axis=0).astype(low)
    attn_out = swapped(attn_part, "wa", "swap_grad")
    attn_out = attn_out.transpose(1, 0, 2, 3).reshape(slots * shard_count, part, 4 * head_dim)
    attn_out = attn_out[:head_count].astype(jnp.float32)

    vec = over_pipe(vec_zero, vec_one)
    length = vec.shape[0]
    fill = -length % 128
    vec = jnp.pad(vec, (0, fill)).reshape(-1, 128)
    vec = gathered(vec, "ctx", "all_small").sum(axis=0).reshape(-1)[:length]
    feature_sum, gain_sum, hidden_own, head_own = jnp.split(
        vec, [4 * width, 6 * width, 6 * width + hidden_bias.shape[1]]
    )
    head_sum = gathered(head_own.reshape(slots, 2 * head_dim), "wa", "all_heads")
    head_sum = head_sum.transpose(1, 0, 2).reshape(slots * shard_count, 2 * head_dim)[:head_count]

    last_traded = lax.ppermute(mine(last_out, d_input), "pipe", swap)
    section_outputs = jnp.where(
        side == 0, jnp.stack([d_input, last_traded]), jnp.stack([last_traded, last_out])
    )
    return (
        section_outputs[None],
        attn_out[None, :, :, : 3 * head_dim],
        attn_out[None, :, :, 3 * head_dim :],
        head_sum[None],
        mlp_out[None],
        hidden_own[None],
        feature_sum.reshape(1, 4, width),
        gain_sum.reshape(1, 2, width),
    )


def tiles_of(total, size=256):
    return [(at, min(size, total - at)) for at in range(0, total, size)]


def shares(ff, n, m):
    share = ff // 128 // n * 128
    return share, ff - n * share


def step_kernel(n, m, sizes, scale, *refs):
    rows, width, ff, slots, micro, head_dim, part, padded = sizes
    (
        inp, pack, mlp, bias, hidden, shift, gain, table,
        out, g_qkv, g_out, g_heads, g_mlp, g_hidden, g_feature, g_gain,
        w_in, stage, wt, mt, mtl, tt, xin, xx, hid_all, hid, a_s, q_s, pair, prob, mix,
        p1, p2, r1, r2, r3, r4, fi, dh, ost, ob, act, slope, dpre, h1, dh1,
        dpair, rpair, dproj, gm, gt, rgm, rgh, sm, smh, zg, zh, ra, s2, za, sv, hv, svc, vec_own, vec_all, snd1, snd2,
        ssem, rsem, loc, go,
    ) = refs
    side = lax.axis_index("pipe")
    c = lax.axis_index("ctx")
    w = lax.axis_index("wa")
    total = micro * rows
    chunk = total // n
    sub = rows // n
    heads = g_heads.shape[0]
    depth = width // n
    share, rest = shares(ff, n, m)
    tail = slice(n * share, n * share + 128)
    left = slice(n * share, ff)
    ffp = n * share + 128
    two = 2 * head_dim
    low = jnp.bfloat16
    f32 = jnp.float32
    mate = {"pipe": 1 - side}
    later = []
    used = [0, 0]

    def take(sends, recvs):
        at = tuple(used)
        used[0] += sends
        used[1] += recvs
        return at

    ctx_peers = [lax.rem(c + d, n) for d in range(1, n)]
    wa_peers = [lax.rem(w + d, m) for d in range(1, m)]

    greet(
        [{"ctx": peer} for peer in ctx_peers]
        + [{"wa": peer} for peer in wa_peers]
        + [{"pipe": 1 - side, "ctx": peer} for peer in [c] + ctx_peers]
    )

    def arrive(ref, sem):
        remote(ref, ref, sem, sem, mate).wait_recv()

    def exchange(axis, src, dst, times=1):
        me, count, peers = (c, n, ctx_peers) if axis == "ctx" else (w, m, wa_peers)
        s0, r0 = take(times * (count - 1), times * count)

        def copy(d, peer, t):
            return remote(
                src(peer, t), dst(me, t), ssem.at[s0 + t * (count - 1) + d], rsem.at[r0 + t * count + me], {axis: peer}
            )

        def start(t=0):
            for d, peer in enumerate(peers):
                copy(d, peer, t).start()

        def got(t=0):
            for peer in peers:
                arrive(dst(peer, t), rsem.at[r0 + t * count + peer])

        def drain():
            def one(t, _):
                for d, peer in enumerate(peers):
                    copy(d, peer, t).wait_send()
                return 0

            if times == 1:
                one(0, 0)
            else:
                lax.fori_loop(0, times, one, 0)

        later.append(drain)
        return start, got

    def single(cond_send, src, dst, peer, cond_recvs, slot):
        s0, r0 = take(1, max(n, m))

        def copy():
            return remote(src, dst(slot), ssem.at[s0], rsem.at[r0 + slot], peer)

        def start():
            pl.when(cond_send)(lambda: copy().start())

        def got():
            for cond, p in cond_recvs:
                pl.when(cond)(functools.partial(arrive, dst(p), rsem.at[r0 + p]))

        later.append(lambda: pl.when(cond_send)(lambda: copy().wait_send()))
        return start, got

    def crows(at):
        return pl.ds(pl.multiple_of(at * depth, 16), depth)

    def chunks(at):
        return pl.ds(pl.multiple_of(at * chunk, 16), chunk)

    def lanes(at):
        return pl.ds(pl.multiple_of(at * share, 128), share)

    def piece(b, at):
        return pl.ds(pl.multiple_of(b * rows + at * sub, 16), sub)

    def batch(b):
        return slice(b * rows, (b + 1) * rows)

    diagonal = c == w

    at_z = exchange("ctx", lambda p, t: pack.at[p, t], lambda me, t: w_in.at[w, t, me], slots)
    at_p = exchange("wa", lambda p, t: w_in.at[w, t], lambda me, t: w_in.at[me, t], slots)
    x_z = exchange("ctx", lambda p, t: inp.at[chunks(w), :], lambda me, t: xin.at[me])
    x_p = exchange("wa", lambda p, t: xin.at[p], lambda me, t: xx.at[0, chunks(me), :])
    hid_p = exchange("wa", lambda p, t: hidden, lambda me, t: hid_all.at[me])
    ml_z = exchange("ctx", lambda p, t: mlp.at[:, :, lanes(p)], lambda me, t: mt.at[:, crows(me), lanes(w)])
    ml_p = exchange("wa", lambda p, t: mt.at[t, :, lanes(w)], lambda me, t: mt.at[t, :, lanes(me)], 2)
    mh_z = single(
        jnp.logical_not(diagonal), mtl, lambda at: tt.at[crows(at), :], {"ctx": w},
        [(diagonal, p) for p in ctx_peers], c,
    )
    mh_s, mh_r = take(m - 1, 1)

    def mh_copy(d, peer):
        return remote(tt, tt, ssem.at[mh_s + d], rsem.at[mh_r], {"wa": peer})

    own_pack = pltpu.make_async_copy(pack.at[c], w_in.at[w, :, c], loc.at[0])
    own_mlp = pltpu.make_async_copy(mlp.at[:, :, lanes(c)], mt.at[:, crows(c), lanes(w)], loc.at[1])
    own_x = pltpu.make_async_copy(inp.at[chunks(w), :], xin.at[c], loc.at[2])
    own_half = pltpu.make_async_copy(mtl, tt.at[crows(c), :], loc.at[3])

    mtl[...] = jnp.zeros_like(mtl)
    mtl[:, :rest] = mlp[0, :, left]
    mtl[:, 64 : 64 + rest] = mlp[1, :, left]
    own_pack.start()
    own_mlp.start()
    own_x.start()
    pl.when(diagonal)(lambda: own_half.start())

    pl.when(side == 1)(lambda: pl.semaphore_wait(go, 1))
    def start_attn(t, _):
        at_z[0](t)
        return 0

    lax.fori_loop(0, slots, start_attn, 0)
    x_z[0]()
    hid_p[0]()
    ml_z[0]()
    mh_z[0]()
    stage[...] = jnp.zeros_like(stage)
    mix[...] = jnp.zeros_like(mix)
    sv[...] = jnp.zeros_like(sv)
    hv[...] = jnp.zeros_like(hv)
    own_pack.wait()

    def pass_attn(t, _):
        at_z[1](t)
        at_p[0](t)
        return 0

    lax.fori_loop(0, slots, pass_attn, 0)
    own_x.wait()
    x_z[1]()
    x_p[0]()
    xx[0, chunks(w), :] = xin[w]
    hid_p[1]()
    hid_all[w] = hidden[...]
    for p in range(m):
        hid[:, p * share : (p + 1) * share] = hid_all[p, :, lanes(c)]
    hid[:, tail] = jnp.zeros((1, 128), f32)
    hid[:, left] = hid_all[c, :, left]
    x_p[1]()
    x_ss, x_rs = take(micro * n, micro * n)
    x_at = side
    c_at = 1 - side

    def norm(stream):
        centre = jnp.mean(stream, axis=-1, keepdims=True)
        centred = stream - centre
        variance = jnp.mean(centred * centred, axis=-1, keepdims=True)
        inv_std = lax.rsqrt(variance + EPS)
        return centred * inv_std, inv_std

    def first_norm(b):
        for at, size in tiles_of(rows, 64):
            here = slice(b * rows + at, b * rows + at + size)
            normed, _ = norm(xx[x_at, here, :].astype(f32))
            a_s[here, :] = (normed * gain[0:1, :] + shift[0:1, :]).astype(low)

    upper = lax.broadcasted_iota(jnp.int32, (1, two), 1) >= head_dim
    pairs = exchange(
        "wa",
        lambda p, t: pair.at[w, lax.rem(t, slots), pl.ds(pl.multiple_of(t // slots * rows, 16), rows), :],
        lambda me, t: pair.at[me, lax.rem(t, slots), pl.ds(pl.multiple_of(t // slots * rows, 16), rows), :],
        slots * micro,
    )

    def lay(s):
        at_p[1](s)
        for j in range(n):
            for p in range(m):
                at = (j * m + p) * part
                stage[at : at + part, :] = w_in[p, s, j].astype(f32)[:part]
        wt[s] = stage[:width, :].astype(low)

    def project(s, b):
        made = dot(a_s[batch(b), :], wt[s], 1, 0)
        row = pltpu.roll(bias[jnp.minimum(s * n + c, heads - 1)], two // 2, 1)
        pair[w, s, batch(b), :] = (made[:, :two] + jnp.where(upper, 0.0, row)).astype(low)
        q_s[s, batch(b), :] = jnp.where(upper, made[:, two:] + row, 0.0).astype(low)
        pairs[0](b * slots + s)

    @pl.when(side == 0)
    def _():
        for b in range(micro):
            first_norm(b)

        def both(s, _):
            lay(s)
            for b in range(micro):
                project(s, b)
            return 0

        lax.fori_loop(0, slots, both, 0)

    @pl.when(side == 1)
    def _():
        def alone(s, _):
            lay(s)
            return 0

        lax.fori_loop(0, slots, alone, 0)

    own_mlp.wait()
    ml_z[1]()
    ml_p[0](0)
    ml_p[0](1)

    @pl.when(diagonal)
    def _():
        own_half.wait()

    mh_z[1]()

    @pl.when(diagonal)
    def _():
        for d, peer in enumerate(wa_peers):
            mh_copy(d, peer).start()

    def mh_drain():
        for d, peer in enumerate(wa_peers):
            mh_copy(d, peer).wait_send()

    later.append(lambda: pl.when(diagonal)(mh_drain))

    @pl.when(side == 0)
    def _():
        pl.semaphore_signal(go, inc=1, device_id=mate, device_id_type=MESH)

    @pl.when(side == 1)
    def _():
        for b in range(micro):
            for p in range(n):
                arrive(xx.at[1, piece(b, p), :], rsem.at[x_rs + b * n + p])
            first_norm(b)

            def one(s, _):
                project(s, b)
                return 0

            lax.fori_loop(0, slots, one, 0)

    block = rows // 2
    step = lax.broadcasted_iota(jnp.int32, (rows, 1), 0)
    qpos = jnp.where(step < block, table[0, w] * block + step, table[1, w] * block + step - block)
    along = lax.broadcasted_iota(jnp.int32, (1, m * rows), 1)
    kpos = along
    for i in range(2 * m):
        inside = (along >= i * block) & (along < (i + 1) * block)
        kpos = jnp.where(inside, table[i % 2, i // 2] * block + along - i * block, kpos)

    def attend(s, b):
        pairs[1](b * slots + s)
        kv = pair[:, s, batch(b), :].reshape(m * rows, two)
        scores = jnp.where(kpos <= qpos, dot(q_s[s, batch(b), :], kv, 1, 1) * scale, -jnp.inf)
        top = jnp.max(scores, axis=-1, keepdims=True)
        raised = jnp.exp(scores - top)
        weight = raised / jnp.sum(raised, axis=-1, keepdims=True)
        prob[s * micro + b] = weight
        mixed = dot(weight.astype(low), kv, 1, 0)
        mix[s, batch(b), two:] = jnp.where(upper, 0.0, mixed).astype(low)

    def summing(part_s, got_s):
        start, got = exchange(
            "ctx", lambda p, t: part_s.at[piece(t, p), :], lambda me, t: got_s.at[me, t], micro
        )

        def finish(b):
            value = part_s[piece(b, c), :].astype(f32)
            got(b)
            for p in ctx_peers:
                value = value + got_s[p, b].astype(f32)
            return value

        return start, finish, later[-1]

    def sharing(ref):
        return exchange("ctx", lambda p, t: ref.at[piece(t, c), :], lambda me, t: ref.at[piece(t, me), :], micro)

    sum1 = summing(p1, r1)
    for b in range(micro):

        def attend_all(s, _):
            attend(s, b)
            return 0

        lax.fori_loop(0, slots, attend_all, 0)
        for at, size in tiles_of(width):
            value = dot(mix[0, batch(b), two:], wt[0, at : at + size, two:], 1, 1)
            for s in range(1, slots):
                value = value + dot(mix[s, batch(b), two:], wt[s, at : at + size, two:], 1, 1)
            p1[batch(b), at : at + size] = value.astype(low)
        sum1[0](b)
    fi_ag = sharing(fi)
    for b in range(micro):
        value = sum1[1](b)
        value = xx[x_at, piece(b, c), :].astype(f32) + value + shift[1:2, :]
        h1[b] = value
        normed, _ = norm(value)
        fi[piece(b, c), :] = (normed * gain[1:2, :] + shift[2:3, :]).astype(low)
        fi_ag[0](b)

    sum2 = summing(p2, r2)
    beyond = lax.broadcasted_iota(jnp.int32, (1, 128), 1) >= 64

    def down(b):
        for at, size in tiles_of(width):
            p2[batch(b), at : at + size] = dot(act[batch(b), :], mt[1, at : at + size, :], 1, 1).astype(low)
        sum2[0](b)

    for b in range(micro):
        if b == 0:
            ml_p[1](0)
            pl.when(jnp.logical_not(diagonal))(lambda: arrive(tt, rsem.at[mh_r]))
            for at, size in tiles_of(width, 64):
                value = tt[at : at + size, :].astype(f32)
                mt[0, at : at + size, tail] = jnp.where(beyond, 0.0, value).astype(low)
                mt[1, at : at + size, tail] = jnp.where(beyond, 0.0, pltpu.roll(value, 64, 1)).astype(low)
        fi_ag[1](b)
        for at, size in tiles_of(ffp):
            pre = dot(fi[batch(b), :], mt[0, :, at : at + size], 1, 0) + hid[:, at : at + size]
            square = pre * pre
            tangent = jnp.tanh(GELU_C * (pre + GELU_A * square * pre))
            act[batch(b), at : at + size] = (0.5 * pre * (1.0 + tangent)).astype(low)
            slope[batch(b), at : at + size] = 0.5 * (1.0 + tangent) + 0.5 * pre * (
                1.0 - tangent * tangent
            ) * GELU_C * (1.0 + 3.0 * GELU_A * square)
        if b == 0:
            ml_p[1](1)
        pl.when(side == 0)(functools.partial(down, b))

    o_ss, o_rs = take(micro * (m - 1), micro * m)
    back = exchange("ctx", lambda p, t: ost.at[p], lambda me, t: ob.at[:, me])
    back_drain = later.pop()

    def cross(snd, other, b):
        return [
            remote(
                snd.at[b], xx.at[1, piece(b, c), :], ssem.at[x_ss + b * n + d], rsem.at[x_rs + b * n + c],
                {"pipe": other, "ctx": peer},
            )
            for d, peer in enumerate([c] + ctx_peers)
        ]

    def spread(snd, b):
        return [
            remote(
                snd.at[b], ost.at[w, b], ssem.at[o_ss + b * (m - 1) + d], rsem.at[o_rs + b * m + w], {"wa": peer}
            )
            for d, peer in enumerate(wa_peers)
        ]

    def hand_on(snd, at, b):
        @pl.when(side == at)
        def _():
            for copy in cross(snd, 1 - at, b):
                copy.start()

        @pl.when(side == 1 - at)
        def _():
            for copy in spread(snd, b):
                copy.start()
            ost[w, b] = snd[b]

    def spread_on():
        for b in range(micro):
            for p in wa_peers:
                arrive(ost.at[p, b], rsem.at[o_rs + b * m + p])
        back[0]()
        ob[:, c] = ost[c]

    def layer_done(b):
        value = sum2[1](b)
        snd1[b] = (h1[b] + value + shift[3:4, :]).astype(low)
        hand_on(snd1, 0, b)

    @pl.when(side == 0)
    def _():
        for b in range(micro):
            layer_done(b)

    later.remove(sum1[2])
    sum1[2]()
    def column(at, x):
        sv[at : at + 1, :] = sv[at : at + 1, :] + jnp.sum(x, axis=0, keepdims=True)

    def norm_back(d_out, normed, inv_std, row):
        lifted = d_out * gain[row : row + 1, :]
        first = jnp.mean(lifted, axis=-1, keepdims=True)
        second = jnp.mean(lifted * normed, axis=-1, keepdims=True)
        return inv_std * (lifted - first - normed * second)

    sum3 = summing(p1, r3)
    for b in range(micro):

        @pl.when(side == 0)
        def _():
            for p in range(n):
                arrive(xx.at[1, piece(b, p), :], rsem.at[x_rs + b * n + p])

        for at, size in tiles_of(ffp):
            d_pre = dot(xx[c_at, batch(b), :], mt[1, :, at : at + size], 1, 0) * slope[batch(b), at : at + size]
            over = slice(at, min(at + size, ff))
            sv[6:7, over] = sv[6:7, over] + jnp.sum(d_pre, axis=0, keepdims=True)[:, : over.stop - at]
            dpre[batch(b), at : at + size] = d_pre.astype(low)
        for at, size in tiles_of(width):
            p1[batch(b), at : at + size] = dot(dpre[batch(b), :], mt[0, at : at + size, :], 1, 1).astype(low)
        sum3[0](b)
    gm_p = exchange("wa", lambda p, t: gm.at[t, :, lanes(p)], lambda me, t: rgm.at[me, t], 2)
    for at, size in tiles_of(width):
        gm[1, at : at + size, :] = dot(xx[c_at, :, at : at + size], act[...], 0, 0).astype(low)
    gm_p[0](1)
    for at, size in tiles_of(width):
        gm[0, at : at + size, :] = dot(fi[:, at : at + size], dpre[...], 0, 0).astype(low)
    dh_ag = sharing(dh)
    for b in range(micro):
        value = sum3[1](b)
        normed, inv_std = norm(h1[b])
        cot = xx[c_at, piece(b, c), :].astype(f32)
        column(2, value)
        column(5, value * normed)
        column(3, cot)
        value = cot + norm_back(value, normed, inv_std, 1)
        dh1[b] = value
        column(1, value)
        dh[piece(b, c), :] = value.astype(low)
        dh_ag[0](b)

    dpairs = exchange(
        "wa",
        lambda p, t: dpair.at[p, lax.rem(t, slots), pl.ds(pl.multiple_of(t // slots * rows, 16), rows), :],
        lambda me, t: rpair.at[me, lax.rem(t, slots), pl.ds(pl.multiple_of(t // slots * rows, 16), rows), :],
        slots * micro,
    )

    def attend_back(s, b):
        d_mixed = dot(dh[batch(b), :], wt[s, :, two:], 1, 0)
        d_mixed = jnp.where(upper, 0.0, d_mixed).astype(low)
        kv = pair[:, s, batch(b), :].reshape(m * rows, two)
        weight = prob[s * micro + b]
        d_probs = dot(d_mixed, kv, 1, 1)
        delta = jnp.sum(weight * d_probs, axis=-1, keepdims=True)
        d_scores = (weight * (d_probs - delta) * scale).astype(low)
        d_query = jnp.where(upper, dot(d_scores, kv, 1, 0), 0.0)
        hv[s] = hv[s] + jnp.sum(d_query, axis=0, keepdims=True)
        dproj[s, batch(b), two:] = d_query.astype(low)
        d_kv = dot(d_scores, q_s[s, batch(b), :], 0, 0) + dot(weight.astype(low), d_mixed, 0, 0)
        dpair[:, s, batch(b), :] = d_kv.astype(low).reshape(m, rows, two)
        dpairs[0](b * slots + s)

    for b in range(micro):
        dh_ag[1](b)

        def attend_back_all(s, _):
            attend_back(s, b)
            return 0

        lax.fori_loop(0, slots, attend_back_all, 0)
    for at, size in tiles_of(width, 64):
        value = pltpu.roll(gm[1, at : at + size, tail].astype(f32), 64, 1)
        gt[at : at + size, :] = jnp.where(beyond, value, gm[0, at : at + size, tail].astype(f32)).astype(low)
    gh_p = single(
        jnp.logical_not(diagonal), gt, lambda at: rgh.at[at], {"wa": c},
        [(diagonal, p) for p in wa_peers], w,
    )
    gm_p[0](0)
    gh_p[0]()

    @pl.when(side == 1)
    def _():
        for b in range(micro):
            down(b)

    later.remove(sum3[2])
    sum3[2]()
    sum4 = summing(p1, r4)
    for b in range(micro):

        def collect(s, _):
            value = dpair[w, s, batch(b), :].astype(f32)
            dpairs[1](b * slots + s)
            for p in wa_peers:
                value = value + rpair[p, s, batch(b), :].astype(f32)
            dproj[s, batch(b), :two] = value.astype(low)
            hv[s] = hv[s] + jnp.where(upper, 0.0, jnp.sum(value, axis=0, keepdims=True))
            return 0

        lax.fori_loop(0, slots, collect, 0)
        for at, size in tiles_of(width):
            value = dot(dproj[0, batch(b), :], wt[0, at : at + size, :], 1, 1)
            for s in range(1, slots):
                value = value + dot(dproj[s, batch(b), :], wt[s, at : at + size, :], 1, 1)
            p1[batch(b), at : at + size] = value.astype(low)
        sum4[0](b)

    @pl.when(side == 1)
    def _():
        for b in range(micro):
            layer_done(b)

    at_drain = later.pop(0), later.pop(0)
    at_drain[0]()
    at_drain[1]()

    ga_p = exchange("wa", lambda p, t: w_in.at[p, t], lambda me, t: ra.at[me, t], slots)

    def attn_grad(s, _):
        for at, size in tiles_of(width):
            stage[at : at + size, :] = dot(a_s[:, at : at + size], dproj[s], 0, 0) + dot(
                dh[:, at : at + size], mix[s], 0, 0
            )
        for j in range(n):
            for p in range(m):
                at = (j * m + p) * part
                w_in[p, s, j] = stage[at : at + padded, :].astype(low)
        ga_p[0](s)
        return 0

    lax.fori_loop(0, slots, attn_grad, 0)
    for b in range(micro):
        value = sum4[1](b)
        normed, inv_std = norm(xx[x_at, piece(b, c), :].astype(f32))
        column(0, value)
        column(4, value * normed)
        snd2[b] = (dh1[b] + norm_back(value, normed, inv_std, 0)).astype(low)
        hand_on(snd2, 1, b)
    for s in range(slots):
        sv[8 + s : 9 + s, :two] = hv[s]
    svc[w] = sv[...]
    sv_p = exchange("wa", lambda p, t: sv, lambda me, t: svc.at[me])
    sv_p[0]()

    gm_z = exchange("ctx", lambda p, t: sm.at[t, crows(p), :], lambda me, t: zg.at[me, t], 2)
    for k in (1, 0):
        gm_p[1](k)

        def sum_mlp(i, _):
            at = pl.ds(pl.multiple_of(i * 64, 64), 64)
            value = gm[k, at, lanes(w)].astype(f32)
            for p in wa_peers:
                value = value + rgm[p, k, at, :].astype(f32)
            sm[k, at, :] = value.astype(low)
            return 0

        lax.fori_loop(0, width // 64, sum_mlp, 0)
        gm_z[0](k)
        zg[c, k] = sm[k, crows(c), :]
    gh_p[1]()
    gh_s, gh_r = take(n - 1, 1)

    def gh_copy(d, peer):
        return remote(smh.at[crows(peer), :], zh, ssem.at[gh_s + d], rsem.at[gh_r], {"ctx": peer})

    @pl.when(diagonal)
    def _():
        def sum_half(i, _):
            at = pl.ds(pl.multiple_of(i * 64, 64), 64)
            value = gt[at, :].astype(f32)
            for p in wa_peers:
                value = value + rgh[p, at, :].astype(f32)
            smh[at, :] = value.astype(low)
            return 0

        lax.fori_loop(0, width // 64, sum_half, 0)
        for d, peer in enumerate(ctx_peers):
            gh_copy(d, peer).start()
        value = smh[crows(c), :].astype(f32)
        g_mlp[0, :, left] = value[:, :rest]
        g_mlp[1, :, left] = value[:, 64 : 64 + rest]

    spread_on()
    sv_p[1]()
    value = svc[0]
    for p in range(1, m):
        value = value + svc[p]
    vec_own[...] = value
    vec_all[c] = value
    sv_z = exchange("ctx", lambda p, t: vec_own, lambda me, t: vec_all.at[me])
    sv_z[0]()
    ga_z = exchange("ctx", lambda p, t: s2.at[p, t], lambda me, t: za.at[me, t], slots)

    def sum_attn(s, _):
        ga_p[1](s)
        for j in range(n):
            value = w_in[w, s, j].astype(f32)
            for p in wa_peers:
                value = value + ra[p, s, j].astype(f32)
            s2[j, s] = value.astype(low)
        ga_z[0](s)
        za[c, s] = s2[c, s]
        return 0

    lax.fori_loop(0, slots, sum_attn, 0)

    for k in (1, 0):
        gm_z[1](k)
        for p in range(n):
            g_mlp[k, :, p * share : (p + 1) * share] = zg[p, k].astype(f32)

    @pl.when(jnp.logical_not(diagonal))
    def _():
        arrive(zh, rsem.at[gh_r])
        value = zh[...].astype(f32)
        g_mlp[0, :, left] = value[:, :rest]
        g_mlp[1, :, left] = value[:, 64 : 64 + rest]

    back[1]()
    for b in range(micro):
        for p in range(n):
            at = b * rows + p * sub
            out[at : at + sub, :] = ob[b, p].astype(f32)
    sv_z[1]()
    value = vec_all[0]
    for p in range(1, n):
        value = value + vec_all[p]
    g_feature[...] = value[0:4, :]
    g_gain[...] = value[4:6, :]
    for p in range(n):
        g_hidden[:, p * share : (p + 1) * share] = vec_all[p, 6:7, lanes(w)]
        for s in range(slots):
            h = s * n + p
            if h < heads:
                g_heads[h] = pltpu.roll(vec_all[p, 8 + s : 9 + s, :two], two // 2, 1)
    g_hidden[:, left] = vec_all[w, 6:7, left]
    for s in range(slots):
        ga_z[1](s)
        for p in range(n):
            h = s * n + p
            if h < heads:
                first = za[p, s, :, :two].astype(f32)[:part]
                second = za[p, s, :, two:].astype(f32)[:part]
                g_qkv[h, :, :two] = jnp.where(upper, first, pltpu.roll(second, two // 2, 1))
                g_qkv[h, :, two:] = first[:, : two // 2]
                g_out[h] = second[:, : two // 2]

    for drain in later:
        drain()
    back_drain()

    @pl.when(diagonal)
    def _():
        for d, peer in enumerate(ctx_peers):
            gh_copy(d, peer).wait_send()

    for snd, at in ((snd1, 0), (snd2, 1)):

        for b in range(micro):

            @pl.when(side == at)
            def _():
                for copy in cross(snd, 1 - at, b):
                    copy.wait_send()

            @pl.when(side == 1 - at)
            def _():
                for copy in spread(snd, b):
                    copy.wait_send()


def whole_step(
    section_inputs, qkv_weight, out_weight, head_bias, mlp_weight, hidden_bias, feature_bias, ln_gain, block_table
):
    n = lax.axis_size("ctx")
    m = lax.axis_size("wa")
    micro, rows, width = section_inputs.shape[1:]
    heads, part = qkv_weight.shape[1:3]
    head_dim = out_weight.shape[3]
    ff = mlp_weight.shape[3]
    depth = mlp_weight.shape[2]
    slots = (heads + n - 1) // n
    pad = slots * n - heads
    padded = part + (-part % 16)
    total = micro * rows
    chunk = total // n
    share, rest = shares(ff, n, m)
    low = jnp.bfloat16
    f32 = jnp.float32
    two = 2 * head_dim
    scale = head_dim ** (-0.5)

    query, key, value = (qkv_weight[0, :, :, i * head_dim : (i + 1) * head_dim] for i in range(3))
    pack = jnp.concatenate([value, key, out_weight[0], query], axis=-1)
    pack = jnp.pad(pack, ((0, pad), (0, padded - part), (0, 0)))
    pack = pack.reshape(slots, n, padded, 2 * two).transpose(1, 0, 2, 3)
    def v(shape, kind=low):
        return pltpu.VMEM(shape, kind)

    sub = rows // n
    ffp = n * share + 128
    wide = (total, width)
    parts = (slots, padded, 2 * two)
    scratch = (
        [v((m, slots, n) + parts[1:]), v((width + 16, 2 * two), f32), v((slots, width, 2 * two)), v((2, width, ffp)), v((depth, 128)), v((width, 128))]
        + [v((n, chunk, width)), v((2,) + wide), v((m, 1, ff), f32), v((1, ffp), f32), v(wide)]
        + [v((slots, total, two)), v((m, slots, total, two)), v((slots * micro, rows, m * rows), f32)]
        + [v((slots, total, 2 * two))]
        + [v(wide)] * 2
        + [v((n, micro, sub, width))] * 4
        + [v(wide), v(wide), v((m, micro, sub, width)), v((micro, n, sub, width))]
        + [v((total, ffp)), v((total, ffp), f32), v((total, ffp))]
        + [v((micro, sub, width), f32), v((micro, sub, width), f32)]
        + [v((m, slots, total, two))] * 2
        + [v((slots, total, 2 * two)), v((2, width, ffp)), v((width, 128)), v((m, 2, width, share)), v((m, width, 128))]
        + [v((2, width, share)), v((width, 128)), v((n, 2, depth, share)), v((depth, 128))]
        + [v((m, slots, n) + parts[1:]), v((n,) + parts), v((n,) + parts)]
        + [v((16, width), f32), v((slots, 1, two), f32), v((m, 16, width), f32), v((16, width), f32)]
        + [v((n, 16, width), f32)]
        + [v((micro, sub, width))] * 2
        + [dma(256), dma(300), dma(4), pltpu.SemaphoreType.REGULAR]
    )
    shapes = [
        jax.ShapeDtypeStruct(shape, f32)
        for shape in (
            wide,
            (heads, part, 3 * head_dim),
            (heads, part, head_dim),
            (heads, 1, two),
            (2, depth, ff),
            (1, ff),
            (4, width),
            (2, width),
        )
    ]
    sizes = (rows, width, ff, slots, micro, head_dim, part, padded)
    out, g_qkv, g_out, g_heads, g_mlp, g_hidden, g_feature, g_gain = pl.pallas_call(
        functools.partial(step_kernel, n, m, sizes, scale),
        out_shape=shapes,
        in_specs=[VM] * 7 + [pl.BlockSpec(memory_space=pltpu.SMEM)],
        out_specs=[VM] * len(shapes),
        scratch_shapes=scratch,
        compiler_params=pltpu.CompilerParams(
            collective_id=IDS["step"], has_side_effects=True, vmem_limit_bytes=61 * 1024 * 1024
        ),
        name="step",
    )(
        section_inputs.reshape(total, width),
        pack,
        mlp_weight[0],
        head_bias.reshape(heads, 1, two),
        hidden_bias,
        feature_bias[0],
        ln_gain[0],
        block_table.T,
    )
    return (
        out.reshape(1, micro, rows, width),
        g_qkv[None],
        g_out[None],
        g_heads.reshape(1, heads, two),
        g_mlp[None],
        g_hidden,
        g_feature[None],
        g_gain[None],
    )


def fits(mesh, rows, micro, width, ff):
    n, m = mesh.shape["ctx"], mesh.shape["wa"]
    depth, chunk = width // n, micro * rows // n
    share, rest = shares(ff, n, m)
    even = depth % 16 == 0 and chunk % 16 == 0 and rows // n % 16 == 0 and width % 64 == 0
    return n == m and n <= 4 and even and ff <= width and 0 < rest <= 64 and share > 0


def either(mesh, *args):
    micro, rows, width = args[0].shape[1:]
    if fits(mesh, rows, micro, width, args[4].shape[3]):
        return whole_step(*args)
    return per_device(*args)


def solution(mesh):
    return jax.shard_map(
        functools.partial(either, mesh),
        mesh=mesh,
        in_specs=(
            P("pipe", None, "ctx", None),
            P("pipe", None, ("ctx", "wa"), None),
            P("pipe", None, ("ctx", "wa"), None),
            P("pipe", None, None),
            P("pipe", None, "ctx", "wa"),
            P("pipe", "wa"),
            P("pipe", None, None),
            P("pipe", None, None),
            P(),
        ),
        out_specs=(
            P("pipe", None, "ctx", None),
            P("pipe", None, ("ctx", "wa"), None),
            P("pipe", None, ("ctx", "wa"), None),
            P("pipe", None, None),
            P("pipe", None, "ctx", "wa"),
            P("pipe", "wa"),
            P("pipe", None, None),
            P("pipe", None, None),
        ),
        check_vma=False,
    )
```

```python
import functools

import jax
import jax.numpy as jnp
from jax import lax
from jax.experimental import pallas as pl
from jax.experimental.pallas import tpu as pltpu
from jax.sharding import PartitionSpec as P

EPS = 1e-05
GELU_C = 0.7978845608028654
GELU_A = 0.044715
KERNELS = True
MESH = pl.DeviceIdType.MESH
VM = pl.BlockSpec(memory_space=pltpu.VMEM)
IDS = {"sum_wa": 1, "swap_wa": 2, "swap_ctx": 3, "line_attn": 4, "line_mlp": 5, "line_pair": 6, "swap_mlp": 7,
       "swap_attn": 8, "all_small": 9, "all_heads": 10, "swap_grad": 11, "step": 12}


def remote(src, dst, send, recv, peer):
    return pltpu.make_async_remote_copy(
        src_ref=src, dst_ref=dst, send_sem=send, recv_sem=recv, device_id=peer, device_id_type=MESH
    )


def greet(peers):
    barrier = pltpu.get_barrier_semaphore()
    for peer in peers:
        pl.semaphore_signal(barrier, inc=1, device_id=peer, device_id_type=MESH)
    pl.semaphore_wait(barrier, len(peers))


def sum_kernel(axis, n, x_ref, o_ref, got, send_a, recv_a, send_b, recv_b):
    me = lax.axis_index(axis)
    peers = [{axis: lax.rem(me + d, n)} for d in range(1, n)]
    greet(peers)
    first = [
        remote(x_ref.at[lax.rem(me + d, n)], got.at[d - 1], send_a.at[d - 1], recv_a.at[d - 1], peers[d - 1])
        for d in range(1, n)
    ]
    for copy in first:
        copy.start()
    total = x_ref[me].astype(jnp.float32)
    for d, copy in enumerate(first):
        copy.wait_recv()
        total = total + got[d].astype(jnp.float32)
    o_ref[me] = total.astype(o_ref.dtype)
    second = [
        remote(o_ref.at[me], o_ref.at[me], send_b.at[d - 1], recv_b.at[d - 1], peers[d - 1]) for d in range(1, n)
    ]
    for copy in second:
        copy.start()
    for copy in first:
        copy.wait_send()
    for copy in second:
        copy.wait()


def swap_kernel(axis, n, x_ref, o_ref, send, recv, local):
    me = lax.axis_index(axis)
    peers = [{axis: lax.rem(me + d, n)} for d in range(1, n)]
    greet(peers)
    copies = [
        remote(x_ref.at[lax.rem(me + d, n)], o_ref.at[me], send.at[d - 1], recv.at[d - 1], peers[d - 1])
        for d in range(1, n)
    ]
    for copy in copies:
        copy.start()
    own = pltpu.make_async_copy(x_ref.at[me], o_ref.at[me], local)
    own.start()
    own.wait()
    for copy in copies:
        copy.wait()


def all_kernel(axis, n, x_ref, o_ref, send, recv, local):
    me = lax.axis_index(axis)
    peers = [{axis: lax.rem(me + d, n)} for d in range(1, n)]
    greet(peers)
    copies = [
        remote(x_ref, o_ref.at[me], send.at[d - 1], recv.at[d - 1], peers[d - 1]) for d in range(1, n)
    ]
    for copy in copies:
        copy.start()
    own = pltpu.make_async_copy(x_ref, o_ref.at[me], local)
    own.start()
    own.wait()
    for copy in copies:
        copy.wait()


def line_kernel(n, both, x_ref, o_ref, send_r, recv_r, send_l, recv_l, send_p, recv_p, local):
    me = lax.axis_index("ctx")
    side = lax.axis_index("pipe")
    row = side if both else 0
    right, left, mate = {"ctx": me + 1}, {"ctx": me - 1}, {"pipe": 1 - side}
    barrier = pltpu.get_barrier_semaphore()
    not_last, not_first = me + 1 < n, me > 0

    @pl.when(not_last)
    def _():
        pl.semaphore_signal(barrier, inc=1, device_id=right, device_id_type=MESH)

    @pl.when(not_first)
    def _():
        pl.semaphore_signal(barrier, inc=1, device_id=left, device_id_type=MESH)

    if both:
        pl.semaphore_signal(barrier, inc=1, device_id=mate, device_id_type=MESH)
    extra = 1 if both else 0

    @pl.when(not_first & not_last)
    def _():
        pl.semaphore_wait(barrier, 2 + extra)

    @pl.when(jnp.logical_not(not_first & not_last))
    def _():
        pl.semaphore_wait(barrier, 1 + extra)

    own = pltpu.make_async_copy(x_ref, o_ref.at[row, me], local)
    own.start()

    def block(at, fresh):
        return x_ref if fresh else o_ref.at[row, at]

    def to_right(s):
        return remote(block(me - s, s == 0), o_ref.at[row, me - s], send_r.at[s], recv_r.at[s], right)

    def to_left(s):
        return remote(block(me + s, s == 0), o_ref.at[row, me + s], send_l.at[s], recv_l.at[s], left)

    def to_mate(at, fresh):
        return remote(block(at, fresh), o_ref.at[row, at], send_p.at[at], recv_p.at[at], mate)

    def arrived(at, sem):
        return remote(o_ref.at[row, at], o_ref.at[row, at], send_r.at[0], sem, mate)

    for s in range(n):

        @pl.when(me - s >= 0)
        def _():
            if s > 0:
                arrived(me - s, recv_r.at[s - 1]).wait_recv()
            if s < n - 1:

                @pl.when(not_last)
                def _():
                    to_right(s).start()

            if both and s > 0:
                to_mate(me - s, False).start()

        @pl.when(me + s < n)
        def _():
            if s > 0:
                arrived(me + s, recv_l.at[s - 1]).wait_recv()
            if s < n - 1:

                @pl.when(not_first)
                def _():
                    to_left(s).start()

            if both:
                to_mate(me + s, s == 0).start()

    own.wait()
    for s in range(n - 1):

        @pl.when((me - s >= 0) & not_last)
        def _():
            to_right(s).wait_send()

        @pl.when((me + s < n) & not_first)
        def _():
            to_left(s).wait_send()

    if both:
        for at in range(n):
            to_mate(at, False).wait_send()
            remote(o_ref.at[1 - side, at], o_ref.at[1 - side, at], send_p.at[at], recv_p.at[at], mate).wait_recv()


def call(kernel, name, shape, scratch, x):
    return pl.pallas_call(
        kernel,
        out_shape=jax.ShapeDtypeStruct(shape, x.dtype),
        in_specs=[VM],
        out_specs=VM,
        scratch_shapes=scratch,
        compiler_params=pltpu.CompilerParams(
            collective_id=IDS[name], has_side_effects=True, vmem_limit_bytes=60 * 1024 * 1024
        ),
        name=name,
    )(x)


def dma(count):
    return pltpu.SemaphoreType.DMA((count,))


def summed(x):
    n = lax.axis_size("wa")
    low = x.astype(jnp.bfloat16)
    if not KERNELS:
        return lax.psum(low.astype(jnp.float32), "wa").astype(jnp.bfloat16).astype(jnp.float32)
    parts = low.reshape(n, low.shape[0] // n, low.shape[1])
    scratch = [pltpu.VMEM((n - 1,) + parts.shape[1:], jnp.bfloat16)] + [dma(n - 1)] * 4
    out = call(functools.partial(sum_kernel, "wa", n), "sum_wa", parts.shape, scratch, parts)
    return out.reshape(low.shape).astype(jnp.float32)


def swapped(x, axis, name):
    n = lax.axis_size(axis)
    if not KERNELS:
        return lax.all_to_all(x, axis, split_axis=0, concat_axis=0, tiled=True)
    scratch = [dma(n - 1)] * 2 + [pltpu.SemaphoreType.DMA]
    return call(functools.partial(swap_kernel, axis, n), name, x.shape, scratch, x)


def gathered(x, axis, name):
    n = lax.axis_size(axis)
    if not KERNELS:
        return lax.all_gather(x, axis)
    scratch = [dma(n - 1)] * 2 + [pltpu.SemaphoreType.DMA]
    return call(functools.partial(all_kernel, axis, n), name, (n,) + x.shape, scratch, x)


def lined(x, both, name):
    n = lax.axis_size("ctx")
    if not KERNELS:
        out = lax.all_gather(x, "ctx")
        return lax.all_gather(out, "pipe") if both else out[None]
    scratch = [dma(n - 1)] * 4 + [dma(n)] * 2 + [pltpu.SemaphoreType.DMA]
    return call(functools.partial(line_kernel, n, both), name, (2 if both else 1, n) + x.shape, scratch, x)


def dot(a, b, ca, cb):
    return lax.dot_general(a, b, (((ca,), (cb,)), ((), ())), preferred_element_type=jnp.float32)


def attend_kernel(scale, qpos, kpos, q_ref, kv_ref, mix_ref, total_ref):
    heads = q_ref.shape[0]
    allowed = kpos[...] <= qpos[...]
    for h in range(heads):
        kv = kv_ref[:, h].reshape(-1, kv_ref.shape[-1])
        scores = jnp.where(allowed, dot(q_ref[h], kv, 1, 1) * scale, -jnp.inf)
        top = jnp.max(scores, axis=-1, keepdims=True)
        total = top + jnp.log(jnp.sum(jnp.exp(scores - top), axis=-1, keepdims=True))
        probs = jnp.exp(scores - total).astype(jnp.bfloat16)
        mix_ref[h] = dot(probs, kv, 1, 0).astype(jnp.bfloat16)
        total_ref[h] = total


def attend_back_kernel(scale, qpos, kpos, q_ref, kv_ref, dm_ref, total_ref, dq_ref, dkv_ref):
    heads = q_ref.shape[0]
    allowed = kpos[...] <= qpos[...]
    for h in range(heads):
        kv = kv_ref[:, h].reshape(-1, kv_ref.shape[-1])
        scores = jnp.where(allowed, dot(q_ref[h], kv, 1, 1) * scale, -jnp.inf)
        probs = jnp.exp(scores - total_ref[h])
        d_probs = dot(dm_ref[h], kv, 1, 1)
        delta = jnp.sum(probs * d_probs, axis=-1, keepdims=True)
        d_scores = (probs * (d_probs - delta) * scale).astype(jnp.bfloat16)
        dq_ref[h] = dot(d_scores, kv, 1, 0)
        d_kv = dot(d_scores, q_ref[h], 0, 0) + dot(probs.astype(jnp.bfloat16), dm_ref[h], 0, 0)
        dkv_ref[:, h] = d_kv.astype(jnp.bfloat16).reshape(dkv_ref.shape[0], dkv_ref.shape[2], dkv_ref.shape[3])


def local_call(kernel, shapes, *args):
    return pl.pallas_call(
        kernel,
        out_shape=[jax.ShapeDtypeStruct(*s) for s in shapes],
        in_specs=[VM] * len(args),
        out_specs=[VM] * len(shapes),
        compiler_params=pltpu.CompilerParams(vmem_limit_bytes=48 * 1024 * 1024),
        interpret=not KERNELS,
    )(*args)

def norm_forward(stream, gain, offset):
    centre = jnp.mean(stream, axis=-1, keepdims=True)
    centred = stream - centre
    variance = jnp.mean(centred * centred, axis=-1, keepdims=True)
    inv_std = lax.rsqrt(variance + EPS)
    normed = centred * inv_std
    return (normed * gain + offset, normed, inv_std)


def norm_backward(grad_out, normed, inv_std, gain):
    grad_normed = grad_out * gain
    first_mean = jnp.mean(grad_normed, axis=-1, keepdims=True)
    second_mean = jnp.mean(grad_normed * normed, axis=-1, keepdims=True)
    return inv_std * (grad_normed - first_mean - normed * second_mean)


def gelu_value(hidden):
    tangent = jnp.tanh(GELU_C * (hidden + GELU_A * hidden * hidden * hidden))
    return 0.5 * hidden * (1.0 + tangent)


def gelu_slope(hidden):
    tangent = jnp.tanh(GELU_C * (hidden + GELU_A * hidden * hidden * hidden))
    return 0.5 * (1.0 + tangent) + 0.5 * hidden * (1.0 - tangent * tangent) * GELU_C * (
        1.0 + 3.0 * GELU_A * hidden * hidden
    )


def per_device(
    section_inputs,
    qkv_weight,
    out_weight,
    head_bias,
    mlp_weight,
    hidden_bias,
    feature_bias,
    ln_gain,
    block_table,
):
    ctx_count = lax.axis_size("ctx")
    shard_count = lax.axis_size("wa")
    side = lax.axis_index("pipe")
    ctx_index = lax.axis_index("ctx")
    shard_index = lax.axis_index("wa")
    rows = section_inputs.shape[2]
    width = section_inputs.shape[3]
    head_count = qkv_weight.shape[1]
    head_dim = out_weight.shape[3]
    part = qkv_weight.shape[2]
    slots = (head_count + shard_count - 1) // shard_count
    pad = slots * shard_count - head_count
    block_rows = rows // 2
    scale = head_dim ** (-0.5)
    swap = [(0, 1), (1, 0)]
    low = jnp.bfloat16

    own_blocks = lax.dynamic_index_in_dim(block_table, ctx_index, 0, keepdims=False)
    step = jnp.arange(block_rows, dtype=jnp.int32)
    query_pos = (own_blocks[:, None] * block_rows + step[None, :]).reshape(rows, 1)
    key_pos = (block_table.reshape(-1)[:, None] * block_rows + step[None, :]).reshape(1, rows * ctx_count)

    def mine(first, second):
        return jnp.where(side == 0, first, second)

    inputs = section_inputs[0]
    traded = lax.ppermute(mine(inputs[1], inputs[0]), "pipe", swap)
    layer_input = mine(inputs[0], traded)
    last_cot = mine(traded, inputs[1])

    packed = jnp.concatenate([qkv_weight[0], out_weight[0]], axis=-1)
    packed = jnp.pad(packed, ((0, pad), (0, 0), (0, 0)))
    packed = packed.reshape(slots, shard_count, part, 4 * head_dim).transpose(1, 0, 2, 3)
    attn_all = lined(swapped(packed, "wa", "swap_wa"), True, "line_attn")
    mlp_all = lined(mlp_weight[0], True, "line_mlp")

    sizes = [head_bias[0].size, hidden_bias[0].size, feature_bias[0].size]
    small = jnp.concatenate(
        [head_bias[0].reshape(-1), hidden_bias[0], feature_bias[0].reshape(-1), ln_gain[0].reshape(-1)]
    )
    small_mate = lax.ppermute(small, "pipe", swap)

    def params_of(layer):
        weight = attn_all[layer].transpose(2, 0, 1, 3, 4).reshape(slots, width, 4 * head_dim)
        up = mlp_all[layer][:, 0].reshape(width, -1)
        down = mlp_all[layer][:, 1].reshape(width, -1)
        flat = jnp.where(side == layer, small, small_mate)
        heads, hidden, feature, gains = jnp.split(flat, [sizes[0], sizes[0] + sizes[1], sum(sizes)])
        heads = jnp.pad(heads.reshape(head_count, 2 * head_dim), ((0, pad), (0, 0)))
        heads = heads.reshape(slots, shard_count, 2 * head_dim)
        heads = lax.dynamic_index_in_dim(heads, shard_index, 1, keepdims=False)
        return (
            weight[:, :, : 3 * head_dim],
            weight[:, :, 3 * head_dim :],
            heads,
            up,
            down,
            hidden,
            feature.reshape(4, width),
            gains.reshape(2, width),
        )

    def widened(x, before):
        zero = jnp.zeros_like(x)
        return jnp.concatenate([zero, x] if before else [x, zero], axis=-1)

    def forward(layer_in, params):
        w_qkv, w_out, bias, w_up, w_down, bias_hidden, shifts, gains = params
        stream = layer_in.astype(jnp.float32)
        normed_in, normed_one, inv_one = norm_forward(stream, gains[0], shifts[0])
        attn_in = normed_in.astype(low)
        projected = jnp.einsum("td,hde->hte", attn_in, w_qkv, preferred_element_type=jnp.float32)
        queries = widened((projected[:, :, :head_dim] + bias[:, None, :head_dim]).astype(low), False)
        key_rows = projected[:, :, head_dim : 2 * head_dim].astype(low)
        values = (projected[:, :, 2 * head_dim :] + bias[:, None, head_dim:]).astype(low)
        pairs = lined(jnp.concatenate([key_rows, values], axis=-1), False, "line_pair")[0]
        mixed, log_total = local_call(
            functools.partial(attend_kernel, scale),
            [((slots, rows, 2 * head_dim), low), ((slots, rows, 1), jnp.float32)],
            query_pos,
            key_pos,
            queries,
            pairs,
        )
        mixed = mixed[:, :, head_dim:]
        attn_out = summed(jnp.einsum("hte,hde->td", mixed, w_out, preferred_element_type=jnp.float32))
        first_sum = stream + attn_out + shifts[1]
        normed_ffn, normed_two, inv_two = norm_forward(first_sum, gains[1], shifts[2])
        ffn_in = normed_ffn.astype(low)
        pre = jnp.dot(ffn_in, w_up, preferred_element_type=jnp.float32) + bias_hidden
        act = gelu_value(pre).astype(low)
        layer_out = (
            first_sum
            + summed(jnp.einsum("tf,df->td", act, w_down, preferred_element_type=jnp.float32))
            + shifts[3]
        )
        return layer_out, (
            normed_one, inv_one, attn_in, queries, pairs, mixed, log_total, normed_two, inv_two, ffn_in, pre, act,
        )

    def backward(cot, saved, params):
        w_qkv, w_out, bias, w_up, w_down, bias_hidden, shifts, gains = params
        normed_one, inv_one, attn_in, queries, pairs, mixed, log_total, normed_two, inv_two, ffn_in, pre, act = saved
        cotangent = cot.astype(jnp.float32)
        grad_down = jnp.einsum("ti,tf->if", cot, act, preferred_element_type=jnp.float32)
        d_act = jnp.einsum("ti,if->tf", cot, w_down, preferred_element_type=jnp.float32)
        d_pre = d_act * gelu_slope(pre)
        grad_hidden = jnp.sum(d_pre, axis=0)
        d_pre_low = d_pre.astype(low)
        grad_up = jnp.einsum("td,tf->df", ffn_in, d_pre_low, preferred_element_type=jnp.float32)
        d_ffn = summed(jnp.einsum("tf,df->td", d_pre_low, w_up, preferred_element_type=jnp.float32))
        d_first = cotangent + norm_backward(d_ffn, normed_two, inv_two, gains[1])
        d_first_low = d_first.astype(low)
        grad_out = jnp.einsum("ti,hte->hie", d_first_low, mixed, preferred_element_type=jnp.float32)
        d_mixed = jnp.einsum("ti,hie->hte", d_first_low, w_out, preferred_element_type=jnp.float32)
        d_query, pair_terms = local_call(
            functools.partial(attend_back_kernel, scale),
            [((slots, rows, 2 * head_dim), jnp.float32), (pairs.shape, low)],
            query_pos,
            key_pos,
            queries,
            pairs,
            widened(d_mixed.astype(low), True),
            log_total,
        )
        d_query = d_query[:, :, :head_dim]
        d_pair = swapped(pair_terms, "ctx", "swap_ctx").astype(jnp.float32).sum(axis=0)
        grad_heads = jnp.concatenate(
            [jnp.sum(d_query, axis=1), jnp.sum(d_pair[:, :, head_dim:], axis=1)], axis=-1
        )
        d_proj = jnp.concatenate([d_query.astype(low), d_pair.astype(low)], axis=-1)
        grad_qkv = jnp.einsum("td,hte->hde", attn_in, d_proj, preferred_element_type=jnp.float32)
        d_attn = summed(jnp.einsum("hte,hde->td", d_proj, w_qkv, preferred_element_type=jnp.float32))
        d_input = d_first + norm_backward(d_attn, normed_one, inv_one, gains[0])
        vectors = [
            jnp.sum(d_attn, axis=0),
            jnp.sum(d_first, axis=0),
            jnp.sum(d_ffn, axis=0),
            jnp.sum(cotangent, axis=0),
            jnp.sum(d_attn * normed_one, axis=0),
            jnp.sum(d_ffn * normed_two, axis=0),
            grad_hidden,
            grad_heads.reshape(-1),
        ]
        attn_grad = jnp.concatenate([grad_qkv, grad_out], axis=-1).astype(low)
        mlp_grad = jnp.stack([grad_up, grad_down]).astype(low)
        return d_input, attn_grad, mlp_grad, jnp.concatenate(vectors)

    params = [params_of(0), params_of(1)]
    first_out, first_saved = forward(layer_input, params[0])
    last_out, last_saved = forward(first_out.astype(low), params[1])
    back, attn_one, mlp_one, vec_one = backward(last_cot, last_saved, params[1])
    d_input, attn_zero, mlp_zero, vec_zero = backward(back.astype(low), first_saved, params[0])

    def over_pipe(zero, one):
        kept = mine(zero, one)
        got = lax.ppermute(mine(one, zero), "pipe", swap)
        return kept.astype(jnp.float32) + got.astype(jnp.float32)

    mlp_sum = over_pipe(mlp_zero, mlp_one).astype(low)
    mlp_sum = mlp_sum.reshape(2, ctx_count, width // ctx_count, -1).transpose(1, 0, 2, 3)
    mlp_out = swapped(mlp_sum, "ctx", "swap_mlp").astype(jnp.float32).sum(axis=0)

    attn_sum = over_pipe(attn_zero, attn_one).astype(low)
    attn_sum = attn_sum.reshape(slots, ctx_count, shard_count, part, 4 * head_dim).transpose(1, 2, 0, 3, 4)
    attn_part = swapped(attn_sum, "ctx", "swap_attn").astype(jnp.float32).sum(axis=0).astype(low)
    attn_out = swapped(attn_part, "wa", "swap_grad")
    attn_out = attn_out.transpose(1, 0, 2, 3).reshape(slots * shard_count, part, 4 * head_dim)
    attn_out = attn_out[:head_count].astype(jnp.float32)

    vec = over_pipe(vec_zero, vec_one)
    length = vec.shape[0]
    fill = -length % 128
    vec = jnp.pad(vec, (0, fill)).reshape(-1, 128)
    vec = gathered(vec, "ctx", "all_small").sum(axis=0).reshape(-1)[:length]
    feature_sum, gain_sum, hidden_own, head_own = jnp.split(
        vec, [4 * width, 6 * width, 6 * width + hidden_bias.shape[1]]
    )
    head_sum = gathered(head_own.reshape(slots, 2 * head_dim), "wa", "all_heads")
    head_sum = head_sum.transpose(1, 0, 2).reshape(slots * shard_count, 2 * head_dim)[:head_count]

    last_traded = lax.ppermute(mine(last_out, d_input), "pipe", swap)
    section_outputs = jnp.where(
        side == 0, jnp.stack([d_input, last_traded]), jnp.stack([last_traded, last_out])
    )
    return (
        section_outputs[None],
        attn_out[None, :, :, : 3 * head_dim],
        attn_out[None, :, :, 3 * head_dim :],
        head_sum[None],
        mlp_out[None],
        hidden_own[None],
        feature_sum.reshape(1, 4, width),
        gain_sum.reshape(1, 2, width),
    )


def tiles_of(total, size=256):
    return [(at, min(size, total - at)) for at in range(0, total, size)]


def shares(ff, n, m):
    share = ff // 128 // n * 128
    return share, ff - n * share


def step_kernel(n, m, sizes, scale, *refs):
    rows, width, ff, slots, micro, head_dim, part, padded = sizes
    (
        inp, pack, mlp, bias, hidden, shift, gain, table,
        out, g_qkv, g_out, g_heads, g_mlp, g_hidden, g_feature, g_gain,
        w_in, stage, wt, mt, mtl, tt, xin, xx, hid_all, hid, a_s, q_s, pair, prob, mix,
        p1, p2, r1, r2, r3, r4, fi, dh, ost, ob, act, slope, dpre, h1, dh1,
        dpair, rpair, dproj, gm, gt, rgm, rgh, sm, smh, zg, zh, ra, s2, za, sv, hv, svc, vec_own, vec_all, snd1, snd2,
        ssem, rsem, loc, go,
    ) = refs
    side = lax.axis_index("pipe")
    c = lax.axis_index("ctx")
    w = lax.axis_index("wa")
    total = micro * rows
    chunk = total // n
    sub = rows // n
    heads = g_heads.shape[0]
    depth = width // n
    share, rest = shares(ff, n, m)
    tail = slice(n * share, n * share + 128)
    left = slice(n * share, ff)
    ffp = n * share + 128
    two = 2 * head_dim
    low = jnp.bfloat16
    f32 = jnp.float32
    mate = {"pipe": 1 - side}
    later = []
    used = [0, 0]

    def take(sends, recvs):
        at = tuple(used)
        used[0] += sends
        used[1] += recvs
        return at

    ctx_peers = [lax.rem(c + d, n) for d in range(1, n)]
    wa_peers = [lax.rem(w + d, m) for d in range(1, m)]

    greet(
        [{"ctx": peer} for peer in ctx_peers]
        + [{"wa": peer} for peer in wa_peers]
        + [{"pipe": 1 - side, "ctx": peer} for peer in [c] + ctx_peers]
    )

    def arrive(ref, sem):
        remote(ref, ref, sem, sem, mate).wait_recv()

    def exchange(axis, src, dst, times=1):
        me, count, peers = (c, n, ctx_peers) if axis == "ctx" else (w, m, wa_peers)
        s0, r0 = take(times * (count - 1), times * count)

        def copy(d, peer, t):
            return remote(
                src(peer, t), dst(me, t), ssem.at[s0 + t * (count - 1) + d], rsem.at[r0 + t * count + me], {axis: peer}
            )

        def start(t=0):
            for d, peer in enumerate(peers):
                copy(d, peer, t).start()

        def got(t=0):
            for peer in peers:
                arrive(dst(peer, t), rsem.at[r0 + t * count + peer])

        def drain():
            def one(t, _):
                for d, peer in enumerate(peers):
                    copy(d, peer, t).wait_send()
                return 0

            if times == 1:
                one(0, 0)
            else:
                lax.fori_loop(0, times, one, 0)

        later.append(drain)
        return start, got

    def single(cond_send, src, dst, peer, cond_recvs, slot):
        s0, r0 = take(1, max(n, m))

        def copy():
            return remote(src, dst(slot), ssem.at[s0], rsem.at[r0 + slot], peer)

        def start():
            pl.when(cond_send)(lambda: copy().start())

        def got():
            for cond, p in cond_recvs:
                pl.when(cond)(functools.partial(arrive, dst(p), rsem.at[r0 + p]))

        later.append(lambda: pl.when(cond_send)(lambda: copy().wait_send()))
        return start, got

    beside = w + 1 - 2 * lax.rem(w, 2)
    above = lax.rem(w + 2, m)
    across = lax.rem(beside + 2, m)

    def plane(whole, half, times):
        s0, r0 = take(4 * times, 4 * times)

        def copy(t, i):
            ref = (whole(t, w), whole(t, w), half(t, beside, 0), half(t, above, 1))[i]
            peer = (beside, above, above, beside)[i]
            return remote(ref, ref, ssem.at[s0 + 4 * t + i], rsem.at[r0 + 4 * t + i], {"wa": peer})

        def start(t):
            copy(t, 0).start()
            copy(t, 1).start()

        def pump(t):
            arrive(whole(t, beside), rsem.at[r0 + 4 * t])
            copy(t, 2).start()
            arrive(whole(t, above), rsem.at[r0 + 4 * t + 1])
            copy(t, 3).start()

        def finish(t):
            arrive(half(t, across, 0), rsem.at[r0 + 4 * t + 2])
            arrive(half(t, across, 1), rsem.at[r0 + 4 * t + 3])

        def drain():
            def one(t, _):
                for i in range(4):
                    copy(t, i).wait_send()
                return 0

            lax.fori_loop(0, times, one, 0)

        later.append(drain)
        return start, finish, pump

    def crows(at):
        return pl.ds(pl.multiple_of(at * depth, 16), depth)

    def chunks(at):
        return pl.ds(pl.multiple_of(at * chunk, 16), chunk)

    def lanes(at):
        return pl.ds(pl.multiple_of(at * share, 128), share)

    def piece(b, at):
        return pl.ds(pl.multiple_of(b * rows + at * sub, 16), sub)

    def batch(b):
        return slice(b * rows, (b + 1) * rows)

    diagonal = c == w

    at_z = exchange("ctx", lambda p, t: pack.at[p, t], lambda me, t: w_in.at[w, t, me], slots)
    at_p = plane(lambda t, at: w_in.at[at, t], lambda t, at, i: w_in.at[at, t, i * (n // 2) : (i + 1) * (n // 2)], slots)
    x_z = exchange("ctx", lambda p, t: inp.at[chunks(w), :], lambda me, t: xin.at[me])
    x_p = exchange("wa", lambda p, t: xin.at[p], lambda me, t: xx.at[0, chunks(me), :])
    hid_p = exchange("wa", lambda p, t: hidden, lambda me, t: hid_all.at[me])
    ml_z = exchange("ctx", lambda p, t: mlp.at[:, :, lanes(p)], lambda me, t: mt.at[:, crows(me), lanes(w)])
    ml_p = plane(
        lambda t, at: mt.at[t, :, lanes(at)],
        lambda t, at, i: mt.at[t, i * (width // 2) : (i + 1) * (width // 2), lanes(at)],
        2,
    )
    mh_z = single(
        jnp.logical_not(diagonal), mtl, lambda at: tt.at[crows(at), :], {"ctx": w},
        [(diagonal, p) for p in ctx_peers], c,
    )
    mh_s, mh_r = take(m - 1, 1)

    def mh_copy(d, peer):
        return remote(tt, tt, ssem.at[mh_s + d], rsem.at[mh_r], {"wa": peer})

    own_pack = pltpu.make_async_copy(pack.at[c], w_in.at[w, :, c], loc.at[0])
    own_mlp = pltpu.make_async_copy(mlp.at[:, :, lanes(c)], mt.at[:, crows(c), lanes(w)], loc.at[1])
    own_x = pltpu.make_async_copy(inp.at[chunks(w), :], xin.at[c], loc.at[2])
    own_half = pltpu.make_async_copy(mtl, tt.at[crows(c), :], loc.at[3])

    mtl[...] = jnp.zeros_like(mtl)
    mtl[:, :rest] = mlp[0, :, left]
    mtl[:, 64 : 64 + rest] = mlp[1, :, left]
    own_pack.start()
    own_mlp.start()
    own_x.start()
    pl.when(diagonal)(lambda: own_half.start())

    pl.when(side == 1)(lambda: pl.semaphore_wait(go, 1))
    def start_attn(t, _):
        at_z[0](t)
        return 0

    lax.fori_loop(0, slots, start_attn, 0)
    x_z[0]()
    hid_p[0]()
    ml_z[0]()
    mh_z[0]()
    stage[...] = jnp.zeros_like(stage)
    mix[...] = jnp.zeros_like(mix)
    sv[...] = jnp.zeros_like(sv)
    hv[...] = jnp.zeros_like(hv)
    own_pack.wait()

    def pass_attn(t, _):
        at_z[1](t)
        at_p[0](t)
        return 0

    lax.fori_loop(0, slots, pass_attn, 0)
    own_x.wait()
    x_z[1]()
    x_p[0]()
    xx[0, chunks(w), :] = xin[w]
    hid_p[1]()
    hid_all[w] = hidden[...]
    for p in range(m):
        hid[:, p * share : (p + 1) * share] = hid_all[p, :, lanes(c)]
    hid[:, tail] = jnp.zeros((1, 128), f32)
    hid[:, left] = hid_all[c, :, left]
    x_p[1]()
    x_ss, x_rs = take(micro * n, micro * n)
    x_at = side
    c_at = 1 - side

    def norm(stream):
        centre = jnp.mean(stream, axis=-1, keepdims=True)
        centred = stream - centre
        variance = jnp.mean(centred * centred, axis=-1, keepdims=True)
        inv_std = lax.rsqrt(variance + EPS)
        return centred * inv_std, inv_std

    def first_norm(b):
        for at, size in tiles_of(rows, 64):
            here = slice(b * rows + at, b * rows + at + size)
            normed, _ = norm(xx[x_at, here, :].astype(f32))
            a_s[here, :] = (normed * gain[0:1, :] + shift[0:1, :]).astype(low)

    upper = lax.broadcasted_iota(jnp.int32, (1, two), 1) >= head_dim
    pairs = exchange(
        "wa",
        lambda p, t: pair.at[w, lax.rem(t, slots), pl.ds(pl.multiple_of(t // slots * rows, 16), rows), :],
        lambda me, t: pair.at[me, lax.rem(t, slots), pl.ds(pl.multiple_of(t // slots * rows, 16), rows), :],
        slots * micro,
    )

    def lay(s):
        pl.when(s + 1 < slots)(lambda: at_p[2](s + 1))
        at_p[1](s)
        for j in range(n):
            for p in range(m):
                at = (j * m + p) * part
                stage[at : at + part, :] = w_in[p, s, j].astype(f32)[:part]
        wt[s] = stage[:width, :].astype(low)

    def project(s, b):
        made = dot(a_s[batch(b), :], wt[s], 1, 0)
        row = pltpu.roll(bias[jnp.minimum(s * n + c, heads - 1)], two // 2, 1)
        pair[w, s, batch(b), :] = (made[:, :two] + jnp.where(upper, 0.0, row)).astype(low)
        q_s[s, batch(b), :] = jnp.where(upper, made[:, two:] + row, 0.0).astype(low)
        pairs[0](b * slots + s)

    @pl.when(side == 0)
    def _():
        for b in range(micro):
            first_norm(b)
        at_p[2](0)

        def both(s, _):
            lay(s)
            for b in range(micro):
                project(s, b)
            return 0

        lax.fori_loop(0, slots, both, 0)

    @pl.when(side == 1)
    def _():
        at_p[2](0)

        def alone(s, _):
            lay(s)
            return 0

        lax.fori_loop(0, slots, alone, 0)

    own_mlp.wait()
    ml_z[1]()
    ml_p[0](0)
    ml_p[0](1)

    @pl.when(diagonal)
    def _():
        own_half.wait()

    mh_z[1]()

    @pl.when(diagonal)
    def _():
        for d, peer in enumerate(wa_peers):
            mh_copy(d, peer).start()

    def mh_drain():
        for d, peer in enumerate(wa_peers):
            mh_copy(d, peer).wait_send()

    later.append(lambda: pl.when(diagonal)(mh_drain))

    @pl.when(side == 0)
    def _():
        pl.semaphore_signal(go, inc=1, device_id=mate, device_id_type=MESH)

    @pl.when(side == 1)
    def _():
        for b in range(micro):
            for p in range(n):
                arrive(xx.at[1, piece(b, p), :], rsem.at[x_rs + b * n + p])
            first_norm(b)

            def one(s, _):
                project(s, b)
                return 0

            lax.fori_loop(0, slots, one, 0)

    block = rows // 2
    step = lax.broadcasted_iota(jnp.int32, (rows, 1), 0)
    qpos = jnp.where(step < block, table[0, w] * block + step, table[1, w] * block + step - block)
    along = lax.broadcasted_iota(jnp.int32, (1, m * rows), 1)
    kpos = along
    for i in range(2 * m):
        inside = (along >= i * block) & (along < (i + 1) * block)
        kpos = jnp.where(inside, table[i % 2, i // 2] * block + along - i * block, kpos)

    def attend(s, b):
        pairs[1](b * slots + s)
        kv = pair[:, s, batch(b), :].reshape(m * rows, two)
        scores = jnp.where(kpos <= qpos, dot(q_s[s, batch(b), :], kv, 1, 1) * scale, -jnp.inf)
        top = jnp.max(scores, axis=-1, keepdims=True)
        raised = jnp.exp(scores - top)
        weight = raised / jnp.sum(raised, axis=-1, keepdims=True)
        prob[s * micro + b] = weight
        mixed = dot(weight.astype(low), kv, 1, 0)
        mix[s, batch(b), two:] = jnp.where(upper, 0.0, mixed).astype(low)

    def summing(part_s, got_s):
        start, got = exchange(
            "ctx", lambda p, t: part_s.at[piece(t, p), :], lambda me, t: got_s.at[me, t], micro
        )

        def finish(b):
            value = part_s[piece(b, c), :].astype(f32)
            got(b)
            for p in ctx_peers:
                value = value + got_s[p, b].astype(f32)
            return value

        return start, finish, later[-1]

    def sharing(ref):
        return exchange("ctx", lambda p, t: ref.at[piece(t, c), :], lambda me, t: ref.at[piece(t, me), :], micro)

    sum1 = summing(p1, r1)
    for b in range(micro):

        def attend_all(s, _):
            attend(s, b)
            return 0

        lax.fori_loop(0, slots, attend_all, 0)
        for at, size in tiles_of(width):
            value = dot(mix[0, batch(b), two:], wt[0, at : at + size, two:], 1, 1)
            for s in range(1, slots):
                value = value + dot(mix[s, batch(b), two:], wt[s, at : at + size, two:], 1, 1)
            p1[batch(b), at : at + size] = value.astype(low)
        sum1[0](b)
    ml_p[2](0)
    fi_ag = sharing(fi)
    for b in range(micro):
        value = sum1[1](b)
        value = xx[x_at, piece(b, c), :].astype(f32) + value + shift[1:2, :]
        h1[b] = value
        normed, _ = norm(value)
        fi[piece(b, c), :] = (normed * gain[1:2, :] + shift[2:3, :]).astype(low)
        fi_ag[0](b)

    ml_p[2](1)
    sum2 = summing(p2, r2)
    beyond = lax.broadcasted_iota(jnp.int32, (1, 128), 1) >= 64

    def down(b):
        for at, size in tiles_of(width):
            p2[batch(b), at : at + size] = dot(act[batch(b), :], mt[1, at : at + size, :], 1, 1).astype(low)
        sum2[0](b)

    for b in range(micro):
        if b == 0:
            ml_p[1](0)
            pl.when(jnp.logical_not(diagonal))(lambda: arrive(tt, rsem.at[mh_r]))
            for at, size in tiles_of(width, 64):
                value = tt[at : at + size, :].astype(f32)
                mt[0, at : at + size, tail] = jnp.where(beyond, 0.0, value).astype(low)
                mt[1, at : at + size, tail] = jnp.where(beyond, 0.0, pltpu.roll(value, 64, 1)).astype(low)
        fi_ag[1](b)
        for at, size in tiles_of(ffp):
            pre = dot(fi[batch(b), :], mt[0, :, at : at + size], 1, 0) + hid[:, at : at + size]
            square = pre * pre
            tangent = jnp.tanh(GELU_C * (pre + GELU_A * square * pre))
            act[batch(b), at : at + size] = (0.5 * pre * (1.0 + tangent)).astype(low)
            slope[batch(b), at : at + size] = 0.5 * (1.0 + tangent) + 0.5 * pre * (
                1.0 - tangent * tangent
            ) * GELU_C * (1.0 + 3.0 * GELU_A * square)
        if b == 0:
            ml_p[1](1)
        pl.when(side == 0)(functools.partial(down, b))

    o_ss, o_rs = take(micro * (m - 1), micro * m)
    back = exchange("ctx", lambda p, t: ost.at[p], lambda me, t: ob.at[:, me])
    back_drain = later.pop()

    def cross(snd, other, b):
        return [
            remote(
                snd.at[b], xx.at[1, piece(b, c), :], ssem.at[x_ss + b * n + d], rsem.at[x_rs + b * n + c],
                {"pipe": other, "ctx": peer},
            )
            for d, peer in enumerate([c] + ctx_peers)
        ]

    def spread(snd, b):
        return [
            remote(
                snd.at[b], ost.at[w, b], ssem.at[o_ss + b * (m - 1) + d], rsem.at[o_rs + b * m + w], {"wa": peer}
            )
            for d, peer in enumerate(wa_peers)
        ]

    def hand_on(snd, at, b):
        @pl.when(side == at)
        def _():
            for copy in cross(snd, 1 - at, b):
                copy.start()

        @pl.when(side == 1 - at)
        def _():
            for copy in spread(snd, b):
                copy.start()
            ost[w, b] = snd[b]

    def spread_on():
        for b in range(micro):
            for p in wa_peers:
                arrive(ost.at[p, b], rsem.at[o_rs + b * m + p])
        back[0]()
        ob[:, c] = ost[c]

    def layer_done(b):
        value = sum2[1](b)
        snd1[b] = (h1[b] + value + shift[3:4, :]).astype(low)
        hand_on(snd1, 0, b)

    @pl.when(side == 0)
    def _():
        for b in range(micro):
            layer_done(b)

    later.remove(sum1[2])
    sum1[2]()
    def column(at, x):
        sv[at : at + 1, :] = sv[at : at + 1, :] + jnp.sum(x, axis=0, keepdims=True)

    def norm_back(d_out, normed, inv_std, row):
        lifted = d_out * gain[row : row + 1, :]
        first = jnp.mean(lifted, axis=-1, keepdims=True)
        second = jnp.mean(lifted * normed, axis=-1, keepdims=True)
        return inv_std * (lifted - first - normed * second)

    sum3 = summing(p1, r3)
    for b in range(micro):

        @pl.when(side == 0)
        def _():
            for p in range(n):
                arrive(xx.at[1, piece(b, p), :], rsem.at[x_rs + b * n + p])

        for at, size in tiles_of(ffp):
            d_pre = dot(xx[c_at, batch(b), :], mt[1, :, at : at + size], 1, 0) * slope[batch(b), at : at + size]
            over = slice(at, min(at + size, ff))
            sv[6:7, over] = sv[6:7, over] + jnp.sum(d_pre, axis=0, keepdims=True)[:, : over.stop - at]
            dpre[batch(b), at : at + size] = d_pre.astype(low)
        for at, size in tiles_of(width):
            p1[batch(b), at : at + size] = dot(dpre[batch(b), :], mt[0, at : at + size, :], 1, 1).astype(low)
        sum3[0](b)
    gm_p = exchange("wa", lambda p, t: gm.at[t, :, lanes(p)], lambda me, t: rgm.at[me, t], 2)
    for at, size in tiles_of(width):
        gm[1, at : at + size, :] = dot(xx[c_at, :, at : at + size], act[...], 0, 0).astype(low)
    gm_p[0](1)
    for at, size in tiles_of(width):
        gm[0, at : at + size, :] = dot(fi[:, at : at + size], dpre[...], 0, 0).astype(low)
    dh_ag = sharing(dh)
    for b in range(micro):
        value = sum3[1](b)
        normed, inv_std = norm(h1[b])
        cot = xx[c_at, piece(b, c), :].astype(f32)
        column(2, value)
        column(5, value * normed)
        column(3, cot)
        value = cot + norm_back(value, normed, inv_std, 1)
        dh1[b] = value
        column(1, value)
        dh[piece(b, c), :] = value.astype(low)
        dh_ag[0](b)

    dpairs = exchange(
        "wa",
        lambda p, t: dpair.at[p, lax.rem(t, slots), pl.ds(pl.multiple_of(t // slots * rows, 16), rows), :],
        lambda me, t: rpair.at[me, lax.rem(t, slots), pl.ds(pl.multiple_of(t // slots * rows, 16), rows), :],
        slots * micro,
    )

    def attend_back(s, b):
        d_mixed = dot(dh[batch(b), :], wt[s, :, two:], 1, 0)
        d_mixed = jnp.where(upper, 0.0, d_mixed).astype(low)
        kv = pair[:, s, batch(b), :].reshape(m * rows, two)
        weight = prob[s * micro + b]
        d_probs = dot(d_mixed, kv, 1, 1)
        delta = jnp.sum(weight * d_probs, axis=-1, keepdims=True)
        d_scores = (weight * (d_probs - delta) * scale).astype(low)
        d_query = jnp.where(upper, dot(d_scores, kv, 1, 0), 0.0)
        hv[s] = hv[s] + jnp.sum(d_query, axis=0, keepdims=True)
        dproj[s, batch(b), two:] = d_query.astype(low)
        d_kv = dot(d_scores, q_s[s, batch(b), :], 0, 0) + dot(weight.astype(low), d_mixed, 0, 0)
        dpair[:, s, batch(b), :] = d_kv.astype(low).reshape(m, rows, two)
        dpairs[0](b * slots + s)

    for b in range(micro):
        dh_ag[1](b)

        def attend_back_all(s, _):
            attend_back(s, b)
            return 0

        lax.fori_loop(0, slots, attend_back_all, 0)
    for at, size in tiles_of(width, 64):
        value = pltpu.roll(gm[1, at : at + size, tail].astype(f32), 64, 1)
        gt[at : at + size, :] = jnp.where(beyond, value, gm[0, at : at + size, tail].astype(f32)).astype(low)
    gh_p = single(
        jnp.logical_not(diagonal), gt, lambda at: rgh.at[at], {"wa": c},
        [(diagonal, p) for p in wa_peers], w,
    )
    gm_p[0](0)
    gh_p[0]()

    @pl.when(side == 1)
    def _():
        for b in range(micro):
            down(b)

    later.remove(sum3[2])
    sum3[2]()
    sum4 = summing(p1, r4)
    for b in range(micro):

        def collect(s, _):
            value = dpair[w, s, batch(b), :].astype(f32)
            dpairs[1](b * slots + s)
            for p in wa_peers:
                value = value + rpair[p, s, batch(b), :].astype(f32)
            dproj[s, batch(b), :two] = value.astype(low)
            hv[s] = hv[s] + jnp.where(upper, 0.0, jnp.sum(value, axis=0, keepdims=True))
            return 0

        lax.fori_loop(0, slots, collect, 0)
        for at, size in tiles_of(width):
            value = dot(dproj[0, batch(b), :], wt[0, at : at + size, :], 1, 1)
            for s in range(1, slots):
                value = value + dot(dproj[s, batch(b), :], wt[s, at : at + size, :], 1, 1)
            p1[batch(b), at : at + size] = value.astype(low)
        sum4[0](b)

    @pl.when(side == 1)
    def _():
        for b in range(micro):
            layer_done(b)

    at_drain = later.pop(0), later.pop(0)
    at_drain[0]()
    at_drain[1]()

    ga_p = exchange("wa", lambda p, t: w_in.at[p, t], lambda me, t: ra.at[me, t], slots)

    def attn_grad(s, _):
        for at, size in tiles_of(width):
            stage[at : at + size, :] = dot(a_s[:, at : at + size], dproj[s], 0, 0) + dot(
                dh[:, at : at + size], mix[s], 0, 0
            )
        for j in range(n):
            for p in range(m):
                at = (j * m + p) * part
                w_in[p, s, j] = stage[at : at + padded, :].astype(low)
        ga_p[0](s)
        return 0

    lax.fori_loop(0, slots, attn_grad, 0)
    for b in range(micro):
        value = sum4[1](b)
        normed, inv_std = norm(xx[x_at, piece(b, c), :].astype(f32))
        column(0, value)
        column(4, value * normed)
        snd2[b] = (dh1[b] + norm_back(value, normed, inv_std, 0)).astype(low)
        hand_on(snd2, 1, b)
    for s in range(slots):
        sv[8 + s : 9 + s, :two] = hv[s]
    svc[w] = sv[...]
    sv_p = exchange("wa", lambda p, t: sv, lambda me, t: svc.at[me])
    sv_p[0]()

    gm_z = exchange("ctx", lambda p, t: sm.at[t, crows(p), :], lambda me, t: zg.at[me, t], 2)
    for k in (1, 0):
        gm_p[1](k)

        def sum_mlp(i, _):
            at = pl.ds(pl.multiple_of(i * 64, 64), 64)
            value = gm[k, at, lanes(w)].astype(f32)
            for p in wa_peers:
                value = value + rgm[p, k, at, :].astype(f32)
            sm[k, at, :] = value.astype(low)
            return 0

        lax.fori_loop(0, width // 64, sum_mlp, 0)
        gm_z[0](k)
        zg[c, k] = sm[k, crows(c), :]
    gh_p[1]()
    gh_s, gh_r = take(n - 1, 1)

    def gh_copy(d, peer):
        return remote(smh.at[crows(peer), :], zh, ssem.at[gh_s + d], rsem.at[gh_r], {"ctx": peer})

    @pl.when(diagonal)
    def _():
        def sum_half(i, _):
            at = pl.ds(pl.multiple_of(i * 64, 64), 64)
            value = gt[at, :].astype(f32)
            for p in wa_peers:
                value = value + rgh[p, at, :].astype(f32)
            smh[at, :] = value.astype(low)
            return 0

        lax.fori_loop(0, width // 64, sum_half, 0)
        for d, peer in enumerate(ctx_peers):
            gh_copy(d, peer).start()
        value = smh[crows(c), :].astype(f32)
        g_mlp[0, :, left] = value[:, :rest]
        g_mlp[1, :, left] = value[:, 64 : 64 + rest]

    spread_on()
    sv_p[1]()
    value = svc[0]
    for p in range(1, m):
        value = value + svc[p]
    vec_own[...] = value
    vec_all[c] = value
    sv_z = exchange("ctx", lambda p, t: vec_own, lambda me, t: vec_all.at[me])
    sv_z[0]()
    ga_z = exchange("ctx", lambda p, t: s2.at[p, t], lambda me, t: za.at[me, t], slots)

    def sum_attn(s, _):
        ga_p[1](s)
        for j in range(n):
            value = w_in[w, s, j].astype(f32)
            for p in wa_peers:
                value = value + ra[p, s, j].astype(f32)
            s2[j, s] = value.astype(low)
        ga_z[0](s)
        za[c, s] = s2[c, s]
        return 0

    lax.fori_loop(0, slots, sum_attn, 0)

    for k in (1, 0):
        gm_z[1](k)
        for p in range(n):
            g_mlp[k, :, p * share : (p + 1) * share] = zg[p, k].astype(f32)

    @pl.when(jnp.logical_not(diagonal))
    def _():
        arrive(zh, rsem.at[gh_r])
        value = zh[...].astype(f32)
        g_mlp[0, :, left] = value[:, :rest]
        g_mlp[1, :, left] = value[:, 64 : 64 + rest]

    back[1]()
    for b in range(micro):
        for p in range(n):
            at = b * rows + p * sub
            out[at : at + sub, :] = ob[b, p].astype(f32)
    sv_z[1]()
    value = vec_all[0]
    for p in range(1, n):
        value = value + vec_all[p]
    g_feature[...] = value[0:4, :]
    g_gain[...] = value[4:6, :]
    for p in range(n):
        g_hidden[:, p * share : (p + 1) * share] = vec_all[p, 6:7, lanes(w)]
        for s in range(slots):
            h = s * n + p
            if h < heads:
                g_heads[h] = pltpu.roll(vec_all[p, 8 + s : 9 + s, :two], two // 2, 1)
    g_hidden[:, left] = vec_all[w, 6:7, left]
    for s in range(slots):
        ga_z[1](s)
        for p in range(n):
            h = s * n + p
            if h < heads:
                first = za[p, s, :, :two].astype(f32)[:part]
                second = za[p, s, :, two:].astype(f32)[:part]
                g_qkv[h, :, :two] = jnp.where(upper, first, pltpu.roll(second, two // 2, 1))
                g_qkv[h, :, two:] = first[:, : two // 2]
                g_out[h] = second[:, : two // 2]

    for drain in later:
        drain()
    back_drain()

    @pl.when(diagonal)
    def _():
        for d, peer in enumerate(ctx_peers):
            gh_copy(d, peer).wait_send()

    for snd, at in ((snd1, 0), (snd2, 1)):

        for b in range(micro):

            @pl.when(side == at)
            def _():
                for copy in cross(snd, 1 - at, b):
                    copy.wait_send()

            @pl.when(side == 1 - at)
            def _():
                for copy in spread(snd, b):
                    copy.wait_send()


def whole_step(
    section_inputs, qkv_weight, out_weight, head_bias, mlp_weight, hidden_bias, feature_bias, ln_gain, block_table
):
    n = lax.axis_size("ctx")
    m = lax.axis_size("wa")
    micro, rows, width = section_inputs.shape[1:]
    heads, part = qkv_weight.shape[1:3]
    head_dim = out_weight.shape[3]
    ff = mlp_weight.shape[3]
    depth = mlp_weight.shape[2]
    slots = (heads + n - 1) // n
    pad = slots * n - heads
    padded = part + (-part % 16)
    total = micro * rows
    chunk = total // n
    share, rest = shares(ff, n, m)
    low = jnp.bfloat16
    f32 = jnp.float32
    two = 2 * head_dim
    scale = head_dim ** (-0.5)

    query, key, value = (qkv_weight[0, :, :, i * head_dim : (i + 1) * head_dim] for i in range(3))
    pack = jnp.concatenate([value, key, out_weight[0], query], axis=-1)
    pack = jnp.pad(pack, ((0, pad), (0, padded - part), (0, 0)))
    pack = pack.reshape(slots, n, padded, 2 * two).transpose(1, 0, 2, 3)
    def v(shape, kind=low):
        return pltpu.VMEM(shape, kind)

    sub = rows // n
    ffp = n * share + 128
    wide = (total, width)
    parts = (slots, padded, 2 * two)
    scratch = (
        [v((m, slots, n) + parts[1:]), v((width + 16, 2 * two), f32), v((slots, width, 2 * two)), v((2, width, ffp)), v((depth, 128)), v((width, 128))]
        + [v((n, chunk, width)), v((2,) + wide), v((m, 1, ff), f32), v((1, ffp), f32), v(wide)]
        + [v((slots, total, two)), v((m, slots, total, two)), v((slots * micro, rows, m * rows), f32)]
        + [v((slots, total, 2 * two))]
        + [v(wide)] * 2
        + [v((n, micro, sub, width))] * 4
        + [v(wide), v(wide), v((m, micro, sub, width)), v((micro, n, sub, width))]
        + [v((total, ffp)), v((total, ffp), f32), v((total, ffp))]
        + [v((micro, sub, width), f32), v((micro, sub, width), f32)]
        + [v((m, slots, total, two))] * 2
        + [v((slots, total, 2 * two)), v((2, width, ffp)), v((width, 128)), v((m, 2, width, share)), v((m, width, 128))]
        + [v((2, width, share)), v((width, 128)), v((n, 2, depth, share)), v((depth, 128))]
        + [v((m, slots, n) + parts[1:]), v((n,) + parts), v((n,) + parts)]
        + [v((16, width), f32), v((slots, 1, two), f32), v((m, 16, width), f32), v((16, width), f32)]
        + [v((n, 16, width), f32)]
        + [v((micro, sub, width))] * 2
        + [dma(256), dma(300), dma(4), pltpu.SemaphoreType.REGULAR]
    )
    shapes = [
        jax.ShapeDtypeStruct(shape, f32)
        for shape in (
            wide,
            (heads, part, 3 * head_dim),
            (heads, part, head_dim),
            (heads, 1, two),
            (2, depth, ff),
            (1, ff),
            (4, width),
            (2, width),
        )
    ]
    sizes = (rows, width, ff, slots, micro, head_dim, part, padded)
    out, g_qkv, g_out, g_heads, g_mlp, g_hidden, g_feature, g_gain = pl.pallas_call(
        functools.partial(step_kernel, n, m, sizes, scale),
        out_shape=shapes,
        in_specs=[VM] * 7 + [pl.BlockSpec(memory_space=pltpu.SMEM)],
        out_specs=[VM] * len(shapes),
        scratch_shapes=scratch,
        compiler_params=pltpu.CompilerParams(
            collective_id=IDS["step"], has_side_effects=True, vmem_limit_bytes=61 * 1024 * 1024
        ),
        name="step",
    )(
        section_inputs.reshape(total, width),
        pack,
        mlp_weight[0],
        head_bias.reshape(heads, 1, two),
        hidden_bias,
        feature_bias[0],
        ln_gain[0],
        block_table.T,
    )
    return (
        out.reshape(1, micro, rows, width),
        g_qkv[None],
        g_out[None],
        g_heads.reshape(1, heads, two),
        g_mlp[None],
        g_hidden,
        g_feature[None],
        g_gain[None],
    )


def fits(mesh, rows, micro, width, ff):
    n, m = mesh.shape["ctx"], mesh.shape["wa"]
    depth, chunk = width // n, micro * rows // n
    share, rest = shares(ff, n, m)
    even = depth % 16 == 0 and chunk % 16 == 0 and rows // n % 16 == 0 and width % 64 == 0
    return n == m == 4 and even and width % 32 == 0 and ff <= width and 0 < rest <= 64 and share > 0


def either(mesh, *args):
    micro, rows, width = args[0].shape[1:]
    if fits(mesh, rows, micro, width, args[4].shape[3]):
        return whole_step(*args)
    return per_device(*args)


def solution(mesh):
    return jax.shard_map(
        functools.partial(either, mesh),
        mesh=mesh,
        in_specs=(
            P("pipe", None, "ctx", None),
            P("pipe", None, ("ctx", "wa"), None),
            P("pipe", None, ("ctx", "wa"), None),
            P("pipe", None, None),
            P("pipe", None, "ctx", "wa"),
            P("pipe", "wa"),
            P("pipe", None, None),
            P("pipe", None, None),
            P(),
        ),
        out_specs=(
            P("pipe", None, "ctx", None),
            P("pipe", None, ("ctx", "wa"), None),
            P("pipe", None, ("ctx", "wa"), None),
            P("pipe", None, None),
            P("pipe", None, "ctx", "wa"),
            P("pipe", "wa"),
            P("pipe", None, None),
            P("pipe", None, None),
        ),
        check_vma=False,
    )
```

```python
import functools

import jax
import jax.numpy as jnp
from jax import lax
from jax.experimental import pallas as pl
from jax.experimental.pallas import tpu as pltpu
from jax.sharding import PartitionSpec as P

EPS = 1e-05
GELU_C = 0.7978845608028654
GELU_A = 0.044715
KERNELS = True
MESH = pl.DeviceIdType.MESH
VM = pl.BlockSpec(memory_space=pltpu.VMEM)
IDS = {"sum_wa": 1, "swap_wa": 2, "swap_ctx": 3, "line_attn": 4, "line_mlp": 5, "line_pair": 6, "swap_mlp": 7,
       "swap_attn": 8, "all_small": 9, "all_heads": 10, "swap_grad": 11, "step": 12}


def remote(src, dst, send, recv, peer):
    return pltpu.make_async_remote_copy(
        src_ref=src, dst_ref=dst, send_sem=send, recv_sem=recv, device_id=peer, device_id_type=MESH
    )


def greet(peers):
    barrier = pltpu.get_barrier_semaphore()
    for peer in peers:
        pl.semaphore_signal(barrier, inc=1, device_id=peer, device_id_type=MESH)
    pl.semaphore_wait(barrier, len(peers))


def sum_kernel(axis, n, x_ref, o_ref, got, send_a, recv_a, send_b, recv_b):
    me = lax.axis_index(axis)
    peers = [{axis: lax.rem(me + d, n)} for d in range(1, n)]
    greet(peers)
    first = [
        remote(x_ref.at[lax.rem(me + d, n)], got.at[d - 1], send_a.at[d - 1], recv_a.at[d - 1], peers[d - 1])
        for d in range(1, n)
    ]
    for copy in first:
        copy.start()
    total = x_ref[me].astype(jnp.float32)
    for d, copy in enumerate(first):
        copy.wait_recv()
        total = total + got[d].astype(jnp.float32)
    o_ref[me] = total.astype(o_ref.dtype)
    second = [
        remote(o_ref.at[me], o_ref.at[me], send_b.at[d - 1], recv_b.at[d - 1], peers[d - 1]) for d in range(1, n)
    ]
    for copy in second:
        copy.start()
    for copy in first:
        copy.wait_send()
    for copy in second:
        copy.wait()


def swap_kernel(axis, n, x_ref, o_ref, send, recv, local):
    me = lax.axis_index(axis)
    peers = [{axis: lax.rem(me + d, n)} for d in range(1, n)]
    greet(peers)
    copies = [
        remote(x_ref.at[lax.rem(me + d, n)], o_ref.at[me], send.at[d - 1], recv.at[d - 1], peers[d - 1])
        for d in range(1, n)
    ]
    for copy in copies:
        copy.start()
    own = pltpu.make_async_copy(x_ref.at[me], o_ref.at[me], local)
    own.start()
    own.wait()
    for copy in copies:
        copy.wait()


def all_kernel(axis, n, x_ref, o_ref, send, recv, local):
    me = lax.axis_index(axis)
    peers = [{axis: lax.rem(me + d, n)} for d in range(1, n)]
    greet(peers)
    copies = [
        remote(x_ref, o_ref.at[me], send.at[d - 1], recv.at[d - 1], peers[d - 1]) for d in range(1, n)
    ]
    for copy in copies:
        copy.start()
    own = pltpu.make_async_copy(x_ref, o_ref.at[me], local)
    own.start()
    own.wait()
    for copy in copies:
        copy.wait()


def line_kernel(n, both, x_ref, o_ref, send_r, recv_r, send_l, recv_l, send_p, recv_p, local):
    me = lax.axis_index("ctx")
    side = lax.axis_index("pipe")
    row = side if both else 0
    right, left, mate = {"ctx": me + 1}, {"ctx": me - 1}, {"pipe": 1 - side}
    barrier = pltpu.get_barrier_semaphore()
    not_last, not_first = me + 1 < n, me > 0

    @pl.when(not_last)
    def _():
        pl.semaphore_signal(barrier, inc=1, device_id=right, device_id_type=MESH)

    @pl.when(not_first)
    def _():
        pl.semaphore_signal(barrier, inc=1, device_id=left, device_id_type=MESH)

    if both:
        pl.semaphore_signal(barrier, inc=1, device_id=mate, device_id_type=MESH)
    extra = 1 if both else 0

    @pl.when(not_first & not_last)
    def _():
        pl.semaphore_wait(barrier, 2 + extra)

    @pl.when(jnp.logical_not(not_first & not_last))
    def _():
        pl.semaphore_wait(barrier, 1 + extra)

    own = pltpu.make_async_copy(x_ref, o_ref.at[row, me], local)
    own.start()

    def block(at, fresh):
        return x_ref if fresh else o_ref.at[row, at]

    def to_right(s):
        return remote(block(me - s, s == 0), o_ref.at[row, me - s], send_r.at[s], recv_r.at[s], right)

    def to_left(s):
        return remote(block(me + s, s == 0), o_ref.at[row, me + s], send_l.at[s], recv_l.at[s], left)

    def to_mate(at, fresh):
        return remote(block(at, fresh), o_ref.at[row, at], send_p.at[at], recv_p.at[at], mate)

    def arrived(at, sem):
        return remote(o_ref.at[row, at], o_ref.at[row, at], send_r.at[0], sem, mate)

    for s in range(n):

        @pl.when(me - s >= 0)
        def _():
            if s > 0:
                arrived(me - s, recv_r.at[s - 1]).wait_recv()
            if s < n - 1:

                @pl.when(not_last)
                def _():
                    to_right(s).start()

            if both and s > 0:
                to_mate(me - s, False).start()

        @pl.when(me + s < n)
        def _():
            if s > 0:
                arrived(me + s, recv_l.at[s - 1]).wait_recv()
            if s < n - 1:

                @pl.when(not_first)
                def _():
                    to_left(s).start()

            if both:
                to_mate(me + s, s == 0).start()

    own.wait()
    for s in range(n - 1):

        @pl.when((me - s >= 0) & not_last)
        def _():
            to_right(s).wait_send()

        @pl.when((me + s < n) & not_first)
        def _():
            to_left(s).wait_send()

    if both:
        for at in range(n):
            to_mate(at, False).wait_send()
            remote(o_ref.at[1 - side, at], o_ref.at[1 - side, at], send_p.at[at], recv_p.at[at], mate).wait_recv()


def call(kernel, name, shape, scratch, x):
    return pl.pallas_call(
        kernel,
        out_shape=jax.ShapeDtypeStruct(shape, x.dtype),
        in_specs=[VM],
        out_specs=VM,
        scratch_shapes=scratch,
        compiler_params=pltpu.CompilerParams(
            collective_id=IDS[name], has_side_effects=True, vmem_limit_bytes=60 * 1024 * 1024
        ),
        name=name,
    )(x)


def dma(count):
    return pltpu.SemaphoreType.DMA((count,))


def summed(x):
    n = lax.axis_size("wa")
    low = x.astype(jnp.bfloat16)
    if not KERNELS:
        return lax.psum(low.astype(jnp.float32), "wa").astype(jnp.bfloat16).astype(jnp.float32)
    parts = low.reshape(n, low.shape[0] // n, low.shape[1])
    scratch = [pltpu.VMEM((n - 1,) + parts.shape[1:], jnp.bfloat16)] + [dma(n - 1)] * 4
    out = call(functools.partial(sum_kernel, "wa", n), "sum_wa", parts.shape, scratch, parts)
    return out.reshape(low.shape).astype(jnp.float32)


def swapped(x, axis, name):
    n = lax.axis_size(axis)
    if not KERNELS:
        return lax.all_to_all(x, axis, split_axis=0, concat_axis=0, tiled=True)
    scratch = [dma(n - 1)] * 2 + [pltpu.SemaphoreType.DMA]
    return call(functools.partial(swap_kernel, axis, n), name, x.shape, scratch, x)


def gathered(x, axis, name):
    n = lax.axis_size(axis)
    if not KERNELS:
        return lax.all_gather(x, axis)
    scratch = [dma(n - 1)] * 2 + [pltpu.SemaphoreType.DMA]
    return call(functools.partial(all_kernel, axis, n), name, (n,) + x.shape, scratch, x)


def lined(x, both, name):
    n = lax.axis_size("ctx")
    if not KERNELS:
        out = lax.all_gather(x, "ctx")
        return lax.all_gather(out, "pipe") if both else out[None]
    scratch = [dma(n - 1)] * 4 + [dma(n)] * 2 + [pltpu.SemaphoreType.DMA]
    return call(functools.partial(line_kernel, n, both), name, (2 if both else 1, n) + x.shape, scratch, x)


def dot(a, b, ca, cb):
    return lax.dot_general(a, b, (((ca,), (cb,)), ((), ())), preferred_element_type=jnp.float32)


def attend_kernel(scale, qpos, kpos, q_ref, kv_ref, mix_ref, total_ref):
    heads = q_ref.shape[0]
    allowed = kpos[...] <= qpos[...]
    for h in range(heads):
        kv = kv_ref[:, h].reshape(-1, kv_ref.shape[-1])
        scores = jnp.where(allowed, dot(q_ref[h], kv, 1, 1) * scale, -jnp.inf)
        top = jnp.max(scores, axis=-1, keepdims=True)
        total = top + jnp.log(jnp.sum(jnp.exp(scores - top), axis=-1, keepdims=True))
        probs = jnp.exp(scores - total).astype(jnp.bfloat16)
        mix_ref[h] = dot(probs, kv, 1, 0).astype(jnp.bfloat16)
        total_ref[h] = total


def attend_back_kernel(scale, qpos, kpos, q_ref, kv_ref, dm_ref, total_ref, dq_ref, dkv_ref):
    heads = q_ref.shape[0]
    allowed = kpos[...] <= qpos[...]
    for h in range(heads):
        kv = kv_ref[:, h].reshape(-1, kv_ref.shape[-1])
        scores = jnp.where(allowed, dot(q_ref[h], kv, 1, 1) * scale, -jnp.inf)
        probs = jnp.exp(scores - total_ref[h])
        d_probs = dot(dm_ref[h], kv, 1, 1)
        delta = jnp.sum(probs * d_probs, axis=-1, keepdims=True)
        d_scores = (probs * (d_probs - delta) * scale).astype(jnp.bfloat16)
        dq_ref[h] = dot(d_scores, kv, 1, 0)
        d_kv = dot(d_scores, q_ref[h], 0, 0) + dot(probs.astype(jnp.bfloat16), dm_ref[h], 0, 0)
        dkv_ref[:, h] = d_kv.astype(jnp.bfloat16).reshape(dkv_ref.shape[0], dkv_ref.shape[2], dkv_ref.shape[3])


def local_call(kernel, shapes, *args):
    return pl.pallas_call(
        kernel,
        out_shape=[jax.ShapeDtypeStruct(*s) for s in shapes],
        in_specs=[VM] * len(args),
        out_specs=[VM] * len(shapes),
        compiler_params=pltpu.CompilerParams(vmem_limit_bytes=48 * 1024 * 1024),
        interpret=not KERNELS,
    )(*args)

def norm_forward(stream, gain, offset):
    centre = jnp.mean(stream, axis=-1, keepdims=True)
    centred = stream - centre
    variance = jnp.mean(centred * centred, axis=-1, keepdims=True)
    inv_std = lax.rsqrt(variance + EPS)
    normed = centred * inv_std
    return (normed * gain + offset, normed, inv_std)


def norm_backward(grad_out, normed, inv_std, gain):
    grad_normed = grad_out * gain
    first_mean = jnp.mean(grad_normed, axis=-1, keepdims=True)
    second_mean = jnp.mean(grad_normed * normed, axis=-1, keepdims=True)
    return inv_std * (grad_normed - first_mean - normed * second_mean)


def gelu_value(hidden):
    tangent = jnp.tanh(GELU_C * (hidden + GELU_A * hidden * hidden * hidden))
    return 0.5 * hidden * (1.0 + tangent)


def gelu_slope(hidden):
    tangent = jnp.tanh(GELU_C * (hidden + GELU_A * hidden * hidden * hidden))
    return 0.5 * (1.0 + tangent) + 0.5 * hidden * (1.0 - tangent * tangent) * GELU_C * (
        1.0 + 3.0 * GELU_A * hidden * hidden
    )


def per_device(
    section_inputs,
    qkv_weight,
    out_weight,
    head_bias,
    mlp_weight,
    hidden_bias,
    feature_bias,
    ln_gain,
    block_table,
):
    ctx_count = lax.axis_size("ctx")
    shard_count = lax.axis_size("wa")
    side = lax.axis_index("pipe")
    ctx_index = lax.axis_index("ctx")
    shard_index = lax.axis_index("wa")
    rows = section_inputs.shape[2]
    width = section_inputs.shape[3]
    head_count = qkv_weight.shape[1]
    head_dim = out_weight.shape[3]
    part = qkv_weight.shape[2]
    slots = (head_count + shard_count - 1) // shard_count
    pad = slots * shard_count - head_count
    block_rows = rows // 2
    scale = head_dim ** (-0.5)
    swap = [(0, 1), (1, 0)]
    low = jnp.bfloat16

    own_blocks = lax.dynamic_index_in_dim(block_table, ctx_index, 0, keepdims=False)
    step = jnp.arange(block_rows, dtype=jnp.int32)
    query_pos = (own_blocks[:, None] * block_rows + step[None, :]).reshape(rows, 1)
    key_pos = (block_table.reshape(-1)[:, None] * block_rows + step[None, :]).reshape(1, rows * ctx_count)

    def mine(first, second):
        return jnp.where(side == 0, first, second)

    inputs = section_inputs[0]
    traded = lax.ppermute(mine(inputs[1], inputs[0]), "pipe", swap)
    layer_input = mine(inputs[0], traded)
    last_cot = mine(traded, inputs[1])

    packed = jnp.concatenate([qkv_weight[0], out_weight[0]], axis=-1)
    packed = jnp.pad(packed, ((0, pad), (0, 0), (0, 0)))
    packed = packed.reshape(slots, shard_count, part, 4 * head_dim).transpose(1, 0, 2, 3)
    attn_all = lined(swapped(packed, "wa", "swap_wa"), True, "line_attn")
    mlp_all = lined(mlp_weight[0], True, "line_mlp")

    sizes = [head_bias[0].size, hidden_bias[0].size, feature_bias[0].size]
    small = jnp.concatenate(
        [head_bias[0].reshape(-1), hidden_bias[0], feature_bias[0].reshape(-1), ln_gain[0].reshape(-1)]
    )
    small_mate = lax.ppermute(small, "pipe", swap)

    def params_of(layer):
        weight = attn_all[layer].transpose(2, 0, 1, 3, 4).reshape(slots, width, 4 * head_dim)
        up = mlp_all[layer][:, 0].reshape(width, -1)
        down = mlp_all[layer][:, 1].reshape(width, -1)
        flat = jnp.where(side == layer, small, small_mate)
        heads, hidden, feature, gains = jnp.split(flat, [sizes[0], sizes[0] + sizes[1], sum(sizes)])
        heads = jnp.pad(heads.reshape(head_count, 2 * head_dim), ((0, pad), (0, 0)))
        heads = heads.reshape(slots, shard_count, 2 * head_dim)
        heads = lax.dynamic_index_in_dim(heads, shard_index, 1, keepdims=False)
        return (
            weight[:, :, : 3 * head_dim],
            weight[:, :, 3 * head_dim :],
            heads,
            up,
            down,
            hidden,
            feature.reshape(4, width),
            gains.reshape(2, width),
        )

    def widened(x, before):
        zero = jnp.zeros_like(x)
        return jnp.concatenate([zero, x] if before else [x, zero], axis=-1)

    def forward(layer_in, params):
        w_qkv, w_out, bias, w_up, w_down, bias_hidden, shifts, gains = params
        stream = layer_in.astype(jnp.float32)
        normed_in, normed_one, inv_one = norm_forward(stream, gains[0], shifts[0])
        attn_in = normed_in.astype(low)
        projected = jnp.einsum("td,hde->hte", attn_in, w_qkv, preferred_element_type=jnp.float32)
        queries = widened((projected[:, :, :head_dim] + bias[:, None, :head_dim]).astype(low), False)
        key_rows = projected[:, :, head_dim : 2 * head_dim].astype(low)
        values = (projected[:, :, 2 * head_dim :] + bias[:, None, head_dim:]).astype(low)
        pairs = lined(jnp.concatenate([key_rows, values], axis=-1), False, "line_pair")[0]
        mixed, log_total = local_call(
            functools.partial(attend_kernel, scale),
            [((slots, rows, 2 * head_dim), low), ((slots, rows, 1), jnp.float32)],
            query_pos,
            key_pos,
            queries,
            pairs,
        )
        mixed = mixed[:, :, head_dim:]
        attn_out = summed(jnp.einsum("hte,hde->td", mixed, w_out, preferred_element_type=jnp.float32))
        first_sum = stream + attn_out + shifts[1]
        normed_ffn, normed_two, inv_two = norm_forward(first_sum, gains[1], shifts[2])
        ffn_in = normed_ffn.astype(low)
        pre = jnp.dot(ffn_in, w_up, preferred_element_type=jnp.float32) + bias_hidden
        act = gelu_value(pre).astype(low)
        layer_out = (
            first_sum
            + summed(jnp.einsum("tf,df->td", act, w_down, preferred_element_type=jnp.float32))
            + shifts[3]
        )
        return layer_out, (
            normed_one, inv_one, attn_in, queries, pairs, mixed, log_total, normed_two, inv_two, ffn_in, pre, act,
        )

    def backward(cot, saved, params):
        w_qkv, w_out, bias, w_up, w_down, bias_hidden, shifts, gains = params
        normed_one, inv_one, attn_in, queries, pairs, mixed, log_total, normed_two, inv_two, ffn_in, pre, act = saved
        cotangent = cot.astype(jnp.float32)
        grad_down = jnp.einsum("ti,tf->if", cot, act, preferred_element_type=jnp.float32)
        d_act = jnp.einsum("ti,if->tf", cot, w_down, preferred_element_type=jnp.float32)
        d_pre = d_act * gelu_slope(pre)
        grad_hidden = jnp.sum(d_pre, axis=0)
        d_pre_low = d_pre.astype(low)
        grad_up = jnp.einsum("td,tf->df", ffn_in, d_pre_low, preferred_element_type=jnp.float32)
        d_ffn = summed(jnp.einsum("tf,df->td", d_pre_low, w_up, preferred_element_type=jnp.float32))
        d_first = cotangent + norm_backward(d_ffn, normed_two, inv_two, gains[1])
        d_first_low = d_first.astype(low)
        grad_out = jnp.einsum("ti,hte->hie", d_first_low, mixed, preferred_element_type=jnp.float32)
        d_mixed = jnp.einsum("ti,hie->hte", d_first_low, w_out, preferred_element_type=jnp.float32)
        d_query, pair_terms = local_call(
            functools.partial(attend_back_kernel, scale),
            [((slots, rows, 2 * head_dim), jnp.float32), (pairs.shape, low)],
            query_pos,
            key_pos,
            queries,
            pairs,
            widened(d_mixed.astype(low), True),
            log_total,
        )
        d_query = d_query[:, :, :head_dim]
        d_pair = swapped(pair_terms, "ctx", "swap_ctx").astype(jnp.float32).sum(axis=0)
        grad_heads = jnp.concatenate(
            [jnp.sum(d_query, axis=1), jnp.sum(d_pair[:, :, head_dim:], axis=1)], axis=-1
        )
        d_proj = jnp.concatenate([d_query.astype(low), d_pair.astype(low)], axis=-1)
        grad_qkv = jnp.einsum("td,hte->hde", attn_in, d_proj, preferred_element_type=jnp.float32)
        d_attn = summed(jnp.einsum("hte,hde->td", d_proj, w_qkv, preferred_element_type=jnp.float32))
        d_input = d_first + norm_backward(d_attn, normed_one, inv_one, gains[0])
        vectors = [
            jnp.sum(d_attn, axis=0),
            jnp.sum(d_first, axis=0),
            jnp.sum(d_ffn, axis=0),
            jnp.sum(cotangent, axis=0),
            jnp.sum(d_attn * normed_one, axis=0),
            jnp.sum(d_ffn * normed_two, axis=0),
            grad_hidden,
            grad_heads.reshape(-1),
        ]
        attn_grad = jnp.concatenate([grad_qkv, grad_out], axis=-1).astype(low)
        mlp_grad = jnp.stack([grad_up, grad_down]).astype(low)
        return d_input, attn_grad, mlp_grad, jnp.concatenate(vectors)

    params = [params_of(0), params_of(1)]
    first_out, first_saved = forward(layer_input, params[0])
    last_out, last_saved = forward(first_out.astype(low), params[1])
    back, attn_one, mlp_one, vec_one = backward(last_cot, last_saved, params[1])
    d_input, attn_zero, mlp_zero, vec_zero = backward(back.astype(low), first_saved, params[0])

    def over_pipe(zero, one):
        kept = mine(zero, one)
        got = lax.ppermute(mine(one, zero), "pipe", swap)
        return kept.astype(jnp.float32) + got.astype(jnp.float32)

    mlp_sum = over_pipe(mlp_zero, mlp_one).astype(low)
    mlp_sum = mlp_sum.reshape(2, ctx_count, width // ctx_count, -1).transpose(1, 0, 2, 3)
    mlp_out = swapped(mlp_sum, "ctx", "swap_mlp").astype(jnp.float32).sum(axis=0)

    attn_sum = over_pipe(attn_zero, attn_one).astype(low)
    attn_sum = attn_sum.reshape(slots, ctx_count, shard_count, part, 4 * head_dim).transpose(1, 2, 0, 3, 4)
    attn_part = swapped(attn_sum, "ctx", "swap_attn").astype(jnp.float32).sum(axis=0).astype(low)
    attn_out = swapped(attn_part, "wa", "swap_grad")
    attn_out = attn_out.transpose(1, 0, 2, 3).reshape(slots * shard_count, part, 4 * head_dim)
    attn_out = attn_out[:head_count].astype(jnp.float32)

    vec = over_pipe(vec_zero, vec_one)
    length = vec.shape[0]
    fill = -length % 128
    vec = jnp.pad(vec, (0, fill)).reshape(-1, 128)
    vec = gathered(vec, "ctx", "all_small").sum(axis=0).reshape(-1)[:length]
    feature_sum, gain_sum, hidden_own, head_own = jnp.split(
        vec, [4 * width, 6 * width, 6 * width + hidden_bias.shape[1]]
    )
    head_sum = gathered(head_own.reshape(slots, 2 * head_dim), "wa", "all_heads")
    head_sum = head_sum.transpose(1, 0, 2).reshape(slots * shard_count, 2 * head_dim)[:head_count]

    last_traded = lax.ppermute(mine(last_out, d_input), "pipe", swap)
    section_outputs = jnp.where(
        side == 0, jnp.stack([d_input, last_traded]), jnp.stack([last_traded, last_out])
    )
    return (
        section_outputs[None],
        attn_out[None, :, :, : 3 * head_dim],
        attn_out[None, :, :, 3 * head_dim :],
        head_sum[None],
        mlp_out[None],
        hidden_own[None],
        feature_sum.reshape(1, 4, width),
        gain_sum.reshape(1, 2, width),
    )


def tiles_of(total, size=256):
    return [(at, min(size, total - at)) for at in range(0, total, size)]


def shares(ff, n, m):
    share = ff // 128 // n * 128
    return share, ff - n * share


def step_kernel(n, m, sizes, scale, *refs):
    rows, width, ff, slots, micro, head_dim, part, padded = sizes
    (
        turned, pack, mlp, bias, hidden, shift, gain, table,
        out, g_qkv, g_out, g_heads, g_mlp, g_hidden, g_feature, g_gain,
        inp, w_in, stage, wt, mt, mtl, tt, xin, xx, hid_all, hid, a_s, q_s, pair, prob, mix,
        p1, p2, r1, r2, r3, r4, fi, dh, ost, ob, act, slope, dpre, h1, dh1,
        dpair, rpair, dproj, gm, gt, rgm, rgh, sm, smh, zg, zh, ra, s2, za, sv, hv, svc, vec_own, vec_all, snd1, snd2,
        ssem, rsem, loc, go,
    ) = refs
    side = lax.axis_index("pipe")
    c = lax.axis_index("ctx")
    w = lax.axis_index("wa")
    total = micro * rows
    chunk = total // n
    sub = rows // n
    heads = g_heads.shape[0]
    depth = width // n
    share, rest = shares(ff, n, m)
    tail = slice(n * share, n * share + 128)
    left = slice(n * share, ff)
    ffp = n * share + 128
    two = 2 * head_dim
    low = jnp.bfloat16
    f32 = jnp.float32
    mate = {"pipe": 1 - side}
    later = []
    used = [0, 0]

    def take(sends, recvs):
        at = tuple(used)
        used[0] += sends
        used[1] += recvs
        return at

    ctx_peers = [lax.rem(c + d, n) for d in range(1, n)]
    wa_peers = [lax.rem(w + d, m) for d in range(1, m)]

    greet(
        [{"ctx": peer} for peer in ctx_peers]
        + [{"wa": peer} for peer in wa_peers]
        + [{"pipe": 1 - side, "ctx": peer} for peer in [c] + ctx_peers]
    )

    def arrive(ref, sem):
        remote(ref, ref, sem, sem, mate).wait_recv()

    def exchange(axis, src, dst, times=1):
        me, count, peers = (c, n, ctx_peers) if axis == "ctx" else (w, m, wa_peers)
        s0, r0 = take(times * (count - 1), times * count)

        def copy(d, peer, t):
            return remote(
                src(peer, t), dst(me, t), ssem.at[s0 + t * (count - 1) + d], rsem.at[r0 + t * count + me], {axis: peer}
            )

        def start(t=0):
            for d, peer in enumerate(peers):
                copy(d, peer, t).start()

        def got(t=0):
            for peer in peers:
                arrive(dst(peer, t), rsem.at[r0 + t * count + peer])

        def drain():
            def one(t, _):
                for d, peer in enumerate(peers):
                    copy(d, peer, t).wait_send()
                return 0

            if times == 1:
                one(0, 0)
            else:
                lax.fori_loop(0, times, one, 0)

        later.append(drain)
        return start, got

    def single(cond_send, src, dst, peer, cond_recvs, slot):
        s0, r0 = take(1, max(n, m))

        def copy():
            return remote(src, dst(slot), ssem.at[s0], rsem.at[r0 + slot], peer)

        def start():
            pl.when(cond_send)(lambda: copy().start())

        def got():
            for cond, p in cond_recvs:
                pl.when(cond)(functools.partial(arrive, dst(p), rsem.at[r0 + p]))

        later.append(lambda: pl.when(cond_send)(lambda: copy().wait_send()))
        return start, got

    beside = w + 1 - 2 * lax.rem(w, 2)
    above = lax.rem(w + 2, m)
    across = lax.rem(beside + 2, m)

    def plane(whole, half, times):
        s0, r0 = take(4 * times, 4 * times)

        def copy(t, i):
            ref = (whole(t, w), whole(t, w), half(t, beside, 0), half(t, above, 1))[i]
            peer = (beside, above, above, beside)[i]
            return remote(ref, ref, ssem.at[s0 + 4 * t + i], rsem.at[r0 + 4 * t + i], {"wa": peer})

        def start(t):
            copy(t, 0).start()
            copy(t, 1).start()

        def pump(t):
            arrive(whole(t, beside), rsem.at[r0 + 4 * t])
            copy(t, 2).start()
            arrive(whole(t, above), rsem.at[r0 + 4 * t + 1])
            copy(t, 3).start()

        def finish(t):
            arrive(half(t, across, 0), rsem.at[r0 + 4 * t + 2])
            arrive(half(t, across, 1), rsem.at[r0 + 4 * t + 3])

        def drain():
            def one(t, _):
                for i in range(4):
                    copy(t, i).wait_send()
                return 0

            lax.fori_loop(0, times, one, 0)

        later.append(drain)
        return start, finish, pump

    def crows(at):
        return pl.ds(pl.multiple_of(at * depth, 16), depth)

    def chunks(at):
        return pl.ds(pl.multiple_of(at * chunk, 16), chunk)

    def lanes(at):
        return pl.ds(pl.multiple_of(at * share, 128), share)

    def piece(b, at):
        return pl.ds(pl.multiple_of(b * rows + at * sub, 16), sub)

    def batch(b):
        return slice(b * rows, (b + 1) * rows)

    diagonal = c == w

    at_z = exchange("ctx", lambda p, t: pack.at[p, t], lambda me, t: w_in.at[w, t, me], slots)
    at_p = plane(lambda t, at: w_in.at[at, t], lambda t, at, i: w_in.at[at, t, i * (n // 2) : (i + 1) * (n // 2)], slots)
    x_z = exchange("ctx", lambda p, t: inp.at[chunks(w), :], lambda me, t: xin.at[me])
    x_p = exchange("wa", lambda p, t: xin.at[p], lambda me, t: xx.at[0, chunks(me), :])
    hid_p = exchange("wa", lambda p, t: hidden, lambda me, t: hid_all.at[me])
    ml_z = exchange("ctx", lambda p, t: mlp.at[:, :, lanes(p)], lambda me, t: mt.at[:, crows(me), lanes(w)])
    ml_p = plane(
        lambda t, at: mt.at[t, :, lanes(at)],
        lambda t, at, i: mt.at[t, i * (width // 2) : (i + 1) * (width // 2), lanes(at)],
        2,
    )
    mh_z = single(
        jnp.logical_not(diagonal), mtl, lambda at: tt.at[crows(at), :], {"ctx": w},
        [(diagonal, p) for p in ctx_peers], c,
    )
    mh_s, mh_r = take(m - 1, 1)

    def mh_copy(d, peer):
        return remote(tt, tt, ssem.at[mh_s + d], rsem.at[mh_r], {"wa": peer})

    own_pack = pltpu.make_async_copy(pack.at[c], w_in.at[w, :, c], loc.at[0])
    own_mlp = pltpu.make_async_copy(mlp.at[:, :, lanes(c)], mt.at[:, crows(c), lanes(w)], loc.at[1])
    own_x = pltpu.make_async_copy(inp.at[chunks(w), :], xin.at[c], loc.at[2])
    own_half = pltpu.make_async_copy(mtl, tt.at[crows(c), :], loc.at[3])

    mtl[...] = jnp.zeros_like(mtl)
    mtl[:, :rest] = mlp[0, :, left]
    mtl[:, 64 : 64 + rest] = mlp[1, :, left]
    own_pack.start()
    own_mlp.start()
    pl.when(diagonal)(lambda: own_half.start())

    pl.when(side == 1)(lambda: pl.semaphore_wait(go, 1))
    def start_attn(t, _):
        at_z[0](t)
        return 0

    lax.fori_loop(0, slots, start_attn, 0)
    for b in range(micro):
        for at, size in tiles_of(width, 128):
            value = turned[b, at : at + size, :].astype(f32)
            inp[b * rows : (b + 1) * rows, at : at + size] = value.T.astype(low)
    own_x.start()
    x_z[0]()
    hid_p[0]()
    ml_z[0]()
    mh_z[0]()
    stage[...] = jnp.zeros_like(stage)
    mix[...] = jnp.zeros_like(mix)
    sv[...] = jnp.zeros_like(sv)
    hv[...] = jnp.zeros_like(hv)
    own_pack.wait()

    def pass_attn(t, _):
        at_z[1](t)
        at_p[0](t)
        return 0

    lax.fori_loop(0, slots, pass_attn, 0)
    own_x.wait()
    x_z[1]()
    x_p[0]()
    xx[0, chunks(w), :] = xin[w]
    hid_p[1]()
    hid_all[w] = hidden[...]
    for p in range(m):
        hid[:, p * share : (p + 1) * share] = hid_all[p, :, lanes(c)]
    hid[:, tail] = jnp.zeros((1, 128), f32)
    hid[:, left] = hid_all[c, :, left]
    x_p[1]()
    x_ss, x_rs = take(micro * n, micro * n)
    x_at = side
    c_at = 1 - side

    def norm(stream):
        centre = jnp.mean(stream, axis=-1, keepdims=True)
        centred = stream - centre
        variance = jnp.mean(centred * centred, axis=-1, keepdims=True)
        inv_std = lax.rsqrt(variance + EPS)
        return centred * inv_std, inv_std

    def first_norm(b):
        for at, size in tiles_of(rows, 64):
            here = slice(b * rows + at, b * rows + at + size)
            normed, _ = norm(xx[x_at, here, :].astype(f32))
            a_s[here, :] = (normed * gain[0:1, :] + shift[0:1, :]).astype(low)

    upper = lax.broadcasted_iota(jnp.int32, (1, two), 1) >= head_dim
    pairs = exchange(
        "wa",
        lambda p, t: pair.at[w, lax.rem(t, slots), pl.ds(pl.multiple_of(t // slots * rows, 16), rows), :],
        lambda me, t: pair.at[me, lax.rem(t, slots), pl.ds(pl.multiple_of(t // slots * rows, 16), rows), :],
        slots * micro,
    )

    def lay(s):
        pl.when(s + 1 < slots)(lambda: at_p[2](s + 1))
        at_p[1](s)
        for j in range(n):
            for p in range(m):
                at = (j * m + p) * part
                stage[at : at + part, :] = w_in[p, s, j].astype(f32)[:part]
        wt[s] = stage[:width, :].astype(low)

    def project(s, b):
        made = dot(a_s[batch(b), :], wt[s], 1, 0)
        row = pltpu.roll(bias[jnp.minimum(s * n + c, heads - 1)], two // 2, 1)
        pair[w, s, batch(b), :] = (made[:, :two] + jnp.where(upper, 0.0, row)).astype(low)
        q_s[s, batch(b), :] = jnp.where(upper, made[:, two:] + row, 0.0).astype(low)
        pairs[0](b * slots + s)

    @pl.when(side == 0)
    def _():
        for b in range(micro):
            first_norm(b)
        at_p[2](0)

        def both(s, _):
            lay(s)
            for b in range(micro):
                project(s, b)
            return 0

        lax.fori_loop(0, slots, both, 0)

    @pl.when(side == 1)
    def _():
        at_p[2](0)

        def alone(s, _):
            lay(s)
            return 0

        lax.fori_loop(0, slots, alone, 0)

    own_mlp.wait()
    ml_z[1]()
    ml_p[0](0)
    ml_p[0](1)

    @pl.when(diagonal)
    def _():
        own_half.wait()

    mh_z[1]()

    @pl.when(diagonal)
    def _():
        for d, peer in enumerate(wa_peers):
            mh_copy(d, peer).start()

    def mh_drain():
        for d, peer in enumerate(wa_peers):
            mh_copy(d, peer).wait_send()

    later.append(lambda: pl.when(diagonal)(mh_drain))

    @pl.when(side == 0)
    def _():
        pl.semaphore_signal(go, inc=1, device_id=mate, device_id_type=MESH)

    @pl.when(side == 1)
    def _():
        for b in range(micro):
            for p in range(n):
                arrive(xx.at[1, piece(b, p), :], rsem.at[x_rs + b * n + p])
            first_norm(b)

            def one(s, _):
                project(s, b)
                return 0

            lax.fori_loop(0, slots, one, 0)

    block = rows // 2
    step = lax.broadcasted_iota(jnp.int32, (rows, 1), 0)
    qpos = jnp.where(step < block, table[0, w] * block + step, table[1, w] * block + step - block)
    along = lax.broadcasted_iota(jnp.int32, (1, m * rows), 1)
    kpos = along
    for i in range(2 * m):
        inside = (along >= i * block) & (along < (i + 1) * block)
        kpos = jnp.where(inside, table[i % 2, i // 2] * block + along - i * block, kpos)

    def attend(s, b):
        pairs[1](b * slots + s)
        kv = pair[:, s, batch(b), :].reshape(m * rows, two)
        scores = jnp.where(kpos <= qpos, dot(q_s[s, batch(b), :], kv, 1, 1) * scale, -jnp.inf)
        top = jnp.max(scores, axis=-1, keepdims=True)
        raised = jnp.exp(scores - top)
        weight = raised / jnp.sum(raised, axis=-1, keepdims=True)
        prob[s * micro + b] = weight
        mixed = dot(weight.astype(low), kv, 1, 0)
        mix[s, batch(b), two:] = jnp.where(upper, 0.0, mixed).astype(low)

    def summing(part_s, got_s):
        start, got = exchange(
            "ctx", lambda p, t: part_s.at[piece(t, p), :], lambda me, t: got_s.at[me, t], micro
        )

        def finish(b):
            value = part_s[piece(b, c), :].astype(f32)
            got(b)
            for p in ctx_peers:
                value = value + got_s[p, b].astype(f32)
            return value

        return start, finish, later[-1]

    def sharing(ref):
        return exchange("ctx", lambda p, t: ref.at[piece(t, c), :], lambda me, t: ref.at[piece(t, me), :], micro)

    sum1 = summing(p1, r1)
    for b in range(micro):

        def attend_all(s, _):
            attend(s, b)
            return 0

        lax.fori_loop(0, slots, attend_all, 0)
        for at, size in tiles_of(width):
            value = dot(mix[0, batch(b), two:], wt[0, at : at + size, two:], 1, 1)
            for s in range(1, slots):
                value = value + dot(mix[s, batch(b), two:], wt[s, at : at + size, two:], 1, 1)
            p1[batch(b), at : at + size] = value.astype(low)
        sum1[0](b)
    ml_p[2](0)
    fi_ag = sharing(fi)
    for b in range(micro):
        value = sum1[1](b)
        value = xx[x_at, piece(b, c), :].astype(f32) + value + shift[1:2, :]
        h1[b] = value
        normed, _ = norm(value)
        fi[piece(b, c), :] = (normed * gain[1:2, :] + shift[2:3, :]).astype(low)
        fi_ag[0](b)

    ml_p[2](1)
    sum2 = summing(p2, r2)
    beyond = lax.broadcasted_iota(jnp.int32, (1, 128), 1) >= 64

    def down(b):
        for at, size in tiles_of(width):
            p2[batch(b), at : at + size] = dot(act[batch(b), :], mt[1, at : at + size, :], 1, 1).astype(low)
        sum2[0](b)

    for b in range(micro):
        if b == 0:
            ml_p[1](0)
            pl.when(jnp.logical_not(diagonal))(lambda: arrive(tt, rsem.at[mh_r]))
            for at, size in tiles_of(width, 64):
                value = tt[at : at + size, :].astype(f32)
                mt[0, at : at + size, tail] = jnp.where(beyond, 0.0, value).astype(low)
                mt[1, at : at + size, tail] = jnp.where(beyond, 0.0, pltpu.roll(value, 64, 1)).astype(low)
        fi_ag[1](b)
        for at, size in tiles_of(ffp):
            pre = dot(fi[batch(b), :], mt[0, :, at : at + size], 1, 0) + hid[:, at : at + size]
            square = pre * pre
            tangent = jnp.tanh(GELU_C * (pre + GELU_A * square * pre))
            act[batch(b), at : at + size] = (0.5 * pre * (1.0 + tangent)).astype(low)
            slope[batch(b), at : at + size] = 0.5 * (1.0 + tangent) + 0.5 * pre * (
                1.0 - tangent * tangent
            ) * GELU_C * (1.0 + 3.0 * GELU_A * square)
        if b == 0:
            ml_p[1](1)
        pl.when(side == 0)(functools.partial(down, b))

    o_ss, o_rs = take(micro * (m - 1), micro * m)
    back = exchange("ctx", lambda p, t: ost.at[p], lambda me, t: ob.at[:, me])
    back_drain = later.pop()

    def cross(snd, other, b):
        return [
            remote(
                snd.at[b], xx.at[1, piece(b, c), :], ssem.at[x_ss + b * n + d], rsem.at[x_rs + b * n + c],
                {"pipe": other, "ctx": peer},
            )
            for d, peer in enumerate([c] + ctx_peers)
        ]

    def spread(snd, b):
        return [
            remote(
                snd.at[b], ost.at[w, b], ssem.at[o_ss + b * (m - 1) + d], rsem.at[o_rs + b * m + w], {"wa": peer}
            )
            for d, peer in enumerate(wa_peers)
        ]

    def hand_on(snd, at, b):
        @pl.when(side == at)
        def _():
            for copy in cross(snd, 1 - at, b):
                copy.start()

        @pl.when(side == 1 - at)
        def _():
            for copy in spread(snd, b):
                copy.start()
            ost[w, b] = snd[b]

    def spread_on():
        for b in range(micro):
            for p in wa_peers:
                arrive(ost.at[p, b], rsem.at[o_rs + b * m + p])
        back[0]()
        ob[:, c] = ost[c]

    def layer_done(b):
        value = sum2[1](b)
        snd1[b] = (h1[b] + value + shift[3:4, :]).astype(low)
        hand_on(snd1, 0, b)

    @pl.when(side == 0)
    def _():
        for b in range(micro):
            layer_done(b)

    later.remove(sum1[2])
    sum1[2]()
    def column(at, x):
        sv[at : at + 1, :] = sv[at : at + 1, :] + jnp.sum(x, axis=0, keepdims=True)

    def norm_back(d_out, normed, inv_std, row):
        lifted = d_out * gain[row : row + 1, :]
        first = jnp.mean(lifted, axis=-1, keepdims=True)
        second = jnp.mean(lifted * normed, axis=-1, keepdims=True)
        return inv_std * (lifted - first - normed * second)

    sum3 = summing(p1, r3)
    for b in range(micro):

        @pl.when(side == 0)
        def _():
            for p in range(n):
                arrive(xx.at[1, piece(b, p), :], rsem.at[x_rs + b * n + p])

        for at, size in tiles_of(ffp):
            d_pre = dot(xx[c_at, batch(b), :], mt[1, :, at : at + size], 1, 0) * slope[batch(b), at : at + size]
            over = slice(at, min(at + size, ff))
            sv[6:7, over] = sv[6:7, over] + jnp.sum(d_pre, axis=0, keepdims=True)[:, : over.stop - at]
            dpre[batch(b), at : at + size] = d_pre.astype(low)
        for at, size in tiles_of(width):
            p1[batch(b), at : at + size] = dot(dpre[batch(b), :], mt[0, at : at + size, :], 1, 1).astype(low)
        sum3[0](b)
    gm_p = exchange("wa", lambda p, t: gm.at[t, :, lanes(p)], lambda me, t: rgm.at[me, t], 2)
    for at, size in tiles_of(width):
        gm[1, at : at + size, :] = dot(xx[c_at, :, at : at + size], act[...], 0, 0).astype(low)
    gm_p[0](1)
    for at, size in tiles_of(width):
        gm[0, at : at + size, :] = dot(fi[:, at : at + size], dpre[...], 0, 0).astype(low)
    dh_ag = sharing(dh)
    for b in range(micro):
        value = sum3[1](b)
        normed, inv_std = norm(h1[b])
        cot = xx[c_at, piece(b, c), :].astype(f32)
        column(2, value)
        column(5, value * normed)
        column(3, cot)
        value = cot + norm_back(value, normed, inv_std, 1)
        dh1[b] = value
        column(1, value)
        dh[piece(b, c), :] = value.astype(low)
        dh_ag[0](b)

    dpairs = exchange(
        "wa",
        lambda p, t: dpair.at[p, lax.rem(t, slots), pl.ds(pl.multiple_of(t // slots * rows, 16), rows), :],
        lambda me, t: rpair.at[me, lax.rem(t, slots), pl.ds(pl.multiple_of(t // slots * rows, 16), rows), :],
        slots * micro,
    )

    def attend_back(s, b):
        d_mixed = dot(dh[batch(b), :], wt[s, :, two:], 1, 0)
        d_mixed = jnp.where(upper, 0.0, d_mixed).astype(low)
        kv = pair[:, s, batch(b), :].reshape(m * rows, two)
        weight = prob[s * micro + b]
        d_probs = dot(d_mixed, kv, 1, 1)
        delta = jnp.sum(weight * d_probs, axis=-1, keepdims=True)
        d_scores = (weight * (d_probs - delta) * scale).astype(low)
        d_query = jnp.where(upper, dot(d_scores, kv, 1, 0), 0.0)
        hv[s] = hv[s] + jnp.sum(d_query, axis=0, keepdims=True)
        dproj[s, batch(b), two:] = d_query.astype(low)
        d_kv = dot(d_scores, q_s[s, batch(b), :], 0, 0) + dot(weight.astype(low), d_mixed, 0, 0)
        dpair[:, s, batch(b), :] = d_kv.astype(low).reshape(m, rows, two)
        dpairs[0](b * slots + s)

    for b in range(micro):
        dh_ag[1](b)

        def attend_back_all(s, _):
            attend_back(s, b)
            return 0

        lax.fori_loop(0, slots, attend_back_all, 0)
    for at, size in tiles_of(width, 64):
        value = pltpu.roll(gm[1, at : at + size, tail].astype(f32), 64, 1)
        gt[at : at + size, :] = jnp.where(beyond, value, gm[0, at : at + size, tail].astype(f32)).astype(low)
    gh_p = single(
        jnp.logical_not(diagonal), gt, lambda at: rgh.at[at], {"wa": c},
        [(diagonal, p) for p in wa_peers], w,
    )
    gm_p[0](0)
    gh_p[0]()

    @pl.when(side == 1)
    def _():
        for b in range(micro):
            down(b)

    later.remove(sum3[2])
    sum3[2]()
    sum4 = summing(p1, r4)
    for b in range(micro):

        def collect(s, _):
            value = dpair[w, s, batch(b), :].astype(f32)
            dpairs[1](b * slots + s)
            for p in wa_peers:
                value = value + rpair[p, s, batch(b), :].astype(f32)
            dproj[s, batch(b), :two] = value.astype(low)
            hv[s] = hv[s] + jnp.where(upper, 0.0, jnp.sum(value, axis=0, keepdims=True))
            return 0

        lax.fori_loop(0, slots, collect, 0)
        for at, size in tiles_of(width):
            value = dot(dproj[0, batch(b), :], wt[0, at : at + size, :], 1, 1)
            for s in range(1, slots):
                value = value + dot(dproj[s, batch(b), :], wt[s, at : at + size, :], 1, 1)
            p1[batch(b), at : at + size] = value.astype(low)
        sum4[0](b)

    @pl.when(side == 1)
    def _():
        for b in range(micro):
            layer_done(b)

    at_drain = later.pop(0), later.pop(0)
    at_drain[0]()
    at_drain[1]()

    ga_p = exchange("wa", lambda p, t: w_in.at[p, t], lambda me, t: ra.at[me, t], slots)

    def attn_grad(s, _):
        for at, size in tiles_of(width):
            stage[at : at + size, :] = dot(a_s[:, at : at + size], dproj[s], 0, 0) + dot(
                dh[:, at : at + size], mix[s], 0, 0
            )
        for j in range(n):
            for p in range(m):
                at = (j * m + p) * part
                w_in[p, s, j] = stage[at : at + padded, :].astype(low)
        ga_p[0](s)
        return 0

    lax.fori_loop(0, slots, attn_grad, 0)
    for b in range(micro):
        value = sum4[1](b)
        normed, inv_std = norm(xx[x_at, piece(b, c), :].astype(f32))
        column(0, value)
        column(4, value * normed)
        snd2[b] = (dh1[b] + norm_back(value, normed, inv_std, 0)).astype(low)
        hand_on(snd2, 1, b)
    for s in range(slots):
        sv[8 + s : 9 + s, :two] = hv[s]
    svc[w] = sv[...]
    sv_p = exchange("wa", lambda p, t: sv, lambda me, t: svc.at[me])
    sv_p[0]()

    gm_z = exchange("ctx", lambda p, t: sm.at[t, crows(p), :], lambda me, t: zg.at[me, t], 2)
    for k in (1, 0):
        gm_p[1](k)

        def sum_mlp(i, _):
            at = pl.ds(pl.multiple_of(i * 64, 64), 64)
            value = gm[k, at, lanes(w)].astype(f32)
            for p in wa_peers:
                value = value + rgm[p, k, at, :].astype(f32)
            sm[k, at, :] = value.astype(low)
            return 0

        lax.fori_loop(0, width // 64, sum_mlp, 0)
        gm_z[0](k)
        zg[c, k] = sm[k, crows(c), :]
    gh_p[1]()
    gh_s, gh_r = take(n - 1, 1)

    def gh_copy(d, peer):
        return remote(smh.at[crows(peer), :], zh, ssem.at[gh_s + d], rsem.at[gh_r], {"ctx": peer})

    @pl.when(diagonal)
    def _():
        def sum_half(i, _):
            at = pl.ds(pl.multiple_of(i * 64, 64), 64)
            value = gt[at, :].astype(f32)
            for p in wa_peers:
                value = value + rgh[p, at, :].astype(f32)
            smh[at, :] = value.astype(low)
            return 0

        lax.fori_loop(0, width // 64, sum_half, 0)
        for d, peer in enumerate(ctx_peers):
            gh_copy(d, peer).start()
        value = smh[crows(c), :].astype(f32)
        g_mlp[0, :, left] = value[:, :rest]
        g_mlp[1, :, left] = value[:, 64 : 64 + rest]

    spread_on()
    sv_p[1]()
    value = svc[0]
    for p in range(1, m):
        value = value + svc[p]
    vec_own[...] = value
    vec_all[c] = value
    sv_z = exchange("ctx", lambda p, t: vec_own, lambda me, t: vec_all.at[me])
    sv_z[0]()
    ga_z = exchange("ctx", lambda p, t: s2.at[p, t], lambda me, t: za.at[me, t], slots)

    def sum_attn(s, _):
        ga_p[1](s)
        for j in range(n):
            value = w_in[w, s, j].astype(f32)
            for p in wa_peers:
                value = value + ra[p, s, j].astype(f32)
            s2[j, s] = value.astype(low)
        ga_z[0](s)
        za[c, s] = s2[c, s]
        return 0

    lax.fori_loop(0, slots, sum_attn, 0)

    for k in (1, 0):
        gm_z[1](k)
        for p in range(n):
            g_mlp[k, :, p * share : (p + 1) * share] = zg[p, k].astype(f32)

    @pl.when(jnp.logical_not(diagonal))
    def _():
        arrive(zh, rsem.at[gh_r])
        value = zh[...].astype(f32)
        g_mlp[0, :, left] = value[:, :rest]
        g_mlp[1, :, left] = value[:, 64 : 64 + rest]

    back[1]()
    for b in range(micro):
        for at, size in tiles_of(width, 128):
            value = ob[b, :, :, at : at + size].astype(f32).reshape(rows, size)
            out[b, at : at + size, :] = value.T
    sv_z[1]()
    value = vec_all[0]
    for p in range(1, n):
        value = value + vec_all[p]
    g_feature[...] = value[0:4, :]
    g_gain[...] = value[4:6, :]
    for p in range(n):
        g_hidden[:, p * share : (p + 1) * share] = vec_all[p, 6:7, lanes(w)]
        for s in range(slots):
            h = s * n + p
            if h < heads:
                g_heads[h] = pltpu.roll(vec_all[p, 8 + s : 9 + s, :two], two // 2, 1)
    g_hidden[:, left] = vec_all[w, 6:7, left]
    for s in range(slots):
        ga_z[1](s)
        for p in range(n):
            h = s * n + p
            if h < heads:
                first = za[p, s, :, :two].astype(f32)[:part]
                second = za[p, s, :, two:].astype(f32)[:part]
                g_qkv[h, :, :two] = jnp.where(upper, first, pltpu.roll(second, two // 2, 1))
                g_qkv[h, :, two:] = first[:, : two // 2]
                g_out[h] = second[:, : two // 2]

    for drain in later:
        drain()
    back_drain()

    @pl.when(diagonal)
    def _():
        for d, peer in enumerate(ctx_peers):
            gh_copy(d, peer).wait_send()

    for snd, at in ((snd1, 0), (snd2, 1)):

        for b in range(micro):

            @pl.when(side == at)
            def _():
                for copy in cross(snd, 1 - at, b):
                    copy.wait_send()

            @pl.when(side == 1 - at)
            def _():
                for copy in spread(snd, b):
                    copy.wait_send()


def whole_step(
    section_inputs, qkv_weight, out_weight, head_bias, mlp_weight, hidden_bias, feature_bias, ln_gain, block_table
):
    n = lax.axis_size("ctx")
    m = lax.axis_size("wa")
    micro, rows, width = section_inputs.shape[1:]
    heads, part = qkv_weight.shape[1:3]
    head_dim = out_weight.shape[3]
    ff = mlp_weight.shape[3]
    depth = mlp_weight.shape[2]
    slots = (heads + n - 1) // n
    pad = slots * n - heads
    padded = part + (-part % 16)
    total = micro * rows
    chunk = total // n
    share, rest = shares(ff, n, m)
    low = jnp.bfloat16
    f32 = jnp.float32
    two = 2 * head_dim
    scale = head_dim ** (-0.5)

    query, key, value = (qkv_weight[0, :, :, i * head_dim : (i + 1) * head_dim] for i in range(3))
    pack = jnp.concatenate([value, key, out_weight[0], query], axis=-1)
    pack = jnp.pad(pack, ((0, pad), (0, padded - part), (0, 0)))
    pack = pack.reshape(slots, n, padded, 2 * two).transpose(1, 0, 2, 3)
    def v(shape, kind=low):
        return pltpu.VMEM(shape, kind)

    sub = rows // n
    ffp = n * share + 128
    wide = (total, width)
    parts = (slots, padded, 2 * two)
    scratch = (
        [v(wide), v((m, slots, n) + parts[1:]), v((width + 16, 2 * two), f32), v((slots, width, 2 * two)), v((2, width, ffp)), v((depth, 128)), v((width, 128))]
        + [v((n, chunk, width)), v((2,) + wide), v((m, 1, ff), f32), v((1, ffp), f32), v(wide)]
        + [v((slots, total, two)), v((m, slots, total, two)), v((slots * micro, rows, m * rows), f32)]
        + [v((slots, total, 2 * two))]
        + [v(wide)] * 2
        + [v((n, micro, sub, width))] * 4
        + [v(wide), v(wide), v((m, micro, sub, width)), v((micro, n, sub, width))]
        + [v((total, ffp)), v((total, ffp), f32), v((total, ffp))]
        + [v((micro, sub, width), f32), v((micro, sub, width), f32)]
        + [v((m, slots, total, two))] * 2
        + [v((slots, total, 2 * two)), v((2, width, ffp)), v((width, 128)), v((m, 2, width, share)), v((m, width, 128))]
        + [v((2, width, share)), v((width, 128)), v((n, 2, depth, share)), v((depth, 128))]
        + [v((m, slots, n) + parts[1:]), v((n,) + parts), v((n,) + parts)]
        + [v((16, width), f32), v((slots, 1, two), f32), v((m, 16, width), f32), v((16, width), f32)]
        + [v((n, 16, width), f32)]
        + [v((micro, sub, width))] * 2
        + [dma(256), dma(300), dma(4), pltpu.SemaphoreType.REGULAR]
    )
    shapes = [
        jax.ShapeDtypeStruct(shape, f32)
        for shape in (
            (micro, width, rows),
            (heads, part, 3 * head_dim),
            (heads, part, head_dim),
            (heads, 1, two),
            (2, depth, ff),
            (1, ff),
            (4, width),
            (2, width),
        )
    ]
    sizes = (rows, width, ff, slots, micro, head_dim, part, padded)
    out, g_qkv, g_out, g_heads, g_mlp, g_hidden, g_feature, g_gain = pl.pallas_call(
        functools.partial(step_kernel, n, m, sizes, scale),
        out_shape=shapes,
        in_specs=[VM] * 7 + [pl.BlockSpec(memory_space=pltpu.SMEM)],
        out_specs=[VM] * len(shapes),
        scratch_shapes=scratch,
        compiler_params=pltpu.CompilerParams(
            collective_id=IDS["step"], has_side_effects=True, vmem_limit_bytes=61 * 1024 * 1024
        ),
        name="step",
    )(
        section_inputs[0].transpose(0, 2, 1),
        pack,
        mlp_weight[0],
        head_bias.reshape(heads, 1, two),
        hidden_bias,
        feature_bias[0],
        ln_gain[0],
        block_table.T,
    )
    return (
        out.transpose(0, 2, 1)[None],
        g_qkv[None],
        g_out[None],
        g_heads.reshape(1, heads, two),
        g_mlp[None],
        g_hidden,
        g_feature[None],
        g_gain[None],
    )


def fits(mesh, rows, micro, width, ff):
    n, m = mesh.shape["ctx"], mesh.shape["wa"]
    depth, chunk = width // n, micro * rows // n
    share, rest = shares(ff, n, m)
    even = depth % 16 == 0 and chunk % 16 == 0 and rows // n % 16 == 0 and width % 64 == 0
    return n == m == 4 and even and width % 32 == 0 and ff <= width and 0 < rest <= 64 and share > 0


def either(mesh, *args):
    micro, rows, width = args[0].shape[1:]
    if fits(mesh, rows, micro, width, args[4].shape[3]):
        return whole_step(*args)
    return per_device(*args)


def solution(mesh):
    return jax.shard_map(
        functools.partial(either, mesh),
        mesh=mesh,
        in_specs=(
            P("pipe", None, "ctx", None),
            P("pipe", None, ("ctx", "wa"), None),
            P("pipe", None, ("ctx", "wa"), None),
            P("pipe", None, None),
            P("pipe", None, "ctx", "wa"),
            P("pipe", "wa"),
            P("pipe", None, None),
            P("pipe", None, None),
            P(),
        ),
        out_specs=(
            P("pipe", None, "ctx", None),
            P("pipe", None, ("ctx", "wa"), None),
            P("pipe", None, ("ctx", "wa"), None),
            P("pipe", None, None),
            P("pipe", None, "ctx", "wa"),
            P("pipe", "wa"),
            P("pipe", None, None),
            P("pipe", None, None),
        ),
        check_vma=False,
    )
```
